32 devices in a mesh: grp: 4 (over x, core), row: 8 (over z, y).
Axes of the slice: x: 2, y: 2, z: 4, core: 2. Of those that a mesh axis runs over, the one named last changes fastest.
Arguments:
- rhs: float32 [64, 4096], P(None, ('grp', 'row')), may hold values from -120 to 120
- guess: float32 [64, 4096], P(None, ('grp', 'row')), may hold values from -6 to 6
- diag_blocks: bfloat16 [64, 64, 4096], P(None, None, ('grp', 'row'))
- diag_inverse: bfloat16 [64, 64, 4096], P(None, None, ('grp', 'row'))
- coupling: bfloat16 [64, 64, 4096], P(None, None, ('grp', 'row'))
- prolong: bfloat16 [64, 64, 4096], P(None, None, ('grp', 'row')), may hold values from -0.75 to 0.75
- coarse_inverse: bfloat16 [64, 64, 512], P(None, None, ('grp', 'row'))
- aggregate: int32 [4096], P(('grp', 'row')), may hold values from 0 to 511, as said below
Outputs:
- solution: float32 [64, 4096], P(None, ('grp', 'row'))
- residual: float32 [64, 4096], P(None, ('grp', 'row'))
The draws below stay inside these ranges and needn't reach their ends.
Inputs may be any that keep to these rules, and one draw needn't show every extreme that they name: The fine blocks held by index g of grp name only the aggregates g * 128 to (g + 1) * 128 - 1, and each aggregate is named by exactly 8 fine blocks.
All inputs are finite; a program needn't handle non-finite values.
Results may differ from the reference program's by a relative error of at most 0.0003.
Values may be sent and summed in bfloat16 or wider, within the bound.
No kernel may reach another device: no remote copies, remote signals or barrier semaphores. Data moves between devices by JAX's collectives and lax.ppermute only.
A program may use at most 64 MiB of HBM per device.

```python
import math
import jax
import jax.numpy as jnp
from jax import lax

B = 64
AGG = 8
SWEEPS = 2
NBT = 4096
NCG = 128
NC = 512
N_GRP = 4


def diagonal_parts(key):
    inner = jax.random.fold_in(key, 11)
    first_key, second_key = jax.random.split(inner)
    scales = jnp.exp(jax.random.uniform(first_key, (B, NBT), jnp.float32, math.log(8.0), math.log(16.0)))
    off_diag = jax.random.normal(second_key, (B, B, NBT), jnp.float32) * (0.24 / math.sqrt(B))
    identity_mask = (jnp.arange(B)[:, None] == jnp.arange(B)[None, :])[:, :, None]
    return (scales, off_diag, identity_mask)


def draw_diag_blocks(key, part):
    scales, off_diag, identity_mask = diagonal_parts(key)
    return jnp.where(identity_mask, scales[:, None, :], off_diag).astype(jnp.bfloat16)


def draw_diag_inverse(key, part):
    scales, off_diag, identity_mask = diagonal_parts(key)
    first_order = -off_diag / (scales[:, None, :] * scales[None, :, :])
    return jnp.where(identity_mask, 1.0 / scales[:, None, :], first_order).astype(jnp.bfloat16)


def draw_coupling(key, part):
    inner = jax.random.fold_in(key, 17)
    first_key, second_key = jax.random.split(inner)
    leading = jax.random.uniform(first_key, (B, NBT), jnp.float32, -2.5, -0.5)
    off_diag = jax.random.normal(second_key, (B, B, NBT), jnp.float32) * (0.24 / math.sqrt(B))
    identity_mask = (jnp.arange(B)[:, None] == jnp.arange(B)[None, :])[:, :, None]
    return jnp.where(identity_mask, leading[:, None, :], off_diag).astype(jnp.bfloat16)


def draw_coarse_inverse(key, part):
    inner = jax.random.fold_in(key, 23)
    first_key, second_key = jax.random.split(inner)
    leading = jnp.exp(jax.random.uniform(first_key, (B, NC), jnp.float32, math.log(0.006), math.log(0.015)))
    off_diag = jax.random.normal(second_key, (B, B, NC), jnp.float32) * (0.0016 / math.sqrt(B))
    identity_mask = (jnp.arange(B)[:, None] == jnp.arange(B)[None, :])[:, :, None]
    return jnp.where(identity_mask, leading[:, None, :], off_diag).astype(jnp.bfloat16)


def draw_aggregate(key, part):
    group_keys = jax.random.split(jax.random.fold_in(key, 29), N_GRP)

    def one_group(group_key, group_index):
        return jax.random.permutation(group_key, NCG * AGG) // AGG + group_index * NCG
    values = jax.vmap(one_group)(group_keys, jnp.arange(N_GRP, dtype=jnp.int32))
    return values.reshape(NBT).astype(jnp.int32)


def block_scale(own_key, extent, cuts, least, top_value):
    level = 1.0
    for dim, parts in cuts:
        draws = jax.random.uniform(jax.random.fold_in(jax.random.fold_in(own_key, 6), dim), (parts,), jnp.float32, least / len(cuts), top_value / len(cuts))
        level = level * jnp.repeat(jnp.exp(draws), extent[dim] // parts).reshape((-1,) + (1,) * (len(extent) - 1 - dim))
    return level


def centred(stream_key, extent, scale, bound, shards=(), kind=jnp.bfloat16):
    gain = block_scale(stream_key, extent, shards, -0.22, 0.18) if shards else 1.0
    entries = jax.random.normal(stream_key, extent, jnp.float32) * scale * gain
    return jnp.minimum(jnp.maximum(entries, -bound), bound).astype(kind)


def setup_inputs(seed: int = 0) -> dict:
    key_list = jax.random.split(jax.random.key(seed), 9)
    rhs = centred(key_list[0], (B, NBT), 20.0, 120.0, ((1, 32),), jnp.float32)
    guess = centred(key_list[1], (B, NBT), 1.0, 6.0, ((1, 32),), jnp.float32)
    diag_blocks = draw_diag_blocks(jax.random.fold_in(key_list[8], 71), 0)
    diag_inverse = draw_diag_inverse(jax.random.fold_in(key_list[8], 71), 0)
    coupling = draw_coupling(jax.random.fold_in(key_list[8], 71), 0)
    prolong = centred(key_list[5], (B, B, NBT), B ** -0.5, 0.75, ((2, 32),))
    coarse_inverse = draw_coarse_inverse(jax.random.fold_in(key_list[8], 71), 0)
    aggregate = draw_aggregate(jax.random.fold_in(key_list[8], 71), 0)
    return dict(rhs=rhs, guess=guess, diag_blocks=diag_blocks, diag_inverse=diag_inverse, coupling=coupling, prolong=prolong, coarse_inverse=coarse_inverse, aggregate=aggregate)


def apply_blocks(blocks, vector):
    return jnp.einsum('ijn,jn->in', blocks.astype(jnp.float32), vector, precision=lax.Precision.HIGHEST)


def apply_transposed(blocks, vector):
    return jnp.einsum('jin,jn->in', blocks.astype(jnp.float32), vector, precision=lax.Precision.HIGHEST)


def reference(rhs, guess, diag_blocks, diag_inverse, coupling, prolong, coarse_inverse, aggregate):
    zero_column = jnp.zeros((B, 1), jnp.float32)

    def operate(vector):
        lower = jnp.concatenate([zero_column, vector[:, :-1]], axis=1)
        upward = apply_transposed(coupling, vector)
        upper = jnp.concatenate([upward[:, 1:], zero_column], axis=1)
        return apply_blocks(diag_blocks, vector) + apply_blocks(coupling, lower) + upper

    def sweep(iterate):
        return iterate + apply_blocks(diag_inverse, rhs - operate(iterate))

    iterate = guess
    for number in range(SWEEPS):
        iterate = sweep(iterate)
    fine_residual = rhs - operate(iterate)
    pieces = apply_transposed(prolong, fine_residual)
    coarse_rhs = jax.ops.segment_sum(pieces.T, aggregate, num_segments=NC).T
    coarse_value = apply_blocks(coarse_inverse, coarse_rhs)
    spread = coarse_value[:, aggregate]
    iterate = iterate + apply_blocks(prolong, spread)
    for number in range(SWEEPS):
        iterate = sweep(iterate)
    return iterate, rhs - operate(iterate)
```

```python
import jax
import jax.numpy as jnp
from jax import lax
from jax.sharding import PartitionSpec as P

AGG = 8
BOTH = ("grp", "row")
EXACT = lax.Precision.HIGHEST


def from_behind(block, distance):
    devices = range(lax.axis_size(BOTH))
    route = [(i - distance, i) for i in devices if i - distance in devices]
    return lax.ppermute(block, BOTH, route)


def apply_blocks(blocks, vector):
    return jnp.einsum(
        "ijn,jn->in", blocks, vector, precision=EXACT, preferred_element_type=jnp.float32
    )


def apply_transposed(blocks, vector):
    return jnp.einsum(
        "jin,jn->in", blocks, vector, precision=EXACT, preferred_element_type=jnp.float32
    )


def one(block, column):
    return jnp.sum(block.astype(jnp.float32) * column[None, :], axis=1)


def one_transposed(block, column):
    return jnp.sum(block.astype(jnp.float32) * column[:, None], axis=0)


def local(rhs, guess, diag_blocks, diag_inverse, coupling, prolong, coarse_inverse, aggregate):
    count = rhs.shape[1]
    lane = jnp.arange(count)[None, :]

    def operate(vector, before, after):
        lower = jnp.concatenate([before[:, None], vector[:, :-1]], axis=1)
        upward = apply_transposed(coupling, vector)
        upper = jnp.concatenate([upward[:, 1:], after[:, None]], axis=1)
        return apply_blocks(diag_blocks, vector) + apply_blocks(coupling, lower) + upper

    def sweep(iterate, before, after):
        return iterate + apply_blocks(diag_inverse, rhs - operate(iterate, before, after))

    first_blocks = jnp.stack(
        [diag_blocks[:, :, 0], diag_inverse[:, :, 0], coupling[:, :, 0], coupling[:, :, 1]]
    )
    last_blocks = jnp.stack([diag_blocks[:, :, -1], diag_inverse[:, :, -1], coupling[:, :, -1]])
    left_blocks = from_behind(last_blocks, 1)
    right_blocks = from_behind(first_blocks, -1)
    zero = jnp.zeros_like(rhs[:, 0])

    def two_sweeps(start):
        trial = sweep(start, zero, zero)
        last = jnp.stack([start[:, -1], trial[:, -1], trial[:, -2], rhs[:, -1]])
        first = jnp.stack([start[:, 0], trial[:, 0], trial[:, 1], rhs[:, 0]])
        left = from_behind(last, 1)
        right = from_behind(first, -1)
        left_diag, left_inverse, left_coupling = left_blocks
        right_diag, right_inverse, right_coupling, right_next = right_blocks
        own_diag, own_inverse, own_coupling, own_next = first_blocks
        last_inverse = last_blocks[1]
        up_right = one_transposed(right_coupling, right[0])
        first_x = trial[:, 0] - one(own_inverse, one(own_coupling, left[0]))
        last_x = trial[:, -1] - one(last_inverse, up_right)
        left_x = left[1] - one(left_inverse, one_transposed(own_coupling, start[:, 0]))
        right_x = right[1] - one(right_inverse, one(right_coupling, start[:, -1]))
        once = jnp.where(lane == 0, first_x[:, None], trial)
        once = jnp.where(lane == count - 1, last_x[:, None], once)
        twice = sweep(once, left_x, one_transposed(right_coupling, right_x))
        left_twice = left_x + one(
            left_inverse,
            left[3]
            - one(left_diag, left_x)
            - one(left_coupling, left[2])
            - one_transposed(own_coupling, first_x),
        )
        right_twice = right_x + one(
            right_inverse,
            right[3]
            - one(right_diag, right_x)
            - one(right_coupling, last_x)
            - one_transposed(right_next, right[2]),
        )
        return twice, rhs - operate(twice, left_twice, one_transposed(right_coupling, right_twice))

    iterate, fine_residual = two_sweeps(guess)
    rows = lax.axis_size("row")
    group_count = count * rows // AGG
    local_index = aggregate - lax.axis_index("grp") * group_count
    selector = (
        local_index[:, None] == jnp.arange(group_count, dtype=jnp.int32)[None, :]
    ).astype(jnp.float32)
    pieces = apply_transposed(prolong, fine_residual)
    partial_coarse = jnp.einsum("in,nc->ci", pieces, selector, precision=EXACT)
    shares = lax.all_to_all(partial_coarse, "row", 0, 0, tiled=True)
    own = group_count // rows
    share = jnp.sum(shares.reshape(rows, own, -1), axis=0)
    corrected = apply_blocks(coarse_inverse, share.T)
    copies = jnp.tile(corrected.T, (rows, 1))
    values = lax.all_to_all(copies, "row", 0, 0, tiled=True)
    spread = jnp.einsum("ci,nc->in", values, selector, precision=EXACT)
    iterate = iterate + apply_blocks(prolong, spread)
    return two_sweeps(iterate)


def solution(mesh):
    vector = P(None, BOTH)
    blocks = P(None, None, BOTH)
    return jax.shard_map(
        local,
        mesh=mesh,
        in_specs=(vector, vector, blocks, blocks, blocks, blocks, blocks, P(BOTH)),
        out_specs=(vector, vector),
        check_vma=False,
    )
```

```python
import functools

import jax
import jax.numpy as jnp
from jax import lax
from jax.experimental import pallas as pl
from jax.experimental.pallas import tpu as pltpu
from jax.sharding import PartitionSpec as P

AGG = 8
BOTH = ("grp", "row")
F32 = jnp.float32
BF16 = jnp.bfloat16
ROWS = 8


def from_behind(block, distance):
    devices = range(lax.axis_size(BOTH))
    route = [(i - distance, i) for i in devices if i - distance in devices]
    return lax.ppermute(block, BOTH, route)


def lanes(like):
    return lax.broadcasted_iota(jnp.int32, like.shape, 1)


def turn(tile, shift):
    return pltpu.roll(tile, shift % tile.shape[1], 1)


def three(tile):
    high = tile.astype(BF16)
    rest = tile - high.astype(F32)
    middle = rest.astype(BF16)
    return high, middle, (rest - middle.astype(F32)).astype(BF16)


def product(left, right, dims):
    left = left.astype(BF16)
    parts = [
        lax.dot_general(left, part, (dims, ((), ())), preferred_element_type=F32)
        for part in three(right)
    ]
    return parts[0] + (parts[1] + parts[2])


def times(block, columns):
    return product(block, columns, ((1,), (0,)))


def times_transposed(block, columns):
    return product(block, columns, ((0,), (0,)))


def operate(diag, coupling, vector_ref, out_ref, lower):
    vector = vector_ref[...]

    def step(chunk, upward):
        start = pl.multiple_of(chunk * ROWS, ROWS)
        own = vector_ref[pl.ds(start, ROWS), :]
        sums = []
        for s in range(ROWS):
            pair = coupling[start + s].astype(F32)
            terms = diag[start + s].astype(F32) * vector + pair * lower
            sums.append(jnp.sum(terms, axis=0, keepdims=True))
            upward = upward + pair * own[s : s + 1, :]
        out_ref[pl.ds(start, ROWS), :] = jnp.concatenate(sums, axis=0)
        return upward

    return lax.fori_loop(0, vector.shape[0] // ROWS, step, jnp.zeros_like(vector))


def apply_blocks(blocks, vector, base_ref, out_ref):
    def step(chunk, carry):
        start = pl.multiple_of(chunk * ROWS, ROWS)
        sums = [
            jnp.sum(blocks[start + s].astype(F32) * vector, axis=0, keepdims=True)
            for s in range(ROWS)
        ]
        base = base_ref[pl.ds(start, ROWS), :]
        out_ref[pl.ds(start, ROWS), :] = base + jnp.concatenate(sums, axis=0)
        return carry

    lax.fori_loop(0, vector.shape[0] // ROWS, step, 0)


def apply_transposed(blocks, vector_ref):
    def step(chunk, total):
        start = pl.multiple_of(chunk * ROWS, ROWS)
        own = vector_ref[pl.ds(start, ROWS), :]
        for s in range(ROWS):
            total = total + blocks[start + s].astype(F32) * own[s : s + 1, :]
        return total

    zero = jnp.zeros(vector_ref.shape, F32)
    return lax.fori_loop(0, vector_ref.shape[0] // ROWS, step, zero)


def edges(blocks, scratch):
    size, count = blocks.shape[0], blocks.shape[2]
    lane = lax.broadcasted_iota(jnp.int32, (size, count), 1)

    def step(chunk, tile):
        start = chunk * ROWS
        for s in range(ROWS):
            turned = pltpu.roll(blocks[start + s].astype(F32), 2 * (start + s) + 1, 1)
            tile = jnp.where(lax.shift_right_logical(lane, 1) == start + s, turned, tile)
        return tile

    tile = lax.fori_loop(0, size // ROWS, step, jnp.zeros((size, count), F32))
    scratch[...] = jnp.transpose(tile)
    return scratch[pl.ds(1, size, stride=2), :], scratch[pl.ds(0, size, stride=2), :]


def trial_sweep(rhs_ref, start_ref, diag, inverse, coupling, last_coupling, trial_ref, work_ref):
    start = start_ref[...]
    lane = lanes(start)
    end = start.shape[1] - 1
    lower = jnp.where(lane == 0, 0.0, turn(start, 1))
    upward = operate(diag, coupling, start_ref, work_ref, lower)
    upper = jnp.where(lane == end, 0.0, turn(upward, -1))
    defect = rhs_ref[...] - (work_ref[...] + upper)
    apply_blocks(inverse, defect, start_ref, trial_ref)
    trial = trial_ref[...]
    upward = apply_transposed(coupling, trial_ref)
    to_left = rhs_ref[...] - turn(upward, -1)
    to_right = rhs_ref[...] - times(last_coupling, turn(trial, 1))
    right = jnp.where(
        lane == 0, turn(start, 1), jnp.where(lane == 1, turn(trial, 2), turn(to_right, 3))
    )
    left = jnp.where(
        lane == end, turn(start, -1), jnp.where(lane == end - 1, turn(trial, -2), turn(to_left, -3))
    )
    return right, left


def first_kernel(
    rhs, guess, diag, inverse, coupling, trial, to_right, to_left, own, work, scratch
):
    size = guess.shape[0]
    first_diag, last_diag = edges(diag, scratch)
    first_inverse, last_inverse = edges(inverse, scratch)
    first_coupling, last_coupling = edges(coupling, scratch)
    to_right[1] = jnp.concatenate([last_diag, last_inverse], axis=1)
    to_left[1] = jnp.concatenate([first_diag, first_inverse], axis=1)
    to_left[2] = jnp.concatenate([first_coupling, first_coupling], axis=1)
    own[0] = first_coupling.astype(BF16)
    own[1] = first_inverse.astype(BF16)
    own[2] = last_coupling.astype(BF16)
    own[3] = last_inverse.astype(BF16)
    right, left = trial_sweep(rhs, guess, diag, inverse, coupling, last_coupling, trial, work)
    to_right[0] = right
    to_left[0] = left


def finish(
    rhs, start_ref, trial_ref, diag, inverse, coupling, own, left, right,
    left_blocks, right_blocks, twice_ref, work_ref, once_ref,
):
    start, trial = start_ref[...], trial_ref[...]
    size = start.shape[0]
    lane = lanes(start)
    end = start.shape[1] - 1
    at_start, at_end = lane == 0, lane == end
    left_diag, left_inverse = left_blocks[0][:, :size], left_blocks[0][:, size:]
    right_diag, right_inverse = right_blocks[0][:, :size], right_blocks[0][:, size:]
    right_coupling = right_blocks[1][:, :size]
    first_coupling, first_inverse, last_inverse = own[0], own[1], own[3]

    up_right = times_transposed(right_coupling, right)
    down_left = times(first_coupling, left)
    once = trial - jnp.where(
        at_start,
        times(first_inverse, down_left),
        jnp.where(at_end, times(last_inverse, up_right), 0.0),
    )
    once_ref[...] = once
    left_once = turn(left, -1) - times(left_inverse, times_transposed(first_coupling, start))
    right_once = turn(right, 1) - times(right_inverse, times(right_coupling, start))
    left_twice = left_once + times(
        left_inverse,
        turn(left, -2) - times(left_diag, left_once) - times_transposed(first_coupling, once),
    )
    right_twice = right_once + times(
        right_inverse,
        turn(right, 2) - times(right_diag, right_once) - times(right_coupling, once),
    )

    upward = operate(
        diag, coupling, once_ref, work_ref, jnp.where(at_start, left_once, turn(once, 1))
    )
    upper = jnp.where(at_end, times_transposed(right_coupling, right_once), turn(upward, -1))
    defect = rhs[...] - (work_ref[...] + upper)
    apply_blocks(inverse, defect, once_ref, twice_ref)
    twice = twice_ref[...]
    upward = operate(
        diag, coupling, twice_ref, work_ref, jnp.where(at_start, left_twice, turn(twice, 1))
    )
    upper = jnp.where(at_end, times_transposed(right_coupling, right_twice), turn(upward, -1))
    return rhs[...] - (work_ref[...] + upper)


def chosen(aggregate, group_count, half):
    rows = group_count // 2
    local_index = jnp.broadcast_to(lax.rem(aggregate[...], group_count), (rows, aggregate.shape[1]))
    row = lax.broadcasted_iota(jnp.int32, local_index.shape, 0)
    named = (row // ROWS) * (2 * ROWS) + lax.rem(row, ROWS) + half * ROWS
    return jnp.where(local_index == named, 1.0, 0.0).astype(F32)


def second_kernel(
    group_count, rhs, guess, trial, diag, inverse, coupling, own, from_left, from_right,
    prolong, aggregate, twice, partial, work, once,
):
    residual = finish(
        rhs, guess, trial, diag, inverse, coupling, own, from_left[0], from_right[0],
        from_left.at[1:], from_right.at[1:], twice, work, once,
    )
    work[...] = residual
    pieces = apply_transposed(prolong, work)
    partial[...] = jnp.concatenate(
        [product(chosen(aggregate, group_count, half), pieces, ((1,), (1,))) for half in (0, 1)],
        axis=1,
    )


def coarse_kernel(shares, coarse_inverse, out, work, zero):
    size, own = coarse_inverse.shape[0], coarse_inverse.shape[2]
    rows = shares.shape[0] // ROWS
    share = shares[0:ROWS]
    for row in range(1, rows):
        share = share + shares[row * ROWS : (row + 1) * ROWS]
    flipped = jnp.transpose(share)
    vector = jnp.concatenate([flipped[:size], flipped[size:]], axis=1)
    zero[...] = jnp.zeros_like(vector)
    apply_blocks(coarse_inverse, vector, zero, work)
    value = jnp.transpose(work[...])
    value = jnp.concatenate([value[:ROWS], value[ROWS:]], axis=1)
    for row in range(rows):
        out[row * ROWS : (row + 1) * ROWS] = value


def third_kernel(
    group_count, rhs, twice, values, diag, inverse, coupling, own, prolong, aggregate,
    start, trial, to_right, to_left, work,
):
    size = twice.shape[0]
    spread = jnp.zeros(twice.shape, F32)
    packed = values[...]
    for half in (0, 1):
        picked = chosen(aggregate, group_count, half).astype(BF16)
        for part in three(packed):
            both = lax.dot_general(
                part, picked, (((0,), (0,)), ((), ())), preferred_element_type=F32
            )
            spread = spread + both[half * size : (half + 1) * size]
    apply_blocks(prolong, spread, twice, start)
    right, left = trial_sweep(rhs, start, diag, inverse, coupling, own[2], trial, work)
    to_right[...] = right
    to_left[...] = left


def fourth_kernel(
    rhs, start, trial, diag, inverse, coupling, own, from_left, from_right,
    left_blocks, right_blocks, twice, residual, work, once,
):
    residual[...] = finish(
        rhs, start, trial, diag, inverse, coupling, own, from_left[...], from_right[...],
        left_blocks.at[1:], right_blocks.at[1:], twice, work, once,
    )


def call(kernel, outs, scratch, *operands):
    inside = pl.BlockSpec(memory_space=pltpu.VMEM)
    single = not isinstance(outs, tuple)
    return pl.pallas_call(
        kernel,
        out_shape=outs,
        in_specs=[inside] * len(operands),
        out_specs=inside if single else (inside,) * len(outs),
        scratch_shapes=[pltpu.VMEM(shape, F32) for shape in scratch],
        compiler_params=pltpu.CompilerParams(vmem_limit_bytes=24 << 20),
    )(*operands)


def local(rhs, guess, diag_blocks, diag_inverse, coupling, prolong, coarse_inverse, aggregate):
    size, count = rhs.shape
    rows = lax.axis_size("row")
    group_count = count * rows // AGG
    own_coarse = coarse_inverse.shape[2]
    assert own_coarse == 2 * ROWS and 2 * size == count
    tile = jax.ShapeDtypeStruct((size, count), F32)
    aggregate = aggregate.reshape(1, count)

    def stack(n):
        return jax.ShapeDtypeStruct((n, size, count), F32)

    packed = jax.ShapeDtypeStruct((group_count // 2, count), F32)
    own_shape = jax.ShapeDtypeStruct((4, size, size), BF16)
    plain = (size, count)
    trial, to_right, to_left, own = call(
        first_kernel, (tile, stack(2), stack(3), own_shape), [plain, (count, size)],
        rhs, guess, diag_blocks, diag_inverse, coupling,
    )
    from_left = from_behind(to_right, 1)
    from_right = from_behind(to_left, -1)
    twice, partial = call(
        functools.partial(second_kernel, group_count), (tile, packed), [plain, plain],
        rhs, guess, trial, diag_blocks, diag_inverse, coupling, own, from_left, from_right,
        prolong, aggregate,
    )
    shares = lax.all_to_all(partial, "row", 0, 0, tiled=True)
    corrected = call(
        coarse_kernel, packed, [(size, own_coarse), (size, own_coarse)], shares, coarse_inverse
    )
    values = lax.all_to_all(corrected, "row", 0, 0, tiled=True)
    start, trial, to_right, to_left = call(
        functools.partial(third_kernel, group_count), (tile, tile, tile, tile), [plain],
        rhs, twice, values, diag_blocks, diag_inverse, coupling, own, prolong, aggregate,
    )
    next_left = from_behind(to_right, 1)
    next_right = from_behind(to_left, -1)
    return call(
        fourth_kernel, (tile, tile), [plain, plain],
        rhs, start, trial, diag_blocks, diag_inverse, coupling, own, next_left, next_right,
        from_left, from_right,
    )


def solution(mesh):
    vector = P(None, BOTH)
    blocks = P(None, None, BOTH)
    return jax.shard_map(
        local,
        mesh=mesh,
        in_specs=(vector, vector, blocks, blocks, blocks, blocks, blocks, P(BOTH)),
        out_specs=(vector, vector),
        check_vma=False,
    )
```

```python
import functools

import jax
import jax.numpy as jnp
from jax import lax
from jax.experimental import pallas as pl
from jax.experimental.pallas import tpu as pltpu
from jax.sharding import PartitionSpec as P

AGG = 8
BOTH = ("grp", "row")
F32 = jnp.float32
BF16 = jnp.bfloat16
ROWS = 8
LOAD = 16


def from_behind(block, distance):
    devices = range(lax.axis_size(BOTH))
    route = [(i - distance, i) for i in devices if i - distance in devices]
    return lax.ppermute(block, BOTH, route)


def lanes(like):
    return lax.broadcasted_iota(jnp.int32, like.shape, 1)


def turn(tile, shift):
    return pltpu.roll(tile, shift % tile.shape[1], 1)


def three(tile):
    high = tile.astype(BF16)
    rest = tile - high.astype(F32)
    middle = rest.astype(BF16)
    return high, middle, (rest - middle.astype(F32)).astype(BF16)


def product(left, right, dims):
    left = left.astype(BF16)
    parts = [
        lax.dot_general(left, part, (dims, ((), ())), preferred_element_type=F32)
        for part in three(right)
    ]
    return parts[0] + (parts[1] + parts[2])


def times(block, columns):
    return product(block, columns, ((1,), (0,)))


def times_transposed(block, columns):
    return product(block, columns, ((0,), (0,)))


def operate(diag, coupling, vector_ref, out_ref, lower):
    vector = vector_ref[...]

    def step(chunk, upward):
        start = pl.multiple_of(chunk * ROWS, ROWS)
        own = vector_ref[pl.ds(start, ROWS), :]
        sums = []
        for s in range(ROWS):
            pair = coupling[start + s]
            terms = diag[start + s] * vector + pair * lower
            sums.append(jnp.sum(terms, axis=0, keepdims=True))
            upward = upward + pair * own[s : s + 1, :]
        out_ref[pl.ds(start, ROWS), :] = jnp.concatenate(sums, axis=0)
        return upward

    return loop(vector.shape[0] // ROWS, step, jnp.zeros_like(vector))


def apply_blocks(blocks, vector, base_ref, out_ref):
    def step(chunk, carry):
        start = pl.multiple_of(chunk * ROWS, ROWS)
        sums = [
            jnp.sum(blocks[start + s].astype(F32) * vector, axis=0, keepdims=True)
            for s in range(ROWS)
        ]
        base = base_ref[pl.ds(start, ROWS), :]
        out_ref[pl.ds(start, ROWS), :] = base + jnp.concatenate(sums, axis=0)
        return carry

    loop(vector.shape[0] // ROWS, step, 0)


def apply_transposed(blocks, vector_ref):
    def step(chunk, total):
        start = pl.multiple_of(chunk * ROWS, ROWS)
        own = vector_ref[pl.ds(start, ROWS), :]
        for s in range(ROWS):
            total = total + blocks[start + s].astype(F32) * own[s : s + 1, :]
        return total

    zero = jnp.zeros(vector_ref.shape, F32)
    return loop(vector_ref.shape[0] // ROWS, step, zero)


def loop(count, step, carry):
    return lax.fori_loop(0, count, step, carry, unroll=True)


def place(tile, block, row):
    shape = (tile.shape[0] // ROWS, ROWS, tile.shape[1])
    lane = lax.broadcasted_iota(jnp.int32, (1,) + shape[1:], 2)
    mine = lax.shift_right_logical(lane, 1) == row
    turned = pltpu.roll(block, 2 * row + 1, 1).reshape(shape)
    return jnp.where(mine, turned, tile.reshape(shape)).reshape(tile.shape)


def split(tile, scratch):
    size = tile.shape[0]
    scratch[...] = jnp.transpose(tile)
    return scratch[pl.ds(1, size, stride=2), :], scratch[pl.ds(0, size, stride=2), :]


def messages(rhs_ref, start, trial, upward, last_coupling):
    lane = lanes(start)
    end = start.shape[1] - 1
    to_left = rhs_ref[...] - turn(upward, -1)
    to_right = rhs_ref[...] - times(last_coupling, turn(trial, 1))
    right = jnp.where(
        lane == 0, turn(start, 1), jnp.where(lane == 1, turn(trial, 2), turn(to_right, 3))
    )
    left = jnp.where(
        lane == end, turn(start, -1), jnp.where(lane == end - 1, turn(trial, -2), turn(to_left, -3))
    )
    return right, left


def first_kernel(
    rhs_in, guess_in, diag_in, inverse_in, coupling_in, prolong_in, coarse_in, aggregate_in,
    rhs, guess, diag, inverse, coupling, prolong, coarse, aggregate,
    trial, to_right, to_left, own, diag_half, inverse_half, coupling_half, work, scratch, sems,
):
    size, count = guess.shape
    parts = diag_half.shape[0] // LOAD
    copies = [
        pltpu.make_async_copy(guess_in, guess, sems.at[0]),
        pltpu.make_async_copy(rhs_in, rhs, sems.at[1]),
    ]
    for p in range(parts):
        rows = pl.ds(p * LOAD, LOAD)
        for source, target in ((coupling_in, coupling_half), (diag_in, diag_half)):
            copies.append(
                pltpu.make_async_copy(source.at[rows], target.at[rows], sems.at[len(copies)])
            )
    for p in range(parts):
        rows = pl.ds(p * LOAD, LOAD)
        copies.append(
            pltpu.make_async_copy(inverse_in.at[rows], inverse_half.at[rows], sems.at[len(copies)])
        )
    for source, target in ((prolong_in, prolong), (coarse_in, coarse), (aggregate_in, aggregate)):
        copies.append(pltpu.make_async_copy(source, target, sems.at[len(copies)]))
    for copy in copies:
        copy.start()
    copies[0].wait()

    start = guess[...]
    lane = lanes(start)
    lower = jnp.where(lane == 0, 0.0, turn(start, 1))
    upward = jnp.zeros_like(start)
    edge = jnp.zeros_like(start)
    for chunk in range(size // ROWS):
        if chunk * ROWS % LOAD == 0:
            at = 2 + 2 * (chunk * ROWS // LOAD)
            copies[at].wait()
            copies[at + 1].wait()
        sums = []
        for i in range(chunk * ROWS, chunk * ROWS + ROWS):
            pair = coupling_half[i].astype(F32)
            block = diag_half[i].astype(F32)
            coupling[i] = pair
            diag[i] = block
            edge = place(edge, block, i)
            sums.append(jnp.sum(block * start + pair * lower, axis=0, keepdims=True))
            upward = upward + pair * guess[i : i + 1, :]
        work[pl.ds(chunk * ROWS, ROWS), :] = jnp.concatenate(sums, axis=0)
    first_diag, last_diag = split(edge, scratch.at[0])
    upper = jnp.where(lane == count - 1, 0.0, turn(upward, -1))
    copies[1].wait()
    defect = rhs[...] - (work[...] + upper)

    edge = jnp.zeros_like(start)
    for chunk in range(size // ROWS):
        if chunk * ROWS % LOAD == 0:
            copies[2 + 2 * parts + chunk * ROWS // LOAD].wait()
        rows = pl.ds(chunk * ROWS, ROWS)
        sums = []
        for i in range(chunk * ROWS, chunk * ROWS + ROWS):
            block = inverse_half[i].astype(F32)
            inverse[i] = block
            edge = place(edge, block, i)
            sums.append(jnp.sum(block * defect, axis=0, keepdims=True))
        trial[rows, :] = guess[rows, :] + jnp.concatenate(sums, axis=0)
    first_inverse, last_inverse = split(edge, scratch.at[1])

    upward = jnp.zeros_like(start)
    edge = jnp.zeros_like(start)
    for i in range(size):
        edge = place(edge, coupling[i], i)
        upward = upward + coupling[i] * trial[i : i + 1, :]
    first_coupling, last_coupling = split(edge, scratch.at[2])

    right, left = messages(rhs, start, trial[...], upward, last_coupling)
    to_right[0] = right
    to_left[0] = left
    to_right[1] = jnp.concatenate([last_diag, last_inverse], axis=1)
    to_left[1] = jnp.concatenate([first_diag, first_inverse], axis=1)
    to_left[2] = jnp.concatenate([first_coupling, first_coupling], axis=1)
    own[0] = first_coupling.astype(BF16)
    own[1] = first_inverse.astype(BF16)
    own[2] = last_coupling.astype(BF16)
    own[3] = last_inverse.astype(BF16)
    for copy in copies[-3:]:
        copy.wait()


def finish(
    rhs, start_ref, trial_ref, diag, inverse, coupling, own, left, right,
    left_blocks, right_blocks, twice_ref, work_ref, once_ref,
):
    start, trial = start_ref[...], trial_ref[...]
    size = start.shape[0]
    lane = lanes(start)
    end = start.shape[1] - 1
    at_start, at_end = lane == 0, lane == end
    left_diag, left_inverse = left_blocks[0][:, :size], left_blocks[0][:, size:]
    right_diag, right_inverse = right_blocks[0][:, :size], right_blocks[0][:, size:]
    right_coupling = right_blocks[1][:, :size]
    first_coupling, first_inverse, last_inverse = own[0], own[1], own[3]

    up_right = times_transposed(right_coupling, right)
    down_left = times(first_coupling, left)
    once = trial - jnp.where(
        at_start,
        times(first_inverse, down_left),
        jnp.where(at_end, times(last_inverse, up_right), 0.0),
    )
    once_ref[...] = once
    left_once = turn(left, -1) - times(left_inverse, times_transposed(first_coupling, start))
    right_once = turn(right, 1) - times(right_inverse, times(right_coupling, start))
    left_twice = left_once + times(
        left_inverse,
        turn(left, -2) - times(left_diag, left_once) - times_transposed(first_coupling, once),
    )
    right_twice = right_once + times(
        right_inverse,
        turn(right, 2) - times(right_diag, right_once) - times(right_coupling, once),
    )

    upward = operate(
        diag, coupling, once_ref, work_ref, jnp.where(at_start, left_once, turn(once, 1))
    )
    upper = jnp.where(at_end, times_transposed(right_coupling, right_once), turn(upward, -1))
    defect = rhs[...] - (work_ref[...] + upper)
    apply_blocks(inverse, defect, once_ref, twice_ref)
    twice = twice_ref[...]
    upward = operate(
        diag, coupling, twice_ref, work_ref, jnp.where(at_start, left_twice, turn(twice, 1))
    )
    upper = jnp.where(at_end, times_transposed(right_coupling, right_twice), turn(upward, -1))
    return rhs[...] - (work_ref[...] + upper)


def chosen(aggregate, group_count, half):
    rows = group_count // 2
    local_index = jnp.broadcast_to(lax.rem(aggregate[...], group_count), (rows, aggregate.shape[1]))
    row = lax.broadcasted_iota(jnp.int32, local_index.shape, 0)
    named = (row // ROWS) * (2 * ROWS) + lax.rem(row, ROWS) + half * ROWS
    return jnp.where(local_index == named, 1.0, 0.0).astype(F32)


def second_kernel(
    group_count, rhs, guess, trial, diag, inverse, coupling, own, from_left, from_right,
    prolong, aggregate, twice, partial, work, once,
):
    residual = finish(
        rhs, guess, trial, diag, inverse, coupling, own, from_left[0], from_right[0],
        from_left.at[1:], from_right.at[1:], twice, work, once,
    )
    work[...] = residual
    pieces = apply_transposed(prolong, work)
    partial[...] = jnp.concatenate(
        [product(chosen(aggregate, group_count, half), pieces, ((1,), (1,))) for half in (0, 1)],
        axis=1,
    )


def coarse_kernel(shares, coarse_inverse, out):
    size = coarse_inverse.shape[0]
    rows = shares.shape[0] // ROWS
    share = shares[0:ROWS]
    for row in range(1, rows):
        share = share + shares[row * ROWS : (row + 1) * ROWS]
    share = jnp.concatenate([share[:, :size], share[:, size:]], axis=0)
    lane = lanes(share)
    value = jnp.zeros_like(share)
    for i in range(size):
        total = jnp.sum(coarse_inverse[i].astype(F32) * share, axis=1, keepdims=True)
        value = jnp.where(lane == i, total, value)
    value = jnp.concatenate([value[:ROWS], value[ROWS:]], axis=1)
    for row in range(rows):
        out[row * ROWS : (row + 1) * ROWS] = value


def third_kernel(
    group_count, rhs, twice, values, diag, inverse, coupling, own, prolong, aggregate,
    start_ref, trial, to_right, to_left, work,
):
    size = twice.shape[0]
    spread = jnp.zeros(twice.shape, F32)
    packed = values[...]
    for half in (0, 1):
        picked = chosen(aggregate, group_count, half).astype(BF16)
        for part in three(packed):
            both = lax.dot_general(
                part, picked, (((0,), (0,)), ((), ())), preferred_element_type=F32
            )
            spread = spread + both[half * size : (half + 1) * size]
    apply_blocks(prolong, spread, twice, start_ref)
    start = start_ref[...]
    lane = lanes(start)
    lower = jnp.where(lane == 0, 0.0, turn(start, 1))
    upward = operate(diag, coupling, start_ref, work, lower)
    upper = jnp.where(lane == start.shape[1] - 1, 0.0, turn(upward, -1))
    apply_blocks(inverse, rhs[...] - (work[...] + upper), start_ref, trial)
    upward = apply_transposed(coupling, trial)
    right, left = messages(rhs, start, trial[...], upward, own[2])
    to_right[...] = right
    to_left[...] = left


def fourth_kernel(
    rhs, start, trial, diag, inverse, coupling, own, from_left, from_right,
    left_blocks, right_blocks, twice, residual, work, once,
):
    residual[...] = finish(
        rhs, start, trial, diag, inverse, coupling, own, from_left[...], from_right[...],
        left_blocks.at[1:], right_blocks.at[1:], twice, work, once,
    )


def call(kernel, outs, scratch, *operands, space=pltpu.VMEM):
    inside = pl.BlockSpec(memory_space=pltpu.VMEM)
    if space == pltpu.HBM:
        operands = [pltpu.with_memory_space_constraint(x, space) for x in operands]
    single = not isinstance(outs, tuple)
    return pl.pallas_call(
        kernel,
        out_shape=outs,
        in_specs=[pl.BlockSpec(memory_space=space)] * len(operands),
        out_specs=inside if single else (inside,) * len(outs),
        scratch_shapes=scratch,
        compiler_params=pltpu.CompilerParams(vmem_limit_bytes=24 << 20),
    )(*operands)


def local(rhs, guess, diag_blocks, diag_inverse, coupling, prolong, coarse_inverse, aggregate):
    size, count = rhs.shape
    rows = lax.axis_size("row")
    group_count = count * rows // AGG
    assert coarse_inverse.shape[2] == 2 * ROWS and 2 * size == count
    aggregate = aggregate.reshape(1, count)
    coarse_inverse = jnp.transpose(coarse_inverse, (0, 2, 1))

    def shape(*sizes, kind=F32):
        return jax.ShapeDtypeStruct(sizes, kind)

    tile = shape(size, count)
    blocks = shape(size, size, count)
    packed = shape(group_count // 2, count)
    plain = pltpu.VMEM((size, count), F32)
    half = pltpu.VMEM((size, size, count), BF16)
    loads = 2 + 3 * (size // LOAD) + 3
    (
        rhs, guess, diag, inverse, coupling, prolong, coarse_inverse, aggregate,
        trial, to_right, to_left, own,
    ) = call(
        first_kernel,
        (
            tile, tile, blocks, blocks, blocks,
            shape(size, size, count, kind=BF16),
            shape(*coarse_inverse.shape, kind=BF16),
            shape(1, count, kind=jnp.int32),
            tile, shape(2, size, count), shape(3, size, count), shape(4, size, size, kind=BF16),
        ),
        [
            half, half, half, plain, pltpu.VMEM((3, count, size), F32),
            pltpu.SemaphoreType.DMA((loads,)),
        ],
        rhs, guess, diag_blocks, diag_inverse, coupling, prolong, coarse_inverse, aggregate,
        space=pltpu.HBM,
    )
    from_left = from_behind(to_right, 1)
    from_right = from_behind(to_left, -1)
    twice, partial = call(
        functools.partial(second_kernel, group_count), (tile, packed), [plain, plain],
        rhs, guess, trial, diag, inverse, coupling, own, from_left, from_right,
        prolong, aggregate,
    )
    shares = lax.all_to_all(partial, "row", 0, 0, tiled=True)
    corrected = call(coarse_kernel, packed, [], shares, coarse_inverse)
    values = lax.all_to_all(corrected, "row", 0, 0, tiled=True)
    start, trial, to_right, to_left = call(
        functools.partial(third_kernel, group_count), (tile, tile, tile, tile), [plain],
        rhs, twice, values, diag, inverse, coupling, own, prolong, aggregate,
    )
    next_left = from_behind(to_right, 1)
    next_right = from_behind(to_left, -1)
    return call(
        fourth_kernel, (tile, tile), [plain, plain],
        rhs, start, trial, diag, inverse, coupling, own, next_left, next_right,
        from_left, from_right,
    )


def solution(mesh):
    vector = P(None, BOTH)
    blocks = P(None, None, BOTH)
    return jax.shard_map(
        local,
        mesh=mesh,
        in_specs=(vector, vector, blocks, blocks, blocks, blocks, blocks, P(BOTH)),
        out_specs=(vector, vector),
        check_vma=False,
    )
```

```python
import functools

import jax
import jax.numpy as jnp
from jax import lax
from jax.experimental import pallas as pl
from jax.experimental.pallas import tpu as pltpu
from jax.sharding import PartitionSpec as P

AGG = 8
BOTH = ("grp", "row")
F32 = jnp.float32
BF16 = jnp.bfloat16
ROWS = 8
LOAD = 16


def swap(block, first):
    pairs = [(i, i + 1) for i in range(first, lax.axis_size(BOTH) - 1, 2)]
    return lax.ppermute(block, BOTH, pairs + [(j, i) for i, j in pairs])


def even_device():
    return lax.rem(lax.axis_index("row"), 2) == 0


def lanes(like):
    return lax.broadcasted_iota(jnp.int32, like.shape, 1)


def turn(tile, shift):
    return pltpu.roll(tile, shift % tile.shape[1], 1)


def three(tile):
    high = tile.astype(BF16)
    rest = tile - high.astype(F32)
    middle = rest.astype(BF16)
    return high, middle, (rest - middle.astype(F32)).astype(BF16)


def product(left, right, dims):
    left = left.astype(BF16)
    parts = [
        lax.dot_general(left, part, (dims, ((), ())), preferred_element_type=F32)
        for part in three(right)
    ]
    return parts[0] + (parts[1] + parts[2])


def times(block, columns):
    return product(block, columns, ((1,), (0,)))


def times_transposed(block, columns):
    return product(block, columns, ((0,), (0,)))


def operate(diag, coupling, vector_ref, out_ref, lower):
    vector = vector_ref[...]

    def step(chunk, upward):
        start = pl.multiple_of(chunk * ROWS, ROWS)
        own = vector_ref[pl.ds(start, ROWS), :]
        sums = []
        for s in range(ROWS):
            pair = coupling[start + s]
            terms = diag[start + s] * vector + pair * lower
            sums.append(jnp.sum(terms, axis=0, keepdims=True))
            upward = upward + pair * own[s : s + 1, :]
        out_ref[pl.ds(start, ROWS), :] = jnp.concatenate(sums, axis=0)
        return upward

    return loop(vector.shape[0] // ROWS, step, jnp.zeros_like(vector))


def apply_blocks(blocks, vector, base_ref, out_ref):
    def step(chunk, carry):
        start = pl.multiple_of(chunk * ROWS, ROWS)
        sums = [
            jnp.sum(blocks[start + s].astype(F32) * vector, axis=0, keepdims=True)
            for s in range(ROWS)
        ]
        base = base_ref[pl.ds(start, ROWS), :]
        out_ref[pl.ds(start, ROWS), :] = base + jnp.concatenate(sums, axis=0)
        return carry

    loop(vector.shape[0] // ROWS, step, 0)


def apply_transposed(blocks, vector_ref):
    def step(chunk, total):
        start = pl.multiple_of(chunk * ROWS, ROWS)
        own = vector_ref[pl.ds(start, ROWS), :]
        for s in range(ROWS):
            total = total + blocks[start + s].astype(F32) * own[s : s + 1, :]
        return total

    zero = jnp.zeros(vector_ref.shape, F32)
    return loop(vector_ref.shape[0] // ROWS, step, zero)


def loop(count, step, carry):
    return lax.fori_loop(0, count, step, carry, unroll=True)


def place(tile, block, row, spacing):
    shape = (tile.shape[0] // ROWS, ROWS, tile.shape[1])
    lane = lax.broadcasted_iota(jnp.int32, (1,) + shape[1:], 2)
    mine = lax.shift_right_logical(lane, spacing // 2) == row
    turned = pltpu.roll(block, spacing * row + 1, 1).reshape(shape)
    return jnp.where(mine, turned, tile.reshape(shape)).reshape(tile.shape)


def split(tile, scratch):
    size = tile.shape[0]
    scratch[...] = jnp.transpose(tile)
    return scratch[pl.ds(1, size, stride=2), :], scratch[pl.ds(0, size, stride=2), :]


def split_more(tiles, scratch):
    half = tiles[0].shape[0] // 2
    for t in (0, 1):
        scratch[t] = jnp.transpose(tiles[t])
    return [
        jnp.concatenate([scratch[t, pl.ds(k, half, stride=4), :] for t in (0, 1)], axis=0)
        for k in (1, 2, 0)
    ]


def message(columns, rightward):
    lane = lanes(columns[0])
    middle = lane.shape[1] // 2
    shift = middle + jnp.where(rightward, 1, 0)
    tile = jnp.zeros(lane.shape, F32)
    for k, column in enumerate(columns):
        tile = jnp.where(lane == middle + k, pltpu.roll(column, shift + k, 1), tile)
    high, rest, last = three(tile)
    return high.astype(F32) + turn(rest.astype(F32), 3) + turn(last.astype(F32), 6)


def columns_of(tile):
    return tile + (turn(tile, -3) + turn(tile, -6))


def wrong(rhs_ref, vector_ref, diag, coupling, work):
    vector = vector_ref[...]
    lane = lanes(vector)
    lower = jnp.where(lane == 0, 0.0, turn(vector, 1))
    upward = operate(diag, coupling, vector_ref, work, lower)
    upper = jnp.where(lane == vector.shape[1] - 1, 0.0, turn(upward, -1))
    return rhs_ref[...] - (work[...] + upper)


def first_kernel(
    rhs_in, guess_in, diag_in, inverse_in, coupling_in, prolong_in, coarse_in, aggregate_in,
    rhs, guess, diag, inverse, coupling, prolong, coarse, aggregate,
    trial, defect_out, near, far, own, diag_half, inverse_half, coupling_half, work, scratch, sems,
):
    size, count = guess.shape
    parts = diag_half.shape[0] // LOAD
    copies = [
        pltpu.make_async_copy(guess_in, guess, sems.at[0]),
        pltpu.make_async_copy(rhs_in, rhs, sems.at[1]),
    ]
    for p in range(parts):
        rows = pl.ds(p * LOAD, LOAD)
        for source, target in ((coupling_in, coupling_half), (diag_in, diag_half)):
            copies.append(
                pltpu.make_async_copy(source.at[rows], target.at[rows], sems.at[len(copies)])
            )
    for p in range(parts):
        rows = pl.ds(p * LOAD, LOAD)
        copies.append(
            pltpu.make_async_copy(inverse_in.at[rows], inverse_half.at[rows], sems.at[len(copies)])
        )
    for source, target in ((prolong_in, prolong), (coarse_in, coarse), (aggregate_in, aggregate)):
        copies.append(pltpu.make_async_copy(source, target, sems.at[len(copies)]))
    for copy in copies:
        copy.start()
    copies[0].wait()

    start = guess[...]
    lane = lanes(start)
    lower = jnp.where(lane == 0, 0.0, turn(start, 1))
    upward = jnp.zeros_like(start)
    edge = jnp.zeros_like(start)
    for chunk in range(size // ROWS):
        if chunk * ROWS % LOAD == 0:
            at = 2 + 2 * (chunk * ROWS // LOAD)
            copies[at].wait()
            copies[at + 1].wait()
        sums = []
        for i in range(chunk * ROWS, chunk * ROWS + ROWS):
            pair = coupling_half[i].astype(F32)
            block = diag_half[i].astype(F32)
            coupling[i] = pair
            diag[i] = block
            edge = place(edge, block, i, 2)
            sums.append(jnp.sum(block * start + pair * lower, axis=0, keepdims=True))
            upward = upward + pair * guess[i : i + 1, :]
        work[pl.ds(chunk * ROWS, ROWS), :] = jnp.concatenate(sums, axis=0)
    first_diag, last_diag = split(edge, scratch.at[0])
    upper = jnp.where(lane == count - 1, 0.0, turn(upward, -1))
    copies[1].wait()
    defect = rhs[...] - (work[...] + upper)

    edge = jnp.zeros_like(start)
    for chunk in range(size // ROWS):
        if chunk * ROWS % LOAD == 0:
            copies[2 + 2 * parts + chunk * ROWS // LOAD].wait()
        rows = pl.ds(chunk * ROWS, ROWS)
        sums = []
        for i in range(chunk * ROWS, chunk * ROWS + ROWS):
            block = inverse_half[i].astype(F32)
            inverse[i] = block
            edge = place(edge, block, i, 2)
            sums.append(jnp.sum(block * defect, axis=0, keepdims=True))
        trial[rows, :] = guess[rows, :] + jnp.concatenate(sums, axis=0)
    first_inverse, last_inverse = split(edge, scratch.at[1])

    second = trial[...]
    lower = jnp.where(lane == 0, 0.0, turn(second, 1))
    upward = jnp.zeros_like(start)
    edge = [jnp.zeros_like(start), jnp.zeros_like(start)]
    for chunk in range(size // ROWS):
        sums = []
        for i in range(chunk * ROWS, chunk * ROWS + ROWS):
            pair = coupling[i]
            t, row = divmod(i, size // 2)
            edge[t] = place(edge[t], pair, row, 4)
            sums.append(jnp.sum(diag[i] * second + pair * lower, axis=0, keepdims=True))
            upward = upward + pair * trial[i : i + 1, :]
        work[pl.ds(chunk * ROWS, ROWS), :] = jnp.concatenate(sums, axis=0)
    first_coupling, second_coupling, last_coupling = split_more(edge, scratch.at[2:4])
    upper = jnp.where(lane == count - 1, 0.0, turn(upward, -1))
    defect = rhs[...] - (work[...] + upper)
    defect_out[...] = defect

    even = even_device()
    columns = (start, second, defect)
    lasts = jnp.concatenate([last_diag, last_inverse], axis=1)
    firsts = jnp.concatenate([first_diag, first_inverse], axis=1)
    link = jnp.concatenate([first_coupling, jnp.zeros_like(first_coupling)], axis=1)
    near[0] = jnp.where(even, lasts, firsts).astype(BF16)
    near[1] = (message(columns, even) + link).astype(BF16)
    far[0] = jnp.where(even, firsts, lasts).astype(BF16)
    far[1] = (message(columns, jnp.logical_not(even)) + link).astype(BF16)
    for k, block in enumerate(
        (
            first_diag, first_inverse, first_coupling, second_coupling,
            last_diag, last_inverse, last_coupling,
        )
    ):
        own[k] = block.astype(BF16)
    for copy in copies[-3:]:
        copy.wait()


def finish(
    rhs, start_ref, trial_ref, defect_ref, diag, inverse, coupling, own, near, far,
    near_blocks, far_blocks, twice_ref, work_ref,
):
    start = start_ref[...]
    size = start.shape[0]
    lane = lanes(start)
    end = start.shape[1] - 1
    middle = start.shape[1] // 2
    at_start, at_end = lane == 0, lane == end
    even = even_device()
    near, far = near[...].astype(F32), far[...].astype(F32)
    left = columns_of(jnp.where(even, far, near))
    right = columns_of(jnp.where(even, near, far))
    near_pair, far_pair = near_blocks[0].astype(F32), far_blocks[0].astype(F32)
    left_pair = jnp.where(even, far_pair, near_pair).astype(BF16)
    right_pair = jnp.where(even, near_pair, far_pair).astype(BF16)
    near_link, far_link = near_blocks[1].astype(F32), far_blocks[1].astype(F32)
    right_coupling = jnp.where(even, near_link, far_link)[:, :size].astype(BF16)
    left_diag, left_inverse = left_pair[:, :size], left_pair[:, size:]
    right_diag, right_inverse = right_pair[:, :size], right_pair[:, size:]
    (
        first_diag, first_inverse, first_coupling, second_coupling,
        last_diag, last_inverse, last_coupling,
    ) = (own[k] for k in range(7))

    def at_ends(first, last):
        return jnp.where(at_start, first, jnp.where(at_end, last, 0.0))

    down = times(first_coupling, turn(left, -middle))
    up = times_transposed(right_coupling, turn(right, middle - 1))
    change = -at_ends(times(first_inverse, down), times(last_inverse, up))
    once = trial_ref[...] + change
    left_change = times(left_inverse, times_transposed(first_coupling, -start))
    right_change = times(right_inverse, times(right_coupling, -start))
    left_once = turn(left, -middle - 1) + left_change
    right_once = turn(right, middle - 2) + right_change
    defect = (
        defect_ref[...]
        - at_ends(
            times(first_diag, change) + times(first_coupling, left_once),
            times(last_diag, change) + times_transposed(right_coupling, right_once),
        )
        - jnp.where(lane == 1, turn(times(second_coupling, change), 1), 0.0)
        - jnp.where(lane == end - 1, turn(times_transposed(last_coupling, change), -1), 0.0)
    )
    work_ref[...] = once
    apply_blocks(inverse, defect, work_ref, twice_ref)
    left_defect = (
        turn(left, -middle - 2)
        - times(left_diag, left_change)
        - times_transposed(first_coupling, once)
    )
    right_defect = (
        turn(right, middle - 3) - times(right_diag, right_change) - times(right_coupling, once)
    )
    left_twice = left_once + times(left_inverse, left_defect)
    right_twice = right_once + times(right_inverse, right_defect)
    twice = twice_ref[...]
    upward = operate(
        diag, coupling, twice_ref, work_ref, jnp.where(at_start, left_twice, turn(twice, 1))
    )
    upper = jnp.where(at_end, times_transposed(right_coupling, right_twice), turn(upward, -1))
    return rhs[...] - (work_ref[...] + upper)


def chosen(aggregate, group_count, half):
    rows = group_count // 2
    local_index = jnp.broadcast_to(lax.rem(aggregate[...], group_count), (rows, aggregate.shape[1]))
    row = lax.broadcasted_iota(jnp.int32, local_index.shape, 0)
    named = (row // ROWS) * (2 * ROWS) + lax.rem(row, ROWS) + half * ROWS
    return jnp.where(local_index == named, 1.0, 0.0).astype(F32)


def second_kernel(
    group_count, rhs, guess, trial, defect, diag, inverse, coupling, own, near, far,
    prolong, aggregate, twice, partial, work,
):
    residual = finish(
        rhs, guess, trial, defect, diag, inverse, coupling, own, near.at[1], far.at[1],
        near, far, twice, work,
    )
    work[...] = residual
    pieces = apply_transposed(prolong, work)
    partial[...] = jnp.concatenate(
        [product(chosen(aggregate, group_count, half), pieces, ((1,), (1,))) for half in (0, 1)],
        axis=1,
    )


def coarse_kernel(shares, coarse_inverse, out):
    size = coarse_inverse.shape[0]
    rows = shares.shape[0] // ROWS
    share = shares[0:ROWS]
    for row in range(1, rows):
        share = share + shares[row * ROWS : (row + 1) * ROWS]
    share = jnp.concatenate([share[:, :size], share[:, size:]], axis=0)
    lane = lanes(share)
    value = jnp.zeros_like(share)
    for i in range(size):
        total = jnp.sum(coarse_inverse[i].astype(F32) * share, axis=1, keepdims=True)
        value = jnp.where(lane == i, total, value)
    value = jnp.concatenate([value[:ROWS], value[ROWS:]], axis=1)
    for row in range(rows):
        out[row * ROWS : (row + 1) * ROWS] = value


def third_kernel(
    group_count, rhs, twice, values, diag, inverse, coupling, own, prolong, aggregate,
    start_ref, trial, defect_out, near, far, work,
):
    size = twice.shape[0]
    spread = jnp.zeros(twice.shape, F32)
    packed = values[...]
    for half in (0, 1):
        picked = chosen(aggregate, group_count, half).astype(BF16)
        for part in three(packed):
            both = lax.dot_general(
                part, picked, (((0,), (0,)), ((), ())), preferred_element_type=F32
            )
            spread = spread + both[half * size : (half + 1) * size]
    apply_blocks(prolong, spread, twice, start_ref)
    apply_blocks(inverse, wrong(rhs, start_ref, diag, coupling, work), start_ref, trial)
    defect = wrong(rhs, trial, diag, coupling, work)
    defect_out[...] = defect
    even = even_device()
    columns = (start_ref[...], trial[...], defect)
    near[...] = message(columns, even).astype(BF16)
    far[...] = message(columns, jnp.logical_not(even)).astype(BF16)


def fourth_kernel(
    rhs, start, trial, defect, diag, inverse, coupling, own, near, far, near_blocks, far_blocks,
    twice, residual, work,
):
    residual[...] = finish(
        rhs, start, trial, defect, diag, inverse, coupling, own, near, far,
        near_blocks, far_blocks, twice, work,
    )


def call(kernel, outs, scratch, *operands, space=pltpu.VMEM):
    inside = pl.BlockSpec(memory_space=pltpu.VMEM)
    if space == pltpu.HBM:
        operands = [pltpu.with_memory_space_constraint(x, space) for x in operands]
    single = not isinstance(outs, tuple)
    return pl.pallas_call(
        kernel,
        out_shape=outs,
        in_specs=[pl.BlockSpec(memory_space=space)] * len(operands),
        out_specs=inside if single else (inside,) * len(outs),
        scratch_shapes=scratch,
        compiler_params=pltpu.CompilerParams(vmem_limit_bytes=24 << 20),
    )(*operands)


def local(rhs, guess, diag_blocks, diag_inverse, coupling, prolong, coarse_inverse, aggregate):
    size, count = rhs.shape
    rows = lax.axis_size("row")
    group_count = count * rows // AGG
    assert coarse_inverse.shape[2] == 2 * ROWS and 2 * size == count and rows % 2 == 0
    aggregate = aggregate.reshape(1, count)
    coarse_inverse = jnp.transpose(coarse_inverse, (0, 2, 1))

    def shape(*sizes, kind=F32):
        return jax.ShapeDtypeStruct(sizes, kind)

    tile = shape(size, count)
    blocks = shape(size, size, count)
    packed = shape(group_count // 2, count)
    edge = shape(2, size, count, kind=BF16)
    line = shape(size, count, kind=BF16)
    plain = pltpu.VMEM((size, count), F32)
    half = pltpu.VMEM((size, size, count), BF16)
    loads = 2 + 3 * (size // LOAD) + 3
    (
        rhs, guess, diag, inverse, coupling, prolong, coarse_inverse, aggregate,
        trial, defect, near, far, own,
    ) = call(
        first_kernel,
        (
            tile, tile, blocks, blocks, blocks,
            shape(size, size, count, kind=BF16),
            shape(*coarse_inverse.shape, kind=BF16),
            shape(1, count, kind=jnp.int32),
            tile, tile, edge, edge, shape(7, size, size, kind=BF16),
        ),
        [
            half, half, half, plain, pltpu.VMEM((4, count, size), F32),
            pltpu.SemaphoreType.DMA((loads,)),
        ],
        rhs, guess, diag_blocks, diag_inverse, coupling, prolong, coarse_inverse, aggregate,
        space=pltpu.HBM,
    )
    far_blocks = swap(far, 1)
    near_blocks = swap(near, 0)
    twice, partial = call(
        functools.partial(second_kernel, group_count), (tile, packed), [plain],
        rhs, guess, trial, defect, diag, inverse, coupling, own, near_blocks, far_blocks,
        prolong, aggregate,
    )
    shares = lax.all_to_all(partial, "row", 0, 0, tiled=True)
    corrected = call(coarse_kernel, packed, [], shares, coarse_inverse)
    values = lax.all_to_all(corrected, "row", 0, 0, tiled=True)
    start, trial, defect, near, far = call(
        functools.partial(third_kernel, group_count), (tile, tile, tile, line, line), [plain],
        rhs, twice, values, diag, inverse, coupling, own, prolong, aggregate,
    )
    far = swap(far, 1)
    near = swap(near, 0)
    return call(
        fourth_kernel, (tile, tile), [plain],
        rhs, start, trial, defect, diag, inverse, coupling, own, near, far,
        near_blocks, far_blocks,
    )


def solution(mesh):
    vector = P(None, BOTH)
    blocks = P(None, None, BOTH)
    return jax.shard_map(
        local,
        mesh=mesh,
        in_specs=(vector, vector, blocks, blocks, blocks, blocks, blocks, P(BOTH)),
        out_specs=(vector, vector),
        check_vma=False,
    )
```

```python
import functools

import jax
import jax.numpy as jnp
from jax import lax
from jax.experimental import pallas as pl
from jax.experimental.pallas import tpu as pltpu
from jax.sharding import PartitionSpec as P

AGG = 8
BOTH = ("grp", "row")
F32 = jnp.float32
BF16 = jnp.bfloat16
ROWS = 8
LOAD = 16


def swap(block, first):
    pairs = [(i, i + 1) for i in range(first, lax.axis_size(BOTH) - 1, 2)]
    return lax.ppermute(block, BOTH, pairs + [(j, i) for i, j in pairs])


def even_device():
    return lax.rem(lax.axis_index("row"), 2) == 0


def lanes(like):
    return lax.broadcasted_iota(jnp.int32, like.shape, 1)


def turn(tile, shift):
    return pltpu.roll(tile, shift % tile.shape[1], 1)


def three(tile):
    high = tile.astype(BF16)
    rest = tile - high.astype(F32)
    middle = rest.astype(BF16)
    return high, middle, (rest - middle.astype(F32)).astype(BF16)


def product(left, right, dims):
    left = left.astype(BF16)
    parts = [
        lax.dot_general(left, part, (dims, ((), ())), preferred_element_type=F32)
        for part in three(right)
    ]
    return parts[0] + (parts[1] + parts[2])


def stack(rows):
    return jnp.concatenate([part.astype(F32) for part in three(rows)], axis=0)


def one(block, row, transposed=False):
    row = jnp.broadcast_to(row, (2 * ROWS, row.shape[1]))
    place = lax.broadcasted_iota(jnp.int32, row.shape, 0)
    high, middle, low = (part.astype(F32) for part in three(row))
    parts = jnp.where(
        place == 0, high, jnp.where(place == 1, middle, jnp.where(place == 2, low, 0.0))
    )
    dims = ((1,), (0,)) if transposed else ((1,), (1,))
    both = lax.dot_general(
        parts.astype(BF16), block, (dims, ((), ())), preferred_element_type=F32
    )
    return jnp.sum(both, axis=0, keepdims=True)


def at_ends(count, first, second, before_last, last):
    rest = jnp.zeros((ROWS - 4, first.shape[1]), F32)
    parts = stack(jnp.concatenate([first, second, before_last, last, rest], axis=0))
    spare = jnp.zeros((ROWS, first.shape[1]), F32)
    parts = jnp.concatenate([parts, spare], axis=0).astype(BF16)
    shape = (4 * ROWS, count)
    row = lax.rem(lax.broadcasted_iota(jnp.int32, shape, 0), ROWS)
    lane = lax.broadcasted_iota(jnp.int32, shape, 1)
    target = jnp.where(row < 2, row, jnp.where(row < 4, row + (count - 4), -1))
    chosen_lane = jnp.where(lane == target, 1.0, 0.0).astype(BF16)
    return lax.dot_general(
        parts, chosen_lane, (((0,), (0,)), ((), ())), preferred_element_type=F32
    )


def operate(diag, coupling, vector_ref, out_ref, lower):
    vector = vector_ref[...]

    def step(chunk, upward):
        start = pl.multiple_of(chunk * ROWS, ROWS)
        own = vector_ref[pl.ds(start, ROWS), :]
        sums = []
        for s in range(ROWS):
            pair = coupling[start + s]
            terms = diag[start + s] * vector + pair * lower
            sums.append(jnp.sum(terms, axis=0, keepdims=True))
            upward = upward + pair * own[s : s + 1, :]
        out_ref[pl.ds(start, ROWS), :] = jnp.concatenate(sums, axis=0)
        return upward

    return loop(vector.shape[0] // ROWS, step, jnp.zeros_like(vector))


def apply_blocks(blocks, vector, base_ref, out_ref):
    def step(chunk, carry):
        start = pl.multiple_of(chunk * ROWS, ROWS)
        sums = [
            jnp.sum(blocks[start + s].astype(F32) * vector, axis=0, keepdims=True)
            for s in range(ROWS)
        ]
        base = base_ref[pl.ds(start, ROWS), :]
        out_ref[pl.ds(start, ROWS), :] = base + jnp.concatenate(sums, axis=0)
        return carry

    loop(vector.shape[0] // ROWS, step, 0)


def apply_transposed(blocks, vector_ref):
    def step(chunk, total):
        start = pl.multiple_of(chunk * ROWS, ROWS)
        own = vector_ref[pl.ds(start, ROWS), :]
        for s in range(ROWS):
            total = total + blocks[start + s].astype(F32) * own[s : s + 1, :]
        return total

    zero = jnp.zeros(vector_ref.shape, F32)
    return loop(vector_ref.shape[0] // ROWS, step, zero)


def loop(count, step, carry):
    return lax.fori_loop(0, count, step, carry, unroll=True)


def place(tile, block, row, ends):
    shape = (tile.shape[0] // ROWS, ROWS, tile.shape[1])
    lane = lax.broadcasted_iota(jnp.int32, (1,) + shape[1:], 2)
    mine = lax.shift_right_logical(lane, ends) == row
    turned = pltpu.roll(block, 2 * ends * row + ends, 1).reshape(shape)
    return jnp.where(mine, turned, tile.reshape(shape)).reshape(tile.shape)


def split(tile, scratch):
    size = tile.shape[0]
    scratch[...] = jnp.transpose(tile)
    return [scratch[pl.ds(k, size, stride=2), :] for k in (0, 1)]


def split_more(tiles, scratch):
    half = tiles[0].shape[0] // 2
    for t in (0, 1):
        scratch[t] = jnp.transpose(tiles[t])
    return [
        jnp.concatenate([scratch[t, pl.ds(k, half, stride=4), :] for t in (0, 1)], axis=0)
        for k in range(4)
    ]


def edge_rows(columns):
    lane = lanes(columns[0])
    tile = jnp.zeros(lane.shape, F32)
    for k, column in enumerate(columns):
        last = len(columns) + k
        tile = jnp.where(lane == k, turn(column, k), tile)
        tile = jnp.where(lane == last, turn(column, last + 1), tile)
    return jnp.transpose(tile)[:ROWS]


def wrong(rhs_ref, vector_ref, diag, coupling, work):
    vector = vector_ref[...]
    lane = lanes(vector)
    lower = jnp.where(lane == 0, 0.0, turn(vector, 1))
    upward = operate(diag, coupling, vector_ref, work, lower)
    upper = jnp.where(lane == vector.shape[1] - 1, 0.0, turn(upward, -1))
    return rhs_ref[...] - (work[...] + upper)


def first_kernel(
    rhs_in, guess_in, diag_in, inverse_in, coupling_in, prolong_in, coarse_in, aggregate_in,
    rhs, diag, inverse, coupling, prolong, coarse, aggregate,
    trial, defect_out, near, far, own, rows_out, guess, diag_half, inverse_half, coupling_half, work, scratch, sems,
):
    size, count = guess.shape
    parts = diag_half.shape[0] // LOAD
    copies = [
        pltpu.make_async_copy(guess_in, guess, sems.at[0]),
        pltpu.make_async_copy(rhs_in, rhs, sems.at[1]),
    ]
    for p in range(parts):
        rows = pl.ds(p * LOAD, LOAD)
        for source, target in ((coupling_in, coupling_half), (diag_in, diag_half)):
            copies.append(
                pltpu.make_async_copy(source.at[rows], target.at[rows], sems.at[len(copies)])
            )
    for p in range(parts):
        rows = pl.ds(p * LOAD, LOAD)
        copies.append(
            pltpu.make_async_copy(inverse_in.at[rows], inverse_half.at[rows], sems.at[len(copies)])
        )
    for source, target in ((prolong_in, prolong), (coarse_in, coarse), (aggregate_in, aggregate)):
        copies.append(pltpu.make_async_copy(source, target, sems.at[len(copies)]))
    for copy in copies:
        copy.start()
    copies[0].wait()

    start = guess[...]
    lane = lanes(start)
    lower = jnp.where(lane == 0, 0.0, turn(start, 1))
    upward = jnp.zeros_like(start)
    edge = jnp.zeros_like(start)
    for chunk in range(size // ROWS):
        if chunk * ROWS % LOAD == 0:
            at = 2 + 2 * (chunk * ROWS // LOAD)
            copies[at].wait()
            copies[at + 1].wait()
        sums = []
        for i in range(chunk * ROWS, chunk * ROWS + ROWS):
            pair = coupling_half[i].astype(F32)
            block = diag_half[i].astype(F32)
            coupling[i] = pair
            diag[i] = block
            edge = place(edge, block, i, 1)
            sums.append(jnp.sum(block * start + pair * lower, axis=0, keepdims=True))
            upward = upward + pair * guess[i : i + 1, :]
        work[pl.ds(chunk * ROWS, ROWS), :] = jnp.concatenate(sums, axis=0)
    last_diag, first_diag = split(edge, scratch.at[0])
    upper = jnp.where(lane == count - 1, 0.0, turn(upward, -1))
    copies[1].wait()
    defect = rhs[...] - (work[...] + upper)

    edge = [jnp.zeros_like(start), jnp.zeros_like(start)]
    for chunk in range(size // ROWS):
        if chunk * ROWS % LOAD == 0:
            copies[2 + 2 * parts + chunk * ROWS // LOAD].wait()
        rows = pl.ds(chunk * ROWS, ROWS)
        sums = []
        for i in range(chunk * ROWS, chunk * ROWS + ROWS):
            block = inverse_half[i].astype(F32)
            inverse[i] = block
            t, row = divmod(i, size // 2)
            edge[t] = place(edge[t], block, row, 2)
            sums.append(jnp.sum(block * defect, axis=0, keepdims=True))
        trial[rows, :] = guess[rows, :] + jnp.concatenate(sums, axis=0)
    inverses = split_more(edge, scratch.at[1:3])

    second = trial[...]
    lower = jnp.where(lane == 0, 0.0, turn(second, 1))
    upward = jnp.zeros_like(start)
    edge = [jnp.zeros_like(start), jnp.zeros_like(start)]
    for chunk in range(size // ROWS):
        sums = []
        for i in range(chunk * ROWS, chunk * ROWS + ROWS):
            pair = coupling[i]
            t, row = divmod(i, size // 2)
            edge[t] = place(edge[t], pair, row, 2)
            sums.append(jnp.sum(diag[i] * second + pair * lower, axis=0, keepdims=True))
            upward = upward + pair * trial[i : i + 1, :]
        work[pl.ds(chunk * ROWS, ROWS), :] = jnp.concatenate(sums, axis=0)
    couplings = split_more(edge, scratch.at[3:5])
    upper = jnp.where(lane == count - 1, 0.0, turn(upward, -1))
    defect = rhs[...] - (work[...] + upper)
    defect_out[...] = defect

    even = even_device()
    rows = edge_rows((start, second, defect))
    rows_out[...] = rows
    lasts = jnp.concatenate([last_diag, inverses[1]], axis=1)
    firsts = jnp.concatenate([first_diag, inverses[2]], axis=1)
    parts = jnp.concatenate([stack(rows), jnp.zeros((size - 3 * ROWS, size), F32)], axis=0)
    link = jnp.concatenate([couplings[2], parts], axis=1).astype(BF16)
    near[0] = jnp.where(even, lasts, firsts).astype(BF16)
    near[1] = link
    far[0] = jnp.where(even, firsts, lasts).astype(BF16)
    far[1] = link
    for k, block in enumerate([last_diag, first_diag] + inverses + couplings[1:]):
        own[k] = block.astype(BF16)
    for copy in copies[-3:]:
        copy.wait()


def finish(
    rhs, trial_ref, defect_ref, diag, inverse, coupling, own, rows, near, far,
    near_blocks, far_blocks, twice_ref, work_ref,
):
    size, count = trial_ref.shape
    even = even_device()
    apply_blocks(inverse, defect_ref[...], trial_ref, twice_ref)

    left, right = jnp.where(even, far, near), jnp.where(even, near, far)
    near_pair, far_pair = near_blocks[0].astype(F32), far_blocks[0].astype(F32)
    left_pair = jnp.where(even, far_pair, near_pair).astype(BF16)
    right_pair = jnp.where(even, near_pair, far_pair).astype(BF16)
    near_link, far_link = near_blocks[1].astype(F32), far_blocks[1].astype(F32)
    right_coupling = jnp.where(even, near_link, far_link)[:, :size].astype(BF16)
    left_diag, left_inverse = left_pair[:, :size], left_pair[:, size:]
    right_diag, right_inverse = right_pair[:, :size], right_pair[:, size:]
    (
        last_diag, first_diag,
        before_inverse, last_inverse, first_inverse, second_inverse,
        last_coupling, first_coupling, second_coupling,
    ) = (own[k] for k in range(9))
    first_start, first_trial, last_start, last_trial = (rows[k : k + 1] for k in (0, 1, 3, 4))
    left_start, left_trial, left_wrong = (left[k : k + 1] for k in (3, 4, 5))
    right_start, right_trial, right_wrong = (right[k : k + 1] for k in (0, 1, 2))

    first_change = -one(first_inverse, one(first_coupling, left_start))
    last_change = -one(last_inverse, one(right_coupling, right_start, True))
    left_change = -one(left_inverse, one(first_coupling, first_start, True))
    right_change = -one(right_inverse, one(right_coupling, last_start))
    left_once, right_once = left_trial + left_change, right_trial + right_change
    first_added = one(first_diag, first_change) + one(first_coupling, left_once)
    last_added = one(last_diag, last_change) + one(right_coupling, right_once, True)
    left_added = one(left_diag, left_change)
    left_added = left_added + one(first_coupling, first_trial + first_change, True)
    right_added = one(right_diag, right_change)
    right_added = right_added + one(right_coupling, last_trial + last_change)
    left_twice = left_once + one(left_inverse, left_wrong - left_added)
    right_twice = right_once + one(right_inverse, right_wrong - right_added)
    twice_ref[...] = twice_ref[...] + at_ends(
        count,
        first_change - one(first_inverse, first_added),
        -one(second_inverse, one(second_coupling, first_change)),
        -one(before_inverse, one(last_coupling, last_change, True)),
        last_change - one(last_inverse, last_added),
    )
    nothing = jnp.zeros_like(left_start)
    beyond = at_ends(
        count,
        one(first_coupling, left_twice), nothing, nothing,
        one(right_coupling, right_twice, True),
    )
    return wrong(rhs, twice_ref, diag, coupling, work_ref) - beyond


def chosen(aggregate, group_count, half):
    rows = group_count // 2
    local_index = jnp.broadcast_to(lax.rem(aggregate[...], group_count), (rows, aggregate.shape[1]))
    row = lax.broadcasted_iota(jnp.int32, local_index.shape, 0)
    named = (row // ROWS) * (2 * ROWS) + lax.rem(row, ROWS) + half * ROWS
    return jnp.where(local_index == named, 1.0, 0.0).astype(F32)


def second_kernel(
    group_count, rhs, trial, defect, diag, inverse, coupling, own, rows, near, far,
    prolong, aggregate, twice, partial, work,
):
    size = rhs.shape[0]
    near_rows, far_rows = (
        sum(side[1][k * ROWS : (k + 1) * ROWS, size:].astype(F32) for k in range(3))
        for side in (near, far)
    )
    residual = finish(
        rhs, trial, defect, diag, inverse, coupling, own, rows[...], near_rows, far_rows,
        near, far, twice, work,
    )
    work[...] = residual
    pieces = apply_transposed(prolong, work)
    partial[...] = jnp.concatenate(
        [product(chosen(aggregate, group_count, half), pieces, ((1,), (1,))) for half in (0, 1)],
        axis=1,
    )


def coarse_kernel(shares, coarse_inverse, out):
    size = coarse_inverse.shape[0]
    rows = shares.shape[0] // ROWS
    share = shares[0:ROWS]
    for row in range(1, rows):
        share = share + shares[row * ROWS : (row + 1) * ROWS]
    share = jnp.concatenate([share[:, :size], share[:, size:]], axis=0)
    lane = lanes(share)
    value = jnp.zeros_like(share)
    for i in range(size):
        total = jnp.sum(coarse_inverse[i].astype(F32) * share, axis=1, keepdims=True)
        value = jnp.where(lane == i, total, value)
    value = jnp.concatenate([value[:ROWS], value[ROWS:]], axis=1)
    for row in range(rows):
        out[row * ROWS : (row + 1) * ROWS] = value


def third_kernel(
    group_count, rhs, twice, values, diag, inverse, coupling, prolong, aggregate,
    trial, defect_out, rows, start_ref, work,
):
    size = twice.shape[0]
    spread = jnp.zeros(twice.shape, F32)
    packed = values[...]
    for half in (0, 1):
        picked = chosen(aggregate, group_count, half).astype(BF16)
        for part in three(packed):
            both = lax.dot_general(
                part, picked, (((0,), (0,)), ((), ())), preferred_element_type=F32
            )
            spread = spread + both[half * size : (half + 1) * size]
    apply_blocks(prolong, spread, twice, start_ref)
    apply_blocks(inverse, wrong(rhs, start_ref, diag, coupling, work), start_ref, trial)
    defect = wrong(rhs, trial, diag, coupling, work)
    defect_out[...] = defect
    rows[...] = edge_rows((start_ref[...], trial[...], defect))


def fourth_kernel(
    rhs, trial, defect, diag, inverse, coupling, own, rows, near, far, near_blocks, far_blocks,
    twice, residual, work,
):
    residual[...] = finish(
        rhs, trial, defect, diag, inverse, coupling, own, rows[...], near[...], far[...],
        near_blocks, far_blocks, twice, work,
    )


def call(kernel, outs, scratch, *operands, space=pltpu.VMEM):
    inside = pl.BlockSpec(memory_space=pltpu.VMEM)
    if space == pltpu.HBM:
        operands = [pltpu.with_memory_space_constraint(x, space) for x in operands]
    single = not isinstance(outs, tuple)
    return pl.pallas_call(
        kernel,
        out_shape=outs,
        in_specs=[pl.BlockSpec(memory_space=space)] * len(operands),
        out_specs=inside if single else (inside,) * len(outs),
        scratch_shapes=scratch,
        compiler_params=pltpu.CompilerParams(vmem_limit_bytes=24 << 20),
    )(*operands)


def local(rhs, guess, diag_blocks, diag_inverse, coupling, prolong, coarse_inverse, aggregate):
    size, count = rhs.shape
    members = lax.axis_size("row")
    group_count = count * members // AGG
    assert coarse_inverse.shape[2] == 2 * ROWS and 2 * size == count and members % 2 == 0
    aggregate = aggregate.reshape(1, count)
    coarse_inverse = jnp.transpose(coarse_inverse, (0, 2, 1))

    def shape(*sizes, kind=F32):
        return jax.ShapeDtypeStruct(sizes, kind)

    tile = shape(size, count)
    blocks = shape(size, size, count)
    packed = shape(group_count // 2, count)
    edge = shape(2, size, count, kind=BF16)
    line = shape(ROWS, size)
    plain = pltpu.VMEM((size, count), F32)
    half = pltpu.VMEM((size, size, count), BF16)
    loads = 2 + 3 * (size // LOAD) + 3
    (
        rhs, diag, inverse, coupling, prolong, coarse_inverse, aggregate,
        trial, defect, near, far, own, rows,
    ) = call(
        first_kernel,
        (
            tile, blocks, blocks, blocks,
            shape(size, size, count, kind=BF16),
            shape(*coarse_inverse.shape, kind=BF16),
            shape(1, count, kind=jnp.int32),
            tile, tile, edge, edge, shape(9, size, size, kind=BF16), line,
        ),
        [
            plain, half, half, half, plain, pltpu.VMEM((5, count, size), F32),
            pltpu.SemaphoreType.DMA((loads,)),
        ],
        rhs, guess, diag_blocks, diag_inverse, coupling, prolong, coarse_inverse, aggregate,
        space=pltpu.HBM,
    )
    far_blocks = swap(far, 1)
    near_blocks = swap(near, 0)
    twice, partial = call(
        functools.partial(second_kernel, group_count), (tile, packed), [plain],
        rhs, trial, defect, diag, inverse, coupling, own, rows, near_blocks, far_blocks,
        prolong, aggregate,
    )
    shares = lax.all_to_all(partial, "row", 0, 0, tiled=True)
    corrected = call(coarse_kernel, packed, [], shares, coarse_inverse)
    values = lax.all_to_all(corrected, "row", 0, 0, tiled=True)
    trial, defect, rows = call(
        functools.partial(third_kernel, group_count), (tile, tile, line), [plain, plain],
        rhs, twice, values, diag, inverse, coupling, prolong, aggregate,
    )
    far = swap(rows, 1)
    near = swap(rows, 0)
    return call(
        fourth_kernel, (tile, tile), [plain],
        rhs, trial, defect, diag, inverse, coupling, own, rows, near, far,
        near_blocks, far_blocks,
    )


def solution(mesh):
    vector = P(None, BOTH)
    blocks = P(None, None, BOTH)
    return jax.shard_map(
        local,
        mesh=mesh,
        in_specs=(vector, vector, blocks, blocks, blocks, blocks, blocks, P(BOTH)),
        out_specs=(vector, vector),
        check_vma=False,
    )
```

```python
import functools

import jax
import jax.numpy as jnp
from jax import lax
from jax.experimental import pallas as pl
from jax.experimental.pallas import tpu as pltpu
from jax.sharding import PartitionSpec as P

AGG = 8
BOTH = ("grp", "row")
F32 = jnp.float32
BF16 = jnp.bfloat16
ROWS = 8
LOAD = 16


def swap(block, first):
    pairs = [(i, i + 1) for i in range(first, lax.axis_size(BOTH) - 1, 2)]
    return lax.ppermute(block, BOTH, pairs + [(j, i) for i, j in pairs])


def even_device():
    return lax.rem(lax.axis_index("row"), 2) == 0


def lanes(like):
    return lax.broadcasted_iota(jnp.int32, like.shape, 1)


def turn(tile, shift):
    return pltpu.roll(tile, shift % tile.shape[1], 1)


def three(tile):
    high = tile.astype(BF16)
    rest = tile - high.astype(F32)
    middle = rest.astype(BF16)
    return high, middle, (rest - middle.astype(F32)).astype(BF16)


def product(left, right, dims):
    left = left.astype(BF16)
    parts = [
        lax.dot_general(left, part, (dims, ((), ())), preferred_element_type=F32)
        for part in three(right)
    ]
    return parts[0] + (parts[1] + parts[2])


def stack(rows):
    return jnp.concatenate([part.astype(F32) for part in three(rows)], axis=0)


def to_column(block, row):
    return jnp.sum(block * row, axis=1, keepdims=True)


def to_row(block, column):
    return jnp.sum(block * column, axis=0, keepdims=True)


def operate(diag, coupling, vector_ref, out_ref, lower):
    vector = vector_ref[...]

    def step(chunk, upward):
        start = pl.multiple_of(chunk * ROWS, ROWS)
        own = vector_ref[pl.ds(start, ROWS), :]
        sums = []
        for s in range(ROWS):
            pair = coupling[start + s]
            terms = diag[start + s] * vector + pair * lower
            sums.append(jnp.sum(terms, axis=0, keepdims=True))
            upward = upward + pair * own[s : s + 1, :]
        out_ref[pl.ds(start, ROWS), :] = jnp.concatenate(sums, axis=0)
        return upward

    return loop(vector.shape[0] // ROWS, step, jnp.zeros_like(vector))


def apply_blocks(blocks, vector, base_ref, out_ref):
    def step(chunk, carry):
        start = pl.multiple_of(chunk * ROWS, ROWS)
        sums = [
            jnp.sum(blocks[start + s].astype(F32) * vector, axis=0, keepdims=True)
            for s in range(ROWS)
        ]
        base = base_ref[pl.ds(start, ROWS), :]
        out_ref[pl.ds(start, ROWS), :] = base + jnp.concatenate(sums, axis=0)
        return carry

    loop(vector.shape[0] // ROWS, step, 0)


def apply_transposed(blocks, vector_ref):
    def step(chunk, total):
        start = pl.multiple_of(chunk * ROWS, ROWS)
        own = vector_ref[pl.ds(start, ROWS), :]
        for s in range(ROWS):
            total = total + blocks[start + s].astype(F32) * own[s : s + 1, :]
        return total

    zero = jnp.zeros(vector_ref.shape, F32)
    return loop(vector_ref.shape[0] // ROWS, step, zero)


def loop(count, step, carry):
    return lax.fori_loop(0, count, step, carry, unroll=True)


def at_lane(tile, turned, lane):
    shape = (tile.shape[0] // ROWS, ROWS, tile.shape[1])
    mine = lax.broadcasted_iota(jnp.int32, (1,) + shape[1:], 2) == lane
    return jnp.where(mine, turned.reshape(shape), tile.reshape(shape)).reshape(tile.shape)


def place(tile, block, row):
    shape = (tile.shape[0] // ROWS, ROWS, tile.shape[1])
    lane = lax.broadcasted_iota(jnp.int32, (1,) + shape[1:], 2)
    mine = lax.shift_right_logical(lane, 2) == row
    turned = pltpu.roll(block, 4 * row + 2, 1).reshape(shape)
    return jnp.where(mine, turned, tile.reshape(shape)).reshape(tile.shape)


def split_more(tiles, scratch):
    half = tiles[0].shape[0] // 2
    for t in (0, 1):
        scratch[t] = jnp.transpose(tiles[t])
    return [
        jnp.concatenate([scratch[t, pl.ds(k, half, stride=4), :] for t in (0, 1)], axis=0)
        for k in range(4)
    ]


def edge_rows(columns):
    lane = lanes(columns[0])
    tile = jnp.zeros(lane.shape, F32)
    for k, column in enumerate(columns):
        last = len(columns) + k
        tile = jnp.where(lane == k, turn(column, k), tile)
        tile = jnp.where(lane == last, turn(column, last + 1), tile)
    return jnp.transpose(tile)[:ROWS]


def wrong(rhs_ref, vector_ref, diag, coupling, work):
    vector = vector_ref[...]
    lane = lanes(vector)
    lower = jnp.where(lane == 0, 0.0, turn(vector, 1))
    upward = operate(diag, coupling, vector_ref, work, lower)
    upper = jnp.where(lane == vector.shape[1] - 1, 0.0, turn(upward, -1))
    return rhs_ref[...] - (work[...] + upper)


def first_kernel(
    rhs_in, guess_in, diag_in, inverse_in, coupling_in, prolong_in, coarse_in, aggregate_in,
    rhs, diag, inverse, coupling, prolong, coarse, aggregate,
    trial, defect_out, near, far, own, rows_out,
    guess, diag_half, inverse_half, coupling_half, work, scratch, sems,
):
    size, count = guess.shape
    parts = diag_half.shape[0] // LOAD
    copies = [
        pltpu.make_async_copy(guess_in, guess, sems.at[0]),
        pltpu.make_async_copy(rhs_in, rhs, sems.at[1]),
    ]
    for p in range(parts):
        rows = pl.ds(p * LOAD, LOAD)
        for source, target in ((coupling_in, coupling_half), (diag_in, diag_half)):
            copies.append(
                pltpu.make_async_copy(source.at[rows], target.at[rows], sems.at[len(copies)])
            )
    for p in range(parts):
        rows = pl.ds(p * LOAD, LOAD)
        copies.append(
            pltpu.make_async_copy(inverse_in.at[rows], inverse_half.at[rows], sems.at[len(copies)])
        )
    for source, target in ((prolong_in, prolong), (coarse_in, coarse), (aggregate_in, aggregate)):
        copies.append(pltpu.make_async_copy(source, target, sems.at[len(copies)]))
    for copy in copies:
        copy.start()
    copies[0].wait()

    start = guess[...]
    lane = lanes(start)
    lower = jnp.where(lane == 0, 0.0, turn(start, 1))
    upward = jnp.zeros_like(start)
    first_diag = jnp.zeros_like(start)
    last_diag = jnp.zeros_like(start)
    for chunk in range(size // ROWS):
        if chunk * ROWS % LOAD == 0:
            at = 2 + 2 * (chunk * ROWS // LOAD)
            copies[at].wait()
            copies[at + 1].wait()
        sums = []
        for i in range(chunk * ROWS, chunk * ROWS + ROWS):
            pair = coupling_half[i].astype(F32)
            block = diag_half[i].astype(F32)
            coupling[i] = pair
            diag[i] = block
            turned = turn(block, i)
            first_diag = at_lane(first_diag, turned, i)
            last_diag = at_lane(last_diag, turned, (i - 1) % count)
            sums.append(jnp.sum(block * start + pair * lower, axis=0, keepdims=True))
            upward = upward + pair * guess[i : i + 1, :]
        work[pl.ds(chunk * ROWS, ROWS), :] = jnp.concatenate(sums, axis=0)
    last_diag = turn(last_diag, 1)
    upper = jnp.where(lane == count - 1, 0.0, turn(upward, -1))
    copies[1].wait()
    defect = rhs[...] - (work[...] + upper)

    edge = [jnp.zeros_like(start), jnp.zeros_like(start)]
    for chunk in range(size // ROWS):
        if chunk * ROWS % LOAD == 0:
            copies[2 + 2 * parts + chunk * ROWS // LOAD].wait()
        rows = pl.ds(chunk * ROWS, ROWS)
        sums = []
        for i in range(chunk * ROWS, chunk * ROWS + ROWS):
            block = inverse_half[i].astype(F32)
            inverse[i] = block
            t, row = divmod(i, size // 2)
            edge[t] = place(edge[t], block, row)
            sums.append(jnp.sum(block * defect, axis=0, keepdims=True))
        trial[rows, :] = guess[rows, :] + jnp.concatenate(sums, axis=0)
    inverses = split_more(edge, scratch.at[0:2])

    second = trial[...]
    lower = jnp.where(lane == 0, 0.0, turn(second, 1))
    upward = jnp.zeros_like(start)
    edge = [jnp.zeros_like(start), jnp.zeros_like(start)]
    for chunk in range(size // ROWS):
        sums = []
        for i in range(chunk * ROWS, chunk * ROWS + ROWS):
            pair = coupling[i]
            t, row = divmod(i, size // 2)
            edge[t] = place(edge[t], pair, row)
            sums.append(jnp.sum(diag[i] * second + pair * lower, axis=0, keepdims=True))
            upward = upward + pair * trial[i : i + 1, :]
        work[pl.ds(chunk * ROWS, ROWS), :] = jnp.concatenate(sums, axis=0)
    couplings = split_more(edge, scratch.at[2:4])
    upper = jnp.where(lane == count - 1, 0.0, turn(upward, -1))
    defect = rhs[...] - (work[...] + upper)
    defect_out[...] = defect

    even = even_device()
    rows = edge_rows((start, second, defect))
    rows_out[...] = rows
    scratch[4] = jnp.transpose(jnp.concatenate(couplings[2:], axis=1))
    first_turned, second_turned = scratch[4, :size], scratch[4, size:]
    last_diag, first_diag = last_diag[:, :size], first_diag[:, :size]
    lasts = jnp.concatenate([last_diag, inverses[1]], axis=1)
    firsts = jnp.concatenate([first_diag, inverses[2]], axis=1)
    link = jnp.concatenate([couplings[2], first_turned], axis=1).astype(BF16)
    near[:size] = jnp.where(even, lasts, firsts).astype(BF16)
    far[:size] = jnp.where(even, firsts, lasts).astype(BF16)
    parts = jnp.concatenate([stack(rows), jnp.zeros((ROWS, size), F32)], axis=0)
    parts = jnp.concatenate([parts, parts], axis=1).astype(BF16)
    for side in (near, far):
        side[size : 2 * size] = link
        side[2 * size :] = parts
    own[0] = last_diag
    own[1] = first_diag
    for k in range(4):
        own[2 + k] = inverses[k]
    own[6] = couplings[1]
    own[7] = couplings[2]
    own[8] = first_turned
    own[9] = second_turned
    for copy in copies[-3:]:
        copy.wait()


def finish(
    rhs, trial_ref, defect_ref, diag, inverse, coupling, own, rows, near, far,
    near_blocks, far_blocks, twice_ref, work_ref,
):
    size, count = trial_ref.shape
    even = even_device()
    apply_blocks(inverse, defect_ref[...], trial_ref, twice_ref)

    left, right = jnp.where(even, far, near), jnp.where(even, near, far)
    near_all, far_all = near_blocks[: 2 * size].astype(F32), far_blocks[: 2 * size].astype(F32)
    left_all, right_all = jnp.where(even, far_all, near_all), jnp.where(even, near_all, far_all)
    left_diag, left_inverse = left_all[:size, :size], left_all[:size, size:]
    right_diag, right_inverse = right_all[:size, :size], right_all[:size, size:]
    right_coupling, right_turned = right_all[size:, :size], right_all[size:, size:]
    last_diag, first_diag = own[0], own[1]
    before_inverse, last_inverse, first_inverse, second_inverse = (own[2 + k] for k in range(4))
    last_coupling, first_coupling, first_turned, second_turned = (own[6 + k] for k in range(4))
    shape = (size, size)
    unit = lax.broadcasted_iota(jnp.int32, shape, 0) == lax.broadcasted_iota(jnp.int32, shape, 1)

    def column(row):
        return jnp.sum(jnp.where(unit, row, 0.0), axis=1, keepdims=True)

    first_start, first_trial, last_start, last_trial = (
        column(rows[k : k + 1]) for k in (0, 1, 3, 4)
    )
    left_start, left_trial, right_start, right_trial = (
        column(side[k : k + 1]) for side, k in ((left, 3), (left, 4), (right, 0), (right, 1))
    )
    left_wrong, right_wrong = left[5:6], right[2:3]

    first_change = -to_column(first_inverse, to_row(first_turned, left_start))
    last_change = -to_column(last_inverse, to_row(right_coupling, right_start))
    left_change = -to_column(left_inverse, to_row(first_coupling, first_start))
    right_change = -to_column(right_inverse, to_row(right_turned, last_start))
    left_once, right_once = left_trial + left_change, right_trial + right_change
    first_added = to_row(first_diag, first_change) + to_row(first_turned, left_once)
    last_added = to_row(last_diag, last_change) + to_row(right_coupling, right_once)
    left_added = to_row(left_diag, left_change)
    left_added = left_added + to_row(first_coupling, first_trial + first_change)
    right_added = to_row(right_diag, right_change)
    right_added = right_added + to_row(right_turned, last_trial + last_change)
    left_twice = left_once + to_column(left_inverse, left_wrong - left_added)
    right_twice = right_once + to_column(right_inverse, right_wrong - right_added)
    second_added = to_row(second_turned, first_change)
    before_added = to_row(last_coupling, last_change)
    lane = lax.broadcasted_iota(jnp.int32, (size, count), 1)
    twice_ref[...] = twice_ref[...] + jnp.where(
        lane == 0,
        first_change - to_column(first_inverse, first_added),
        jnp.where(
            lane == 1,
            -to_column(second_inverse, second_added),
            jnp.where(
                lane == count - 2,
                -to_column(before_inverse, before_added),
                jnp.where(
                    lane == count - 1, last_change - to_column(last_inverse, last_added), 0.0
                ),
            ),
        ),
    )
    beyond = jnp.where(
        lane == 0,
        column(to_row(first_turned, left_twice)),
        jnp.where(lane == count - 1, column(to_row(right_coupling, right_twice)), 0.0),
    )
    return wrong(rhs, twice_ref, diag, coupling, work_ref) - beyond


def chosen(aggregate, group_count, half):
    rows = group_count // 2
    local_index = jnp.broadcast_to(lax.rem(aggregate[...], group_count), (rows, aggregate.shape[1]))
    row = lax.broadcasted_iota(jnp.int32, local_index.shape, 0)
    named = (row // ROWS) * (2 * ROWS) + lax.rem(row, ROWS) + half * ROWS
    return jnp.where(local_index == named, 1.0, 0.0).astype(F32)


def second_kernel(
    group_count, rhs, trial, defect, diag, inverse, coupling, own, rows, near, far,
    prolong, aggregate, twice, partial, work,
):
    size = rhs.shape[0]
    near_rows, far_rows = (
        sum(
            side[2 * size :, :size].astype(F32)[k * ROWS : (k + 1) * ROWS] for k in range(3)
        )
        for side in (near, far)
    )
    residual = finish(
        rhs, trial, defect, diag, inverse, coupling, own, rows[...], near_rows, far_rows,
        near, far, twice, work,
    )
    work[...] = residual
    pieces = apply_transposed(prolong, work)
    partial[...] = jnp.concatenate(
        [product(chosen(aggregate, group_count, half), pieces, ((1,), (1,))) for half in (0, 1)],
        axis=1,
    )


def coarse_kernel(shares, coarse_inverse, out):
    size = coarse_inverse.shape[0]
    rows = shares.shape[0] // ROWS
    share = shares[0:ROWS]
    for row in range(1, rows):
        share = share + shares[row * ROWS : (row + 1) * ROWS]
    share = jnp.concatenate([share[:, :size], share[:, size:]], axis=0)
    lane = lanes(share)
    value = jnp.zeros_like(share)
    for i in range(size):
        total = jnp.sum(coarse_inverse[i].astype(F32) * share, axis=1, keepdims=True)
        value = jnp.where(lane == i, total, value)
    value = jnp.concatenate([value[:ROWS], value[ROWS:]], axis=1)
    for row in range(rows):
        out[row * ROWS : (row + 1) * ROWS] = value


def third_kernel(
    group_count, rhs, twice, values, diag, inverse, coupling, prolong, aggregate,
    trial, defect_out, rows, start_ref, work,
):
    size = twice.shape[0]
    spread = jnp.zeros(twice.shape, F32)
    packed = values[...]
    for half in (0, 1):
        picked = chosen(aggregate, group_count, half).astype(BF16)
        for part in three(packed):
            both = lax.dot_general(
                part, picked, (((0,), (0,)), ((), ())), preferred_element_type=F32
            )
            spread = spread + both[half * size : (half + 1) * size]
    apply_blocks(prolong, spread, twice, start_ref)
    apply_blocks(inverse, wrong(rhs, start_ref, diag, coupling, work), start_ref, trial)
    defect = wrong(rhs, trial, diag, coupling, work)
    defect_out[...] = defect
    rows[...] = edge_rows((start_ref[...], trial[...], defect))


def fourth_kernel(
    rhs, trial, defect, diag, inverse, coupling, own, rows, near, far, near_blocks, far_blocks,
    twice, residual, work,
):
    residual[...] = finish(
        rhs, trial, defect, diag, inverse, coupling, own, rows[...], near[...], far[...],
        near_blocks, far_blocks, twice, work,
    )


def call(kernel, outs, scratch, *operands, space=pltpu.VMEM):
    inside = pl.BlockSpec(memory_space=pltpu.VMEM)
    if space == pltpu.HBM:
        operands = [pltpu.with_memory_space_constraint(x, space) for x in operands]
    single = not isinstance(outs, tuple)
    return pl.pallas_call(
        kernel,
        out_shape=outs,
        in_specs=[pl.BlockSpec(memory_space=space)] * len(operands),
        out_specs=inside if single else (inside,) * len(outs),
        scratch_shapes=scratch,
        compiler_params=pltpu.CompilerParams(vmem_limit_bytes=24 << 20),
    )(*operands)


def local(rhs, guess, diag_blocks, diag_inverse, coupling, prolong, coarse_inverse, aggregate):
    size, count = rhs.shape
    members = lax.axis_size("row")
    group_count = count * members // AGG
    assert coarse_inverse.shape[2] == 2 * ROWS and 2 * size == count and members % 2 == 0
    aggregate = aggregate.reshape(1, count)
    coarse_inverse = jnp.transpose(coarse_inverse, (0, 2, 1))

    def shape(*sizes, kind=F32):
        return jax.ShapeDtypeStruct(sizes, kind)

    tile = shape(size, count)
    blocks = shape(size, size, count)
    packed = shape(group_count // 2, count)
    edge = shape(2 * size + 4 * ROWS, count, kind=BF16)
    line = shape(ROWS, size)
    plain = pltpu.VMEM((size, count), F32)
    half = pltpu.VMEM((size, size, count), BF16)
    loads = 2 + 3 * (size // LOAD) + 3
    (
        rhs, diag, inverse, coupling, prolong, coarse_inverse, aggregate,
        trial, defect, near, far, own, rows,
    ) = call(
        first_kernel,
        (
            tile, blocks, blocks, blocks,
            shape(size, size, count, kind=BF16),
            shape(*coarse_inverse.shape, kind=BF16),
            shape(1, count, kind=jnp.int32),
            tile, tile, edge, edge, shape(10, size, size), line,
        ),
        [
            plain, half, half, half, plain, pltpu.VMEM((5, count, size), F32),
            pltpu.SemaphoreType.DMA((loads,)),
        ],
        rhs, guess, diag_blocks, diag_inverse, coupling, prolong, coarse_inverse, aggregate,
        space=pltpu.HBM,
    )
    far_blocks = swap(far, 1)
    near_blocks = swap(near, 0)
    twice, partial = call(
        functools.partial(second_kernel, group_count), (tile, packed), [plain],
        rhs, trial, defect, diag, inverse, coupling, own, rows, near_blocks, far_blocks,
        prolong, aggregate,
    )
    shares = lax.all_to_all(partial, "row", 0, 0, tiled=True)
    corrected = call(coarse_kernel, packed, [], shares, coarse_inverse)
    values = lax.all_to_all(corrected, "row", 0, 0, tiled=True)
    trial, defect, rows = call(
        functools.partial(third_kernel, group_count), (tile, tile, line), [plain, plain],
        rhs, twice, values, diag, inverse, coupling, prolong, aggregate,
    )
    far = swap(rows, 1)
    near = swap(rows, 0)
    return call(
        fourth_kernel, (tile, tile), [plain],
        rhs, trial, defect, diag, inverse, coupling, own, rows, near, far,
        near_blocks, far_blocks,
    )


def solution(mesh):
    vector = P(None, BOTH)
    blocks = P(None, None, BOTH)
    return jax.shard_map(
        local,
        mesh=mesh,
        in_specs=(vector, vector, blocks, blocks, blocks, blocks, blocks, P(BOTH)),
        out_specs=(vector, vector),
        check_vma=False,
    )
```

```python
import functools

import jax
import jax.numpy as jnp
from jax import lax
from jax.experimental import pallas as pl
from jax.experimental.pallas import tpu as pltpu
from jax.sharding import PartitionSpec as P

AGG = 8
BOTH = ("grp", "row")
F32 = jnp.float32
BF16 = jnp.bfloat16
ROWS = 8
LOAD = 16
EDGES = 24
EDGE_ROWS = 10


def swap(block, first):
    pairs = [(i, i + 1) for i in range(first, lax.axis_size(BOTH) - 1, 2)]
    return lax.ppermute(block, BOTH, pairs + [(j, i) for i, j in pairs])


def even_device():
    return lax.rem(lax.axis_index("row"), 2) == 0


def lanes(like):
    return lax.broadcasted_iota(jnp.int32, like.shape, 1)


def turn(tile, shift):
    return pltpu.roll(tile, shift % tile.shape[1], 1)


def three(tile):
    high = tile.astype(BF16)
    rest = tile - high.astype(F32)
    middle = rest.astype(BF16)
    return high, middle, (rest - middle.astype(F32)).astype(BF16)


def product(left, right, dims):
    left = left.astype(BF16)
    parts = [
        lax.dot_general(left, part, (dims, ((), ())), preferred_element_type=F32)
        for part in three(right)
    ]
    return parts[0] + (parts[1] + parts[2])


def stack(rows):
    return jnp.concatenate([part.astype(F32) for part in three(rows)], axis=0)


def to_column(block, row):
    return jnp.sum(block * row, axis=1, keepdims=True)


def to_row(block, column):
    return jnp.sum(block * column, axis=0, keepdims=True)


def operate(diag, coupling, vector_ref, out_ref, lower):
    vector = vector_ref[...]

    def step(chunk, upward):
        start = pl.multiple_of(chunk * ROWS, ROWS)
        own = vector_ref[pl.ds(start, ROWS), :]
        sums = []
        for s in range(ROWS):
            pair = coupling[start + s]
            terms = diag[start + s] * vector + pair * lower
            sums.append(jnp.sum(terms, axis=0, keepdims=True))
            upward = upward + pair * own[s : s + 1, :]
        out_ref[pl.ds(start, ROWS), :] = jnp.concatenate(sums, axis=0)
        return upward

    return loop(vector.shape[0] // ROWS, step, jnp.zeros_like(vector))


def apply_blocks(blocks, vector, base_ref, out_ref):
    def step(chunk, carry):
        start = pl.multiple_of(chunk * ROWS, ROWS)
        sums = [
            jnp.sum(blocks[start + s].astype(F32) * vector, axis=0, keepdims=True)
            for s in range(ROWS)
        ]
        base = base_ref[pl.ds(start, ROWS), :]
        out_ref[pl.ds(start, ROWS), :] = base + jnp.concatenate(sums, axis=0)
        return carry

    loop(vector.shape[0] // ROWS, step, 0)


def apply_transposed(blocks, vector_ref):
    def step(chunk, total):
        start = pl.multiple_of(chunk * ROWS, ROWS)
        own = vector_ref[pl.ds(start, ROWS), :]
        for s in range(ROWS):
            total = total + blocks[start + s].astype(F32) * own[s : s + 1, :]
        return total

    zero = jnp.zeros(vector_ref.shape, F32)
    return loop(vector_ref.shape[0] // ROWS, step, zero)


def loop(count, step, carry):
    return lax.fori_loop(0, count, step, carry, unroll=True)


def place(tile, block, row):
    shape = (tile.shape[0] // ROWS, ROWS, tile.shape[1])
    lane = lax.broadcasted_iota(jnp.int32, (1,) + shape[1:], 2)
    mine = lax.shift_right_logical(lane, 3) == row
    turned = pltpu.roll(block, 8 * row + 3, 1).reshape(shape)
    return jnp.where(mine, turned, tile.reshape(shape)).reshape(tile.shape)


def picker(size, width, ends):
    shape = (size * len(ends), width)
    row = lax.broadcasted_iota(jnp.int32, shape, 0)
    lane = lax.broadcasted_iota(jnp.int32, shape, 1)
    target = 8 * lax.rem(row, size) + row // size + ends[0]
    return jnp.where(lane == target, 1.0, 0.0).astype(BF16)


def end_blocks(tiles, ends):
    packed = jnp.concatenate(tiles, axis=1).astype(BF16)
    size = packed.shape[0]
    blocks = lax.dot_general(
        picker(size, packed.shape[1], ends), packed, (((1,), (1,)), ((), ())),
        preferred_element_type=F32,
    )
    return [blocks[k * size : (k + 1) * size] for k in range(len(ends))]


def end_blocks_turned(tiles, ends):
    packed = jnp.concatenate(tiles, axis=1).astype(BF16)
    return lax.dot_general(
        packed, picker(packed.shape[0], packed.shape[1], ends), (((1,), (1,)), ((), ())),
        preferred_element_type=F32,
    )


def edge_rows(firsts, lasts, count):
    lane = lanes(firsts[0][0])
    tile = jnp.zeros(lane.shape, F32)
    for k, (column, where) in enumerate(firsts + lasts):
        tile = jnp.where(lane == k, turn(column, k - where), tile)
    return jnp.transpose(tile)[:EDGES]


def wrong(rhs_ref, vector_ref, diag, coupling, work):
    vector = vector_ref[...]
    lane = lanes(vector)
    lower = jnp.where(lane == 0, 0.0, turn(vector, 1))
    upward = operate(diag, coupling, vector_ref, work, lower)
    upper = jnp.where(lane == vector.shape[1] - 1, 0.0, turn(upward, -1))
    return rhs_ref[...] - (work[...] + upper)


def first_kernel(
    rhs_in, guess_in, diag_in, inverse_in, coupling_in, prolong_in, coarse_in, aggregate_in,
    rhs, diag, inverse, coupling, prolong, coarse, aggregate,
    trial, twice, near, far, own, rows_out,
    guess, diag_half, inverse_half, coupling_half, work, sems,
):
    size, count = guess.shape
    parts = diag_half.shape[0] // LOAD
    copies = [
        pltpu.make_async_copy(guess_in, guess, sems.at[0]),
        pltpu.make_async_copy(rhs_in, rhs, sems.at[1]),
    ]
    for p in range(parts):
        rows = pl.ds(p * LOAD, LOAD)
        for source, target in ((coupling_in, coupling_half), (diag_in, diag_half)):
            copies.append(
                pltpu.make_async_copy(source.at[rows], target.at[rows], sems.at[len(copies)])
            )
    for p in range(parts):
        rows = pl.ds(p * LOAD, LOAD)
        copies.append(
            pltpu.make_async_copy(inverse_in.at[rows], inverse_half.at[rows], sems.at[len(copies)])
        )
    for source, target in ((prolong_in, prolong), (coarse_in, coarse), (aggregate_in, aggregate)):
        copies.append(pltpu.make_async_copy(source, target, sems.at[len(copies)]))
    for copy in copies:
        copy.start()
    copies[0].wait()

    start = guess[...]
    lane = lanes(start)
    lower = jnp.where(lane == 0, 0.0, turn(start, 1))
    upward = jnp.zeros_like(start)
    diag_ends = [jnp.zeros_like(start) for _ in range(4)]
    inverse_ends, coupling_ends, prolong_ends = list(diag_ends), list(diag_ends), list(diag_ends)
    for chunk in range(size // ROWS):
        if chunk * ROWS % LOAD == 0:
            at = 2 + 2 * (chunk * ROWS // LOAD)
            copies[at].wait()
            copies[at + 1].wait()
        sums = []
        for i in range(chunk * ROWS, chunk * ROWS + ROWS):
            pair = coupling_half[i].astype(F32)
            block = diag_half[i].astype(F32)
            coupling[i] = pair
            diag[i] = block
            t, row = divmod(i, size // 4)
            diag_ends[t] = place(diag_ends[t], block, row)
            sums.append(jnp.sum(block * start + pair * lower, axis=0, keepdims=True))
            upward = upward + pair * guess[i : i + 1, :]
        work[pl.ds(chunk * ROWS, ROWS), :] = jnp.concatenate(sums, axis=0)
    upper = jnp.where(lane == count - 1, 0.0, turn(upward, -1))
    copies[1].wait()
    defect = rhs[...] - (work[...] + upper)

    for chunk in range(size // ROWS):
        if chunk * ROWS % LOAD == 0:
            copies[2 + 2 * parts + chunk * ROWS // LOAD].wait()
        rows = pl.ds(chunk * ROWS, ROWS)
        sums = []
        for i in range(chunk * ROWS, chunk * ROWS + ROWS):
            block = inverse_half[i].astype(F32)
            inverse[i] = block
            t, row = divmod(i, size // 4)
            inverse_ends[t] = place(inverse_ends[t], block, row)
            sums.append(jnp.sum(block * defect, axis=0, keepdims=True))
        trial[rows, :] = guess[rows, :] + jnp.concatenate(sums, axis=0)

    second = trial[...]
    lower = jnp.where(lane == 0, 0.0, turn(second, 1))
    upward = jnp.zeros_like(start)
    for chunk in range(size // ROWS):
        sums = []
        for i in range(chunk * ROWS, chunk * ROWS + ROWS):
            pair = coupling[i]
            t, row = divmod(i, size // 4)
            coupling_ends[t] = place(coupling_ends[t], pair, row)
            sums.append(jnp.sum(diag[i] * second + pair * lower, axis=0, keepdims=True))
            upward = upward + pair * trial[i : i + 1, :]
        work[pl.ds(chunk * ROWS, ROWS), :] = jnp.concatenate(sums, axis=0)
    upper = jnp.where(lane == count - 1, 0.0, turn(upward, -1))
    defect = rhs[...] - (work[...] + upper)

    for copy in copies[-3:]:
        copy.wait()
    for chunk in range(size // ROWS):
        rows = pl.ds(chunk * ROWS, ROWS)
        sums = []
        for i in range(chunk * ROWS, chunk * ROWS + ROWS):
            t, row = divmod(i, size // 4)
            prolong_ends[t] = place(prolong_ends[t], prolong[i].astype(F32), row)
            sums.append(jnp.sum(inverse[i] * defect, axis=0, keepdims=True))
        twice[rows, :] = trial[rows, :] + jnp.concatenate(sums, axis=0)

    last = count - 1
    named = jnp.broadcast_to(aggregate[...].astype(F32), (size, count))
    after = twice[...]
    both = [(start, 0), (second, 0), (defect, 0), (after, 1), (after, 2), (rhs[...], 0), (rhs[...], 1)]
    both = both + [(named, 0), (named, 1), (named, 2)]
    rows = edge_rows(both, [(column, last - k) for column, k in both], count)
    rows_out[...] = rows
    diag_turned = end_blocks_turned(diag_ends, (1, 2, 3, 4))
    coupling_turned = end_blocks_turned(coupling_ends, (1, 2, 3, 4))
    inverses = end_blocks(inverse_ends, (1, 2, 3, 4))
    couplings = end_blocks(coupling_ends, (2, 3, 4, 5))
    prolongs = end_blocks(prolong_ends, (0, 1, 2, 3, 4, 5))
    turned_diag = [diag_turned[:, k * size : (k + 1) * size] for k in range(4)]
    turned = [coupling_turned[:, k * size : (k + 1) * size] for k in range(4)]
    lasts = (
        (turned_diag[1], inverses[1]), (couplings[0], turned[1]), (prolongs[2], prolongs[1]),
        (prolongs[0], turned[0]), (turned_diag[0], inverses[0]), (couplings[2], turned[3]),
    )
    firsts = (
        (turned_diag[2], inverses[2]), (couplings[1], turned[2]), (prolongs[3], prolongs[4]),
        (prolongs[5], couplings[3]), (turned_diag[3], inverses[3]), (couplings[2], turned[3]),
    )
    even = even_device()
    for k, (one, other) in enumerate(zip(lasts, firsts)):
        one, other = jnp.concatenate(one, axis=1), jnp.concatenate(other, axis=1)
        at = slice(k * size, (k + 1) * size)
        near[at] = jnp.where(even, one, other).astype(BF16)
        far[at] = jnp.where(even, other, one).astype(BF16)
    shares = jnp.concatenate([stack(rows), jnp.zeros((ROWS, size), F32)], axis=0)
    shares = jnp.concatenate([shares, shares], axis=1).astype(BF16)
    near[len(lasts) * size :] = shares
    far[len(lasts) * size :] = shares
    blocks = [turned_diag[1], turned_diag[2]] + inverses
    for k, block in enumerate(blocks + [couplings[0], couplings[1], turned[2], turned[3]]):
        own[k] = block


def beyond_ends(even, near, far, size):
    tiles = 6
    near_pairs = near[: tiles * size].astype(F32)
    far_pairs = far[: tiles * size].astype(F32)
    sides = []
    for pairs in (jnp.where(even, far_pairs, near_pairs), jnp.where(even, near_pairs, far_pairs)):
        pairs = [pairs[k * size : (k + 1) * size] for k in range(tiles)]
        sides.append([(pair[:, :size], pair[:, size:]) for pair in pairs])
    near_rows, far_rows = (
        sum(
            side[tiles * size :, :size].astype(F32)[k * EDGES : (k + 1) * EDGES]
            for k in range(3)
        )
        for side in (near, far)
    )
    rows = [jnp.where(even, far_rows, near_rows), jnp.where(even, near_rows, far_rows)]
    return sides, rows


def columns_from(size):
    shape = (size, size)
    unit = lax.broadcasted_iota(jnp.int32, shape, 0) == lax.broadcasted_iota(jnp.int32, shape, 1)
    return lambda row: jnp.sum(jnp.where(unit, row, 0.0), axis=1, keepdims=True)


def ends(lane, first, last):
    return jnp.where(lane == 0, first, jnp.where(lane == lane.shape[1] - 1, last, 0.0))


def second_kernel(
    group_count, rhs, trial, trial_twice, diag, coupling, own, rows, near, far,
    prolong, aggregate, twice, partial, ghosts, work,
):
    size, count = rhs.shape
    (left_blocks, right_blocks), (left, right) = beyond_ends(even_device(), near, far, size)
    column = columns_from(size)
    half = EDGE_ROWS
    (left_diag, left_inverse), (left_coupling, _), _, _, (_, left_next_inverse), _ = left_blocks
    (right_diag, right_inverse), (right_coupling, right_turned) = right_blocks[:2]
    right_next_inverse, right_next_turned = right_blocks[4][1], right_blocks[5][1]
    last_diag, first_diag = own[0], own[1]
    before_inverse, last_inverse, first_inverse, second_inverse = (own[2 + k] for k in range(4))
    last_coupling, first_coupling, first_turned, second_turned = (own[6 + k] for k in range(4))
    first_start, first_trial, last_start, last_trial = (
        column(rows[k : k + 1]) for k in (0, 1, half, half + 1)
    )
    left_start, left_trial, left_second, left_third = (
        column(left[half + k : half + k + 1]) for k in (0, 1, 3, 4)
    )
    right_start, right_trial, right_second, right_third = (
        column(right[k : k + 1]) for k in (0, 1, 3, 4)
    )
    left_wrong, right_wrong = left[half + 2 : half + 3], right[2:3]

    first_change = -to_column(first_inverse, to_row(first_turned, left_start))
    last_change = -to_column(last_inverse, to_row(right_coupling, right_start))
    left_change = -to_column(left_inverse, to_row(first_coupling, first_start))
    right_change = -to_column(right_inverse, to_row(right_turned, last_start))
    left_once, right_once = left_trial + left_change, right_trial + right_change
    first_added = to_row(first_diag, first_change) + to_row(first_turned, left_once)
    last_added = to_row(last_diag, last_change) + to_row(right_coupling, right_once)
    left_added = to_row(left_diag, left_change)
    left_added = left_added + to_row(first_coupling, first_trial + first_change)
    right_added = to_row(right_diag, right_change)
    right_added = right_added + to_row(right_turned, last_trial + last_change)
    left_twice = left_once + to_column(left_inverse, left_wrong - left_added)
    right_twice = right_once + to_column(right_inverse, right_wrong - right_added)
    left_second = left_second - to_column(left_next_inverse, to_row(left_coupling, left_change))
    right_second = right_second - to_column(
        right_next_inverse, to_row(right_next_turned, right_change)
    )
    second_added = to_row(second_turned, first_change)
    before_added = to_row(last_coupling, last_change)
    lane = lax.broadcasted_iota(jnp.int32, (size, count), 1)
    change = ends(
        lane,
        first_change - to_column(first_inverse, first_added),
        last_change - to_column(last_inverse, last_added),
    )
    change = jnp.where(lane == 1, -to_column(second_inverse, second_added), change)
    change = jnp.where(lane == count - 2, -to_column(before_inverse, before_added), change)
    twice[...] = trial_twice[...] + change
    tile = jnp.zeros((size, count), F32)
    beyond = (left_twice, left_second, left_third, right_twice, right_second, right_third)
    for k, ghost in enumerate(beyond):
        tile = jnp.where(lane == k, ghost, tile)
    ghosts[...] = tile
    added = ends(
        lane,
        column(to_row(first_turned, left_twice)),
        column(to_row(right_coupling, right_twice)),
    )
    work[...] = wrong(rhs, twice, diag, coupling, work) - added
    pieces = apply_transposed(prolong, work)
    partial[...] = jnp.concatenate(
        [product(chosen(aggregate, group_count, half), pieces, ((1,), (1,))) for half in (0, 1)],
        axis=1,
    )


def chosen(aggregate, group_count, half):
    rows = group_count // 2
    local_index = jnp.broadcast_to(lax.rem(aggregate[...], group_count), (rows, aggregate.shape[1]))
    row = lax.broadcasted_iota(jnp.int32, local_index.shape, 0)
    named = (row // ROWS) * (2 * ROWS) + lax.rem(row, ROWS) + half * ROWS
    return jnp.where(local_index == named, 1.0, 0.0).astype(F32)


def coarse_kernel(shares, coarse_inverse, out):
    size = coarse_inverse.shape[0]
    rows = shares.shape[0] // ROWS
    share = shares[0:ROWS]
    for row in range(1, rows):
        share = share + shares[row * ROWS : (row + 1) * ROWS]
    share = jnp.concatenate([share[:, :size], share[:, size:]], axis=0)
    lane = lanes(share)
    value = jnp.zeros_like(share)
    for i in range(size):
        total = jnp.sum(coarse_inverse[i].astype(F32) * share, axis=1, keepdims=True)
        value = jnp.where(lane == i, total, value)
    value = jnp.concatenate([value[:ROWS], value[ROWS:]], axis=1)
    for row in range(out.shape[0] // ROWS):
        out[row * ROWS : (row + 1) * ROWS] = value


def third_kernel(
    group_count, rhs, twice, values, diag, inverse, coupling, own, near, far, ghosts,
    prolong, aggregate, solution_out, residual, start, once, work,
):
    size, count = rhs.shape
    every = values.shape[0]
    in_group = group_count // 2
    group = pl.ds(pl.multiple_of(lax.axis_index("grp") * in_group, ROWS), in_group)
    mine = three(values[group, :])
    spread = jnp.zeros((size, count), F32)
    for half in (0, 1):
        picked = chosen(aggregate, group_count, half).astype(BF16)
        for part in mine:
            both = lax.dot_general(
                part, picked, (((0,), (0,)), ((), ())), preferred_element_type=F32
            )
            spread = spread + both[half * size : (half + 1) * size]
    apply_blocks(prolong, spread, twice, start)

    (left_blocks, right_blocks), (left, right) = beyond_ends(even_device(), near, far, size)
    column = columns_from(size)
    lane = lax.broadcasted_iota(jnp.int32, (size, count), 1)
    half = EDGE_ROWS
    blank = jnp.zeros((2, size), F32)
    names = jnp.concatenate([left[half + 7 : half + 10], right[7:10], blank], axis=0)[:, 0:1]
    source = lax.broadcasted_iota(jnp.int32, (ROWS, every), 1)
    first_name = (source // ROWS) * (2 * ROWS) + lax.rem(source, ROWS)
    everything = three(values[...])
    coarse = jnp.zeros((ROWS, size), F32)
    for k in (0, 1):
        named = jnp.where(names == (first_name + k * ROWS).astype(F32), 1.0, 0.0).astype(BF16)
        for part in everything:
            both = jnp.dot(named, part, preferred_element_type=F32)
            coarse = coarse + both[:, k * size : (k + 1) * size]

    (left_diag, left_inverse), (left_coupling, left_turned) = left_blocks[:2]
    left_next_diag, left_next_inverse = left_blocks[4]
    left_next_turned = left_blocks[3][1]
    (right_diag, right_inverse), (right_coupling, right_turned) = right_blocks[:2]
    right_next_diag, right_next_inverse = right_blocks[4]
    right_next_coupling, right_next_turned = right_blocks[5]
    right_third_coupling = right_blocks[3][1]
    first_coupling, first_turned = own[7], own[8]
    prolongs = (left_blocks[2][0], left_blocks[2][1], left_blocks[3][0])
    prolongs = prolongs + (right_blocks[2][0], right_blocks[2][1], right_blocks[3][0])
    left_x, left_y, left_z, right_x, right_y, right_z = (
        ghosts[:, k : k + 1] + to_column(block, coarse[k : k + 1])
        for k, block in enumerate(prolongs)
    )
    left_rhs, left_next_rhs = left[half + 5 : half + 6], left[half + 6 : half + 7]
    right_rhs, right_next_rhs = right[5:6], right[6:7]

    def added(left_column, right_column):
        return ends(
            lane,
            column(to_row(first_turned, left_column)),
            column(to_row(right_coupling, right_column)),
        )

    def nearest(vector, left_x, left_y, right_x, right_y):
        left_sum = to_row(left_diag, left_x) + to_row(left_turned, left_y)
        left_sum = left_sum + to_row(first_coupling, vector[:, 0:1])
        right_sum = to_row(right_diag, right_x) + to_row(right_turned, vector[:, count - 1 : count])
        right_sum = right_sum + to_row(right_next_coupling, right_y)
        return (
            left_x + to_column(left_inverse, left_rhs - left_sum),
            right_x + to_column(right_inverse, right_rhs - right_sum),
        )

    defect = wrong(rhs, start, diag, coupling, work) - added(left_x, right_x)
    left_once, right_once = nearest(start, left_x, left_y, right_x, right_y)
    left_sum = to_row(left_next_diag, left_y) + to_row(left_next_turned, left_z)
    left_sum = left_sum + to_row(left_coupling, left_x)
    left_y = left_y + to_column(left_next_inverse, left_next_rhs - left_sum)
    right_sum = to_row(right_next_diag, right_y) + to_row(right_next_turned, right_x)
    right_sum = right_sum + to_row(right_third_coupling, right_z)
    right_y = right_y + to_column(right_next_inverse, right_next_rhs - right_sum)
    apply_blocks(inverse, defect, start, once)
    defect = wrong(rhs, once, diag, coupling, work) - added(left_once, right_once)
    left_twice, right_twice = nearest(once, left_once, left_y, right_once, right_y)
    apply_blocks(inverse, defect, once, solution_out)
    defect = wrong(rhs, solution_out, diag, coupling, work)
    residual[...] = defect - added(left_twice, right_twice)


def call(kernel, outs, scratch, *operands, space=pltpu.VMEM):
    inside = pl.BlockSpec(memory_space=pltpu.VMEM)
    if space == pltpu.HBM:
        operands = [pltpu.with_memory_space_constraint(x, space) for x in operands]
    single = not isinstance(outs, tuple)
    return pl.pallas_call(
        kernel,
        out_shape=outs,
        in_specs=[pl.BlockSpec(memory_space=space)] * len(operands),
        out_specs=inside if single else (inside,) * len(outs),
        scratch_shapes=scratch,
        compiler_params=pltpu.CompilerParams(vmem_limit_bytes=24 << 20),
    )(*operands)


def local(rhs, guess, diag_blocks, diag_inverse, coupling, prolong, coarse_inverse, aggregate):
    size, count = rhs.shape
    members = lax.axis_size("row")
    group_count = count * members // AGG
    assert coarse_inverse.shape[2] == 2 * ROWS and 2 * size == count and members % 2 == 0
    aggregate = aggregate.reshape(1, count)
    coarse_inverse = jnp.transpose(coarse_inverse, (0, 2, 1))

    def shape(*sizes, kind=F32):
        return jax.ShapeDtypeStruct(sizes, kind)

    tile = shape(size, count)
    blocks = shape(size, size, count)
    packed = shape(group_count // 2, count)
    edge = shape(6 * size + 3 * EDGES + ROWS, count, kind=BF16)
    line = shape(EDGES, size)
    plain = pltpu.VMEM((size, count), F32)
    half = pltpu.VMEM((size, size, count), BF16)
    loads = 2 + 3 * (size // LOAD) + 3
    (
        rhs, diag, inverse, coupling, prolong, coarse_inverse, aggregate,
        trial, trial_twice, near, far, own, rows,
    ) = call(
        first_kernel,
        (
            tile, blocks, blocks, blocks,
            shape(size, size, count, kind=BF16),
            shape(*coarse_inverse.shape, kind=BF16),
            shape(1, count, kind=jnp.int32),
            tile, tile, edge, edge, shape(10, size, size), line,
        ),
        [
            plain, half, half, half, plain,
            pltpu.SemaphoreType.DMA((loads,)),
        ],
        rhs, guess, diag_blocks, diag_inverse, coupling, prolong, coarse_inverse, aggregate,
        space=pltpu.HBM,
    )
    far = swap(far, 1)
    near = swap(near, 0)
    twice, partial, ghosts = call(
        functools.partial(second_kernel, group_count), (tile, packed, tile), [plain],
        rhs, trial, trial_twice, diag, coupling, own, rows, near, far, prolong, aggregate,
    )
    shares = lax.all_to_all(partial, "row", 0, 0, tiled=True)
    corrected = call(
        coarse_kernel, shape(lax.axis_size(BOTH) * ROWS, count), [], shares, coarse_inverse
    )
    values = lax.all_to_all(corrected, BOTH, 0, 0, tiled=True)
    return call(
        functools.partial(third_kernel, group_count), (tile, tile), [plain, plain, plain],
        rhs, twice, values, diag, inverse, coupling, own, near, far, ghosts, prolong, aggregate,
    )


def solution(mesh):
    vector = P(None, BOTH)
    blocks = P(None, None, BOTH)
    return jax.shard_map(
        local,
        mesh=mesh,
        in_specs=(vector, vector, blocks, blocks, blocks, blocks, blocks, P(BOTH)),
        out_specs=(vector, vector),
        check_vma=False,
    )
```

```python
import functools

import jax
import jax.numpy as jnp
from jax import lax
from jax.experimental import pallas as pl
from jax.experimental.pallas import tpu as pltpu
from jax.sharding import PartitionSpec as P

AGG = 8
BOTH = ("grp", "row")
F32 = jnp.float32
BF16 = jnp.bfloat16
ROWS = 8
LOAD = 16
EDGES = 24
EDGE_ROWS = 10


def swap(block, first):
    pairs = [(i, i + 1) for i in range(first, lax.axis_size(BOTH) - 1, 2)]
    return lax.ppermute(block, BOTH, pairs + [(j, i) for i, j in pairs])


def even_device():
    return lax.rem(lax.axis_index("row"), 2) == 0


def lanes(like):
    return lax.broadcasted_iota(jnp.int32, like.shape, 1)


def turn(tile, shift):
    return pltpu.roll(tile, shift % tile.shape[1], 1)


def three(tile):
    high = tile.astype(BF16)
    rest = tile - high.astype(F32)
    middle = rest.astype(BF16)
    return high, middle, (rest - middle.astype(F32)).astype(BF16)


def product(left, right, dims):
    left = left.astype(BF16)
    parts = [
        lax.dot_general(left, part, (dims, ((), ())), preferred_element_type=F32)
        for part in three(right)
    ]
    return parts[0] + (parts[1] + parts[2])


def stack(rows):
    return jnp.concatenate([part.astype(F32) for part in three(rows)], axis=0)


def to_column(block, row):
    return jnp.sum(block * row, axis=1, keepdims=True)


def to_row(block, column):
    return jnp.sum(block * column, axis=0, keepdims=True)


def operate(diag, coupling, vector_ref, out_ref, lower):
    vector = vector_ref[...]

    def step(chunk, upward):
        start = pl.multiple_of(chunk * ROWS, ROWS)
        own = vector_ref[pl.ds(start, ROWS), :]
        sums = []
        for s in range(ROWS):
            pair = coupling[start + s]
            terms = diag[start + s] * vector + pair * lower
            sums.append(jnp.sum(terms, axis=0, keepdims=True))
            upward = upward + pair * own[s : s + 1, :]
        out_ref[pl.ds(start, ROWS), :] = jnp.concatenate(sums, axis=0)
        return upward

    return loop(vector.shape[0] // ROWS, step, jnp.zeros_like(vector))


def apply_blocks(blocks, vector, base_ref, out_ref):
    def step(chunk, carry):
        start = pl.multiple_of(chunk * ROWS, ROWS)
        sums = [
            jnp.sum(blocks[start + s].astype(F32) * vector, axis=0, keepdims=True)
            for s in range(ROWS)
        ]
        base = base_ref[pl.ds(start, ROWS), :]
        out_ref[pl.ds(start, ROWS), :] = base + jnp.concatenate(sums, axis=0)
        return carry

    loop(vector.shape[0] // ROWS, step, 0)


def apply_transposed(blocks, vector_ref):
    def step(chunk, total):
        start = pl.multiple_of(chunk * ROWS, ROWS)
        own = vector_ref[pl.ds(start, ROWS), :]
        for s in range(ROWS):
            total = total + blocks[start + s].astype(F32) * own[s : s + 1, :]
        return total

    zero = jnp.zeros(vector_ref.shape, F32)
    return loop(vector_ref.shape[0] // ROWS, step, zero)


def loop(count, step, carry):
    return lax.fori_loop(0, count, step, carry, unroll=True)


def place(tile, block, row):
    shape = (tile.shape[0] // ROWS, ROWS, tile.shape[1])
    lane = lax.broadcasted_iota(jnp.int32, (1,) + shape[1:], 2)
    mine = lax.shift_right_logical(lane, 3) == row
    turned = pltpu.roll(block, 8 * row + 3, 1).reshape(shape)
    return jnp.where(mine, turned, tile.reshape(shape)).reshape(tile.shape)


def picker(size, width, ends):
    shape = (size * len(ends), width)
    row = lax.broadcasted_iota(jnp.int32, shape, 0)
    lane = lax.broadcasted_iota(jnp.int32, shape, 1)
    target = 8 * lax.rem(row, size) + row // size + ends[0]
    return jnp.where(lane == target, 1.0, 0.0).astype(BF16)


def end_blocks(tiles, ends):
    packed = jnp.concatenate(tiles, axis=1).astype(BF16)
    size = packed.shape[0]
    blocks = lax.dot_general(
        picker(size, packed.shape[1], ends), packed, (((1,), (1,)), ((), ())),
        preferred_element_type=F32,
    )
    return [blocks[k * size : (k + 1) * size] for k in range(len(ends))]


def end_blocks_turned(tiles, ends):
    packed = jnp.concatenate(tiles, axis=1).astype(BF16)
    return lax.dot_general(
        packed, picker(packed.shape[0], packed.shape[1], ends), (((1,), (1,)), ((), ())),
        preferred_element_type=F32,
    )


def edge_rows(firsts, lasts, count):
    lane = lanes(firsts[0][0])
    tile = jnp.zeros(lane.shape, F32)
    for k, (column, where) in enumerate(firsts + lasts):
        tile = jnp.where(lane == k, turn(column, k - where), tile)
    return jnp.transpose(tile)[:EDGES]


def wrong(rhs_ref, vector_ref, diag, coupling, work):
    vector = vector_ref[...]
    lane = lanes(vector)
    lower = jnp.where(lane == 0, 0.0, turn(vector, 1))
    upward = operate(diag, coupling, vector_ref, work, lower)
    upper = jnp.where(lane == vector.shape[1] - 1, 0.0, turn(upward, -1))
    return rhs_ref[...] - (work[...] + upper)


def first_kernel(
    rhs_in, guess_in, diag_in, inverse_in, coupling_in, prolong_in, coarse_in, aggregate_in,
    rhs, diag, inverse, coupling, prolong, coarse, aggregate,
    trial, twice, near, far, own, rows_out,
    guess, diag_half, inverse_half, coupling_half, work, sems,
):
    size, count = guess.shape
    parts = diag_half.shape[0] // LOAD
    copies = [
        pltpu.make_async_copy(guess_in, guess, sems.at[0]),
        pltpu.make_async_copy(rhs_in, rhs, sems.at[1]),
    ]
    for p in range(parts):
        rows = pl.ds(p * LOAD, LOAD)
        for source, target in ((coupling_in, coupling_half), (diag_in, diag_half)):
            copies.append(
                pltpu.make_async_copy(source.at[rows], target.at[rows], sems.at[len(copies)])
            )
    for p in range(parts):
        rows = pl.ds(p * LOAD, LOAD)
        copies.append(
            pltpu.make_async_copy(inverse_in.at[rows], inverse_half.at[rows], sems.at[len(copies)])
        )
    for source, target in ((prolong_in, prolong), (coarse_in, coarse), (aggregate_in, aggregate)):
        copies.append(pltpu.make_async_copy(source, target, sems.at[len(copies)]))
    for copy in copies:
        copy.start()
    copies[0].wait()

    start = guess[...]
    lane = lanes(start)
    lower = jnp.where(lane == 0, 0.0, turn(start, 1))
    upward = jnp.zeros_like(start)
    diag_ends = [jnp.zeros_like(start) for _ in range(4)]
    inverse_ends, coupling_ends, prolong_ends = list(diag_ends), list(diag_ends), list(diag_ends)
    for chunk in range(size // ROWS):
        if chunk * ROWS % LOAD == 0:
            at = 2 + 2 * (chunk * ROWS // LOAD)
            copies[at].wait()
            copies[at + 1].wait()
        sums = []
        for i in range(chunk * ROWS, chunk * ROWS + ROWS):
            pair = coupling_half[i].astype(F32)
            block = diag_half[i].astype(F32)
            coupling[i] = pair
            diag[i] = block
            t, row = divmod(i, size // 4)
            diag_ends[t] = place(diag_ends[t], block, row)
            sums.append(jnp.sum(block * start + pair * lower, axis=0, keepdims=True))
            upward = upward + pair * guess[i : i + 1, :]
        work[pl.ds(chunk * ROWS, ROWS), :] = jnp.concatenate(sums, axis=0)
    upper = jnp.where(lane == count - 1, 0.0, turn(upward, -1))
    copies[1].wait()
    defect = rhs[...] - (work[...] + upper)

    for chunk in range(size // ROWS):
        if chunk * ROWS % LOAD == 0:
            copies[2 + 2 * parts + chunk * ROWS // LOAD].wait()
        rows = pl.ds(chunk * ROWS, ROWS)
        sums = []
        for i in range(chunk * ROWS, chunk * ROWS + ROWS):
            block = inverse_half[i].astype(F32)
            inverse[i] = block
            t, row = divmod(i, size // 4)
            inverse_ends[t] = place(inverse_ends[t], block, row)
            sums.append(jnp.sum(block * defect, axis=0, keepdims=True))
        trial[rows, :] = guess[rows, :] + jnp.concatenate(sums, axis=0)

    second = trial[...]
    lower = jnp.where(lane == 0, 0.0, turn(second, 1))
    upward = jnp.zeros_like(start)
    for chunk in range(size // ROWS):
        sums = []
        for i in range(chunk * ROWS, chunk * ROWS + ROWS):
            pair = coupling[i]
            t, row = divmod(i, size // 4)
            coupling_ends[t] = place(coupling_ends[t], pair, row)
            sums.append(jnp.sum(diag[i] * second + pair * lower, axis=0, keepdims=True))
            upward = upward + pair * trial[i : i + 1, :]
        work[pl.ds(chunk * ROWS, ROWS), :] = jnp.concatenate(sums, axis=0)
    upper = jnp.where(lane == count - 1, 0.0, turn(upward, -1))
    defect = rhs[...] - (work[...] + upper)

    for copy in copies[-3:]:
        copy.wait()
    for chunk in range(size // ROWS):
        rows = pl.ds(chunk * ROWS, ROWS)
        sums = []
        for i in range(chunk * ROWS, chunk * ROWS + ROWS):
            t, row = divmod(i, size // 4)
            prolong_ends[t] = place(prolong_ends[t], prolong[i].astype(F32), row)
            sums.append(jnp.sum(inverse[i] * defect, axis=0, keepdims=True))
        twice[rows, :] = trial[rows, :] + jnp.concatenate(sums, axis=0)

    last = count - 1
    named = jnp.broadcast_to(aggregate[...].astype(F32), (size, count))
    after = twice[...]
    both = [(start, 0), (second, 0), (defect, 0), (after, 1), (after, 2), (rhs[...], 0), (rhs[...], 1)]
    both = both + [(named, 0), (named, 1), (named, 2)]
    rows = edge_rows(both, [(column, last - k) for column, k in both], count)
    rows_out[...] = rows
    diag_turned = end_blocks_turned(diag_ends, (1, 2, 3, 4))
    coupling_turned = end_blocks_turned(coupling_ends, (1, 2, 3, 4))
    inverses = end_blocks(inverse_ends, (1, 2, 3, 4))
    couplings = end_blocks(coupling_ends, (2, 3, 4, 5))
    prolongs = end_blocks(prolong_ends, (0, 1, 2, 3, 4, 5))
    turned_diag = [diag_turned[:, k * size : (k + 1) * size] for k in range(4)]
    turned = [coupling_turned[:, k * size : (k + 1) * size] for k in range(4)]
    lasts = (
        (turned_diag[1], inverses[1]), (couplings[0], turned[1]), (prolongs[2], prolongs[1]),
        (prolongs[0], turned[0]), (turned_diag[0], inverses[0]), (couplings[2], turned[3]),
    )
    firsts = (
        (turned_diag[2], inverses[2]), (couplings[1], turned[2]), (prolongs[3], prolongs[4]),
        (prolongs[5], couplings[3]), (turned_diag[3], inverses[3]), (couplings[2], turned[3]),
    )
    even = even_device()
    for k, (one, other) in enumerate(zip(lasts, firsts)):
        one, other = jnp.concatenate(one, axis=1), jnp.concatenate(other, axis=1)
        at = slice(k * size, (k + 1) * size)
        near[at] = jnp.where(even, one, other).astype(BF16)
        far[at] = jnp.where(even, other, one).astype(BF16)
    shares = jnp.concatenate([stack(rows), jnp.zeros((ROWS, size), F32)], axis=0)
    shares = jnp.concatenate([shares, shares], axis=1).astype(BF16)
    near[len(lasts) * size :] = shares
    far[len(lasts) * size :] = shares
    blocks = [turned_diag[1], turned_diag[2]] + inverses
    for k, block in enumerate(blocks + [couplings[0], couplings[1], turned[2], turned[3]]):
        own[k] = block


def beyond_ends(even, near, far, size):
    tiles = 6
    near_pairs = near[: tiles * size].astype(F32)
    far_pairs = far[: tiles * size].astype(F32)
    sides = []
    for pairs in (jnp.where(even, far_pairs, near_pairs), jnp.where(even, near_pairs, far_pairs)):
        pairs = [pairs[k * size : (k + 1) * size] for k in range(tiles)]
        sides.append([(pair[:, :size], pair[:, size:]) for pair in pairs])
    near_rows, far_rows = (
        sum(
            side[tiles * size :, :size].astype(F32)[k * EDGES : (k + 1) * EDGES]
            for k in range(3)
        )
        for side in (near, far)
    )
    rows = [jnp.where(even, far_rows, near_rows), jnp.where(even, near_rows, far_rows)]
    return sides, rows


def columns_from(size):
    shape = (size, size)
    unit = lax.broadcasted_iota(jnp.int32, shape, 0) == lax.broadcasted_iota(jnp.int32, shape, 1)
    return lambda row: jnp.sum(jnp.where(unit, row, 0.0), axis=1, keepdims=True)


def ends(lane, first, last):
    return jnp.where(lane == 0, first, jnp.where(lane == lane.shape[1] - 1, last, 0.0))


def second_kernel(
    group_count, rhs, trial, trial_twice, diag, coupling, own, rows, far, near,
    prolong, aggregate, twice, partial, ghosts, work,
):
    size, count = rhs.shape
    (left_blocks, right_blocks), (left, right) = beyond_ends(even_device(), near, far, size)
    column = columns_from(size)
    half = EDGE_ROWS
    (left_diag, left_inverse), (left_coupling, _), _, _, (_, left_next_inverse), _ = left_blocks
    (right_diag, right_inverse), (right_coupling, right_turned) = right_blocks[:2]
    right_next_inverse, right_next_turned = right_blocks[4][1], right_blocks[5][1]
    last_diag, first_diag = own[0], own[1]
    before_inverse, last_inverse, first_inverse, second_inverse = (own[2 + k] for k in range(4))
    last_coupling, first_coupling, first_turned, second_turned = (own[6 + k] for k in range(4))
    first_start, first_trial, last_start, last_trial = (
        column(rows[k : k + 1]) for k in (0, 1, half, half + 1)
    )
    left_start, left_trial, left_second, left_third = (
        column(left[half + k : half + k + 1]) for k in (0, 1, 3, 4)
    )
    right_start, right_trial, right_second, right_third = (
        column(right[k : k + 1]) for k in (0, 1, 3, 4)
    )
    left_wrong, right_wrong = left[half + 2 : half + 3], right[2:3]

    first_change = -to_column(first_inverse, to_row(first_turned, left_start))
    last_change = -to_column(last_inverse, to_row(right_coupling, right_start))
    left_change = -to_column(left_inverse, to_row(first_coupling, first_start))
    right_change = -to_column(right_inverse, to_row(right_turned, last_start))
    left_once, right_once = left_trial + left_change, right_trial + right_change
    first_added = to_row(first_diag, first_change) + to_row(first_turned, left_once)
    last_added = to_row(last_diag, last_change) + to_row(right_coupling, right_once)
    left_added = to_row(left_diag, left_change)
    left_added = left_added + to_row(first_coupling, first_trial + first_change)
    right_added = to_row(right_diag, right_change)
    right_added = right_added + to_row(right_turned, last_trial + last_change)
    left_twice = left_once + to_column(left_inverse, left_wrong - left_added)
    right_twice = right_once + to_column(right_inverse, right_wrong - right_added)
    left_second = left_second - to_column(left_next_inverse, to_row(left_coupling, left_change))
    right_second = right_second - to_column(
        right_next_inverse, to_row(right_next_turned, right_change)
    )
    second_added = to_row(second_turned, first_change)
    before_added = to_row(last_coupling, last_change)
    lane = lax.broadcasted_iota(jnp.int32, (size, count), 1)
    change = ends(
        lane,
        first_change - to_column(first_inverse, first_added),
        last_change - to_column(last_inverse, last_added),
    )
    change = jnp.where(lane == 1, -to_column(second_inverse, second_added), change)
    change = jnp.where(lane == count - 2, -to_column(before_inverse, before_added), change)
    twice[...] = trial_twice[...] + change
    tile = jnp.zeros((size, count), F32)
    beyond = (left_twice, left_second, left_third, right_twice, right_second, right_third)
    for k, ghost in enumerate(beyond):
        tile = jnp.where(lane == k, ghost, tile)
    ghosts[...] = tile
    added = ends(
        lane,
        column(to_row(first_turned, left_twice)),
        column(to_row(right_coupling, right_twice)),
    )
    work[...] = wrong(rhs, twice, diag, coupling, work) - added
    pieces = apply_transposed(prolong, work)
    partial[...] = jnp.concatenate(
        [product(chosen(aggregate, group_count, half), pieces, ((1,), (1,))) for half in (0, 1)],
        axis=1,
    )


def chosen(aggregate, group_count, half):
    rows = group_count // 2
    local_index = jnp.broadcast_to(lax.rem(aggregate[...], group_count), (rows, aggregate.shape[1]))
    row = lax.broadcasted_iota(jnp.int32, local_index.shape, 0)
    named = (row // ROWS) * (2 * ROWS) + lax.rem(row, ROWS) + half * ROWS
    return jnp.where(local_index == named, 1.0, 0.0).astype(F32)


def coarse_kernel(shares, coarse_inverse, out):
    size = coarse_inverse.shape[0]
    rows = shares.shape[0] // ROWS
    share = shares[0:ROWS]
    for row in range(1, rows):
        share = share + shares[row * ROWS : (row + 1) * ROWS]
    share = jnp.concatenate([share[:, :size], share[:, size:]], axis=0)
    lane = lanes(share)
    value = jnp.zeros_like(share)
    for i in range(size):
        total = jnp.sum(coarse_inverse[i].astype(F32) * share, axis=1, keepdims=True)
        value = jnp.where(lane == i, total, value)
    value = jnp.concatenate([value[:ROWS], value[ROWS:]], axis=1)
    for row in range(out.shape[0] // ROWS):
        out[row * ROWS : (row + 1) * ROWS] = value


def third_kernel(
    group_count, rhs, twice, values, diag, inverse, coupling, own, near, far, ghosts,
    prolong, aggregate, solution_out, residual, start, once, work,
):
    size, count = rhs.shape
    every = values.shape[0]
    in_group = group_count // 2
    group = pl.ds(pl.multiple_of(lax.axis_index("grp") * in_group, ROWS), in_group)
    mine = three(values[group, :])
    spread = jnp.zeros((size, count), F32)
    for half in (0, 1):
        picked = chosen(aggregate, group_count, half).astype(BF16)
        for part in mine:
            both = lax.dot_general(
                part, picked, (((0,), (0,)), ((), ())), preferred_element_type=F32
            )
            spread = spread + both[half * size : (half + 1) * size]
    apply_blocks(prolong, spread, twice, start)

    (left_blocks, right_blocks), (left, right) = beyond_ends(even_device(), near, far, size)
    column = columns_from(size)
    lane = lax.broadcasted_iota(jnp.int32, (size, count), 1)
    half = EDGE_ROWS
    blank = jnp.zeros((2, size), F32)
    names = jnp.concatenate([left[half + 7 : half + 10], right[7:10], blank], axis=0)[:, 0:1]
    source = lax.broadcasted_iota(jnp.int32, (ROWS, every), 1)
    first_name = (source // ROWS) * (2 * ROWS) + lax.rem(source, ROWS)
    everything = three(values[...])
    coarse = jnp.zeros((ROWS, size), F32)
    for k in (0, 1):
        named = jnp.where(names == (first_name + k * ROWS).astype(F32), 1.0, 0.0).astype(BF16)
        for part in everything:
            both = jnp.dot(named, part, preferred_element_type=F32)
            coarse = coarse + both[:, k * size : (k + 1) * size]

    (left_diag, left_inverse), (left_coupling, left_turned) = left_blocks[:2]
    left_next_diag, left_next_inverse = left_blocks[4]
    left_next_turned = left_blocks[3][1]
    (right_diag, right_inverse), (right_coupling, right_turned) = right_blocks[:2]
    right_next_diag, right_next_inverse = right_blocks[4]
    right_next_coupling, right_next_turned = right_blocks[5]
    right_third_coupling = right_blocks[3][1]
    first_coupling, first_turned = own[7], own[8]
    prolongs = (left_blocks[2][0], left_blocks[2][1], left_blocks[3][0])
    prolongs = prolongs + (right_blocks[2][0], right_blocks[2][1], right_blocks[3][0])
    left_x, left_y, left_z, right_x, right_y, right_z = (
        ghosts[:, k : k + 1] + to_column(block, coarse[k : k + 1])
        for k, block in enumerate(prolongs)
    )
    left_rhs, left_next_rhs = left[half + 5 : half + 6], left[half + 6 : half + 7]
    right_rhs, right_next_rhs = right[5:6], right[6:7]

    def added(left_column, right_column):
        return ends(
            lane,
            column(to_row(first_turned, left_column)),
            column(to_row(right_coupling, right_column)),
        )

    def nearest(vector, left_x, left_y, right_x, right_y):
        left_sum = to_row(left_diag, left_x) + to_row(left_turned, left_y)
        left_sum = left_sum + to_row(first_coupling, vector[:, 0:1])
        right_sum = to_row(right_diag, right_x) + to_row(right_turned, vector[:, count - 1 : count])
        right_sum = right_sum + to_row(right_next_coupling, right_y)
        return (
            left_x + to_column(left_inverse, left_rhs - left_sum),
            right_x + to_column(right_inverse, right_rhs - right_sum),
        )

    defect = wrong(rhs, start, diag, coupling, work) - added(left_x, right_x)
    left_once, right_once = nearest(start, left_x, left_y, right_x, right_y)
    left_sum = to_row(left_next_diag, left_y) + to_row(left_next_turned, left_z)
    left_sum = left_sum + to_row(left_coupling, left_x)
    left_y = left_y + to_column(left_next_inverse, left_next_rhs - left_sum)
    right_sum = to_row(right_next_diag, right_y) + to_row(right_next_turned, right_x)
    right_sum = right_sum + to_row(right_third_coupling, right_z)
    right_y = right_y + to_column(right_next_inverse, right_next_rhs - right_sum)
    apply_blocks(inverse, defect, start, once)
    defect = wrong(rhs, once, diag, coupling, work) - added(left_once, right_once)
    left_twice, right_twice = nearest(once, left_once, left_y, right_once, right_y)
    apply_blocks(inverse, defect, once, solution_out)
    defect = wrong(rhs, solution_out, diag, coupling, work)
    residual[...] = defect - added(left_twice, right_twice)


def call(kernel, outs, scratch, *operands, space=pltpu.VMEM):
    inside = pl.BlockSpec(memory_space=pltpu.VMEM)
    if space == pltpu.HBM:
        operands = [pltpu.with_memory_space_constraint(x, space) for x in operands]
    single = not isinstance(outs, tuple)
    return pl.pallas_call(
        kernel,
        out_shape=outs,
        in_specs=[pl.BlockSpec(memory_space=space)] * len(operands),
        out_specs=inside if single else (inside,) * len(outs),
        scratch_shapes=scratch,
        compiler_params=pltpu.CompilerParams(vmem_limit_bytes=24 << 20),
    )(*operands)


def local(rhs, guess, diag_blocks, diag_inverse, coupling, prolong, coarse_inverse, aggregate):
    size, count = rhs.shape
    members = lax.axis_size("row")
    group_count = count * members // AGG
    assert coarse_inverse.shape[2] == 2 * ROWS and 2 * size == count and members % 2 == 0
    aggregate = aggregate.reshape(1, count)
    coarse_inverse = jnp.transpose(coarse_inverse, (0, 2, 1))

    def shape(*sizes, kind=F32):
        return jax.ShapeDtypeStruct(sizes, kind)

    tile = shape(size, count)
    blocks = shape(size, size, count)
    packed = shape(group_count // 2, count)
    edge = shape(6 * size + 3 * EDGES + ROWS, count, kind=BF16)
    line = shape(EDGES, size)
    plain = pltpu.VMEM((size, count), F32)
    half = pltpu.VMEM((size, size, count), BF16)
    loads = 2 + 3 * (size // LOAD) + 3
    (
        rhs, diag, inverse, coupling, prolong, coarse_inverse, aggregate,
        trial, trial_twice, near, far, own, rows,
    ) = call(
        first_kernel,
        (
            tile, blocks, blocks, blocks,
            shape(size, size, count, kind=BF16),
            shape(*coarse_inverse.shape, kind=BF16),
            shape(1, count, kind=jnp.int32),
            tile, tile, edge, edge, shape(10, size, size), line,
        ),
        [
            plain, half, half, half, plain,
            pltpu.SemaphoreType.DMA((loads,)),
        ],
        rhs, guess, diag_blocks, diag_inverse, coupling, prolong, coarse_inverse, aggregate,
        space=pltpu.HBM,
    )
    far = swap(far, 1)
    near = swap(near, 0)
    twice, partial, ghosts = call(
        functools.partial(second_kernel, group_count), (tile, packed, tile), [plain],
        rhs, trial, trial_twice, diag, coupling, own, rows, far, near, prolong, aggregate,
    )
    shares = lax.all_to_all(partial, "row", 0, 0, tiled=True)
    corrected = call(
        coarse_kernel, shape(lax.axis_size(BOTH) * ROWS, count), [], shares, coarse_inverse
    )
    values = lax.all_to_all(corrected, BOTH, 0, 0, tiled=True)
    return call(
        functools.partial(third_kernel, group_count), (tile, tile), [plain, plain, plain],
        rhs, twice, values, diag, inverse, coupling, own, near, far, ghosts, prolong, aggregate,
    )


def solution(mesh):
    vector = P(None, BOTH)
    blocks = P(None, None, BOTH)
    return jax.shard_map(
        local,
        mesh=mesh,
        in_specs=(vector, vector, blocks, blocks, blocks, blocks, blocks, P(BOTH)),
        out_specs=(vector, vector),
        check_vma=False,
    )
```

```python
import functools

import jax
import jax.numpy as jnp
from jax import lax
from jax.experimental import pallas as pl
from jax.experimental.pallas import tpu as pltpu
from jax.sharding import PartitionSpec as P

AGG = 8
BOTH = ("grp", "row")
F32 = jnp.float32
BF16 = jnp.bfloat16
ROWS = 8
LOAD = 16
EDGES = 24
EDGE_ROWS = 10
TILES = 5


def swap(block, first):
    pairs = [(i, i + 1) for i in range(first, lax.axis_size(BOTH) - 1, 2)]
    return lax.ppermute(block, BOTH, pairs + [(j, i) for i, j in pairs])


def even_device():
    return lax.rem(lax.axis_index("row"), 2) == 0


def lanes(like):
    return lax.broadcasted_iota(jnp.int32, like.shape, 1)


def turn(tile, shift):
    return pltpu.roll(tile, shift % tile.shape[1], 1)


def three(tile):
    high = tile.astype(BF16)
    rest = tile - high.astype(F32)
    middle = rest.astype(BF16)
    return high, middle, (rest - middle.astype(F32)).astype(BF16)


def product(left, right, dims):
    left = left.astype(BF16)
    parts = [
        lax.dot_general(left, part, (dims, ((), ())), preferred_element_type=F32)
        for part in three(right)
    ]
    return parts[0] + (parts[1] + parts[2])


def stack(rows):
    return jnp.concatenate([part.astype(F32) for part in three(rows)], axis=0)


def to_column(block, row):
    return jnp.sum(block * row, axis=1, keepdims=True)


def to_row(block, column):
    return jnp.sum(block * column, axis=0, keepdims=True)


def operate(diag, coupling, vector_ref, out_ref, lower):
    vector = vector_ref[...]

    def step(chunk, upward):
        start = pl.multiple_of(chunk * ROWS, ROWS)
        own = vector_ref[pl.ds(start, ROWS), :]
        sums = []
        for s in range(ROWS):
            pair = coupling[start + s]
            terms = diag[start + s] * vector + pair * lower
            sums.append(jnp.sum(terms, axis=0, keepdims=True))
            upward = upward + pair * own[s : s + 1, :]
        out_ref[pl.ds(start, ROWS), :] = jnp.concatenate(sums, axis=0)
        return upward

    return loop(vector.shape[0] // ROWS, step, jnp.zeros_like(vector))


def apply_blocks(blocks, vector, base_ref, out_ref):
    def step(chunk, carry):
        start = pl.multiple_of(chunk * ROWS, ROWS)
        sums = [
            jnp.sum(blocks[start + s].astype(F32) * vector, axis=0, keepdims=True)
            for s in range(ROWS)
        ]
        base = base_ref[pl.ds(start, ROWS), :]
        out_ref[pl.ds(start, ROWS), :] = base + jnp.concatenate(sums, axis=0)
        return carry

    loop(vector.shape[0] // ROWS, step, 0)


def apply_transposed(blocks, vector_ref):
    def step(chunk, total):
        start = pl.multiple_of(chunk * ROWS, ROWS)
        own = vector_ref[pl.ds(start, ROWS), :]
        for s in range(ROWS):
            total = total + blocks[start + s].astype(F32) * own[s : s + 1, :]
        return total

    zero = jnp.zeros(vector_ref.shape, F32)
    return loop(vector_ref.shape[0] // ROWS, step, zero)


def loop(count, step, carry):
    return lax.fori_loop(0, count, step, carry, unroll=True)


def place(tile, block, row):
    shape = (tile.shape[0] // ROWS, ROWS, tile.shape[1])
    lane = lax.broadcasted_iota(jnp.int32, (1,) + shape[1:], 2)
    mine = lax.shift_right_logical(lane, 3) == row
    turned = pltpu.roll(block, 8 * row + 3, 1).reshape(shape)
    return jnp.where(mine, turned, tile.reshape(shape)).reshape(tile.shape)


def picker(size, width, ends):
    shape = (size * len(ends), width)
    row = lax.broadcasted_iota(jnp.int32, shape, 0)
    lane = lax.broadcasted_iota(jnp.int32, shape, 1)
    target = 8 * lax.rem(row, size) + row // size + ends[0]
    return jnp.where(lane == target, 1.0, 0.0).astype(BF16)


def end_blocks(tiles, ends):
    packed = jnp.concatenate(tiles, axis=1).astype(BF16)
    size = packed.shape[0]
    blocks = lax.dot_general(
        picker(size, packed.shape[1], ends), packed, (((1,), (1,)), ((), ())),
        preferred_element_type=F32,
    )
    return [blocks[k * size : (k + 1) * size] for k in range(len(ends))]


def end_blocks_turned(tiles, ends):
    packed = jnp.concatenate(tiles, axis=1).astype(BF16)
    return lax.dot_general(
        packed, picker(packed.shape[0], packed.shape[1], ends), (((1,), (1,)), ((), ())),
        preferred_element_type=F32,
    )


def edge_rows(firsts, lasts, count):
    lane = lanes(firsts[0][0])
    tile = jnp.zeros(lane.shape, F32)
    for k, (column, where) in enumerate(firsts + lasts):
        tile = jnp.where(lane == k, turn(column, k - where), tile)
    return jnp.transpose(tile)[:EDGES]


def wrong(rhs_ref, vector_ref, diag, coupling, work):
    vector = vector_ref[...]
    lane = lanes(vector)
    lower = jnp.where(lane == 0, 0.0, turn(vector, 1))
    upward = operate(diag, coupling, vector_ref, work, lower)
    upper = jnp.where(lane == vector.shape[1] - 1, 0.0, turn(upward, -1))
    return rhs_ref[...] - (work[...] + upper)


def first_kernel(
    rhs_in, guess_in, diag_in, inverse_in, coupling_in, prolong_in, coarse_in, aggregate_in,
    rhs, diag, inverse, coupling, prolong, coarse, aggregate,
    trial, twice, near, far, own, rows_out,
    guess, diag_half, inverse_half, coupling_half, work, sems,
):
    size, count = guess.shape
    parts = diag_half.shape[0] // LOAD
    copies = [
        pltpu.make_async_copy(guess_in, guess, sems.at[0]),
        pltpu.make_async_copy(rhs_in, rhs, sems.at[1]),
    ]
    for p in range(parts):
        rows = pl.ds(p * LOAD, LOAD)
        for source, target in ((coupling_in, coupling_half), (diag_in, diag_half)):
            copies.append(
                pltpu.make_async_copy(source.at[rows], target.at[rows], sems.at[len(copies)])
            )
    for p in range(parts):
        rows = pl.ds(p * LOAD, LOAD)
        copies.append(
            pltpu.make_async_copy(inverse_in.at[rows], inverse_half.at[rows], sems.at[len(copies)])
        )
    for source, target in ((prolong_in, prolong), (coarse_in, coarse), (aggregate_in, aggregate)):
        copies.append(pltpu.make_async_copy(source, target, sems.at[len(copies)]))
    for copy in copies:
        copy.start()
    copies[0].wait()

    start = guess[...]
    lane = lanes(start)
    lower = jnp.where(lane == 0, 0.0, turn(start, 1))
    upward = jnp.zeros_like(start)
    diag_ends = [jnp.zeros_like(start) for _ in range(4)]
    inverse_ends, coupling_ends, prolong_ends = list(diag_ends), list(diag_ends), list(diag_ends)
    for chunk in range(size // ROWS):
        if chunk * ROWS % LOAD == 0:
            at = 2 + 2 * (chunk * ROWS // LOAD)
            copies[at].wait()
            copies[at + 1].wait()
        sums = []
        for i in range(chunk * ROWS, chunk * ROWS + ROWS):
            pair = coupling_half[i].astype(F32)
            block = diag_half[i].astype(F32)
            coupling[i] = pair
            diag[i] = block
            t, row = divmod(i, size // 4)
            diag_ends[t] = place(diag_ends[t], block, row)
            sums.append(jnp.sum(block * start + pair * lower, axis=0, keepdims=True))
            upward = upward + pair * guess[i : i + 1, :]
        work[pl.ds(chunk * ROWS, ROWS), :] = jnp.concatenate(sums, axis=0)
    upper = jnp.where(lane == count - 1, 0.0, turn(upward, -1))
    copies[1].wait()
    defect = rhs[...] - (work[...] + upper)

    for chunk in range(size // ROWS):
        if chunk * ROWS % LOAD == 0:
            copies[2 + 2 * parts + chunk * ROWS // LOAD].wait()
        rows = pl.ds(chunk * ROWS, ROWS)
        sums = []
        for i in range(chunk * ROWS, chunk * ROWS + ROWS):
            block = inverse_half[i].astype(F32)
            inverse[i] = block
            t, row = divmod(i, size // 4)
            inverse_ends[t] = place(inverse_ends[t], block, row)
            sums.append(jnp.sum(block * defect, axis=0, keepdims=True))
        trial[rows, :] = guess[rows, :] + jnp.concatenate(sums, axis=0)

    second = trial[...]
    lower = jnp.where(lane == 0, 0.0, turn(second, 1))
    upward = jnp.zeros_like(start)
    for chunk in range(size // ROWS):
        sums = []
        for i in range(chunk * ROWS, chunk * ROWS + ROWS):
            pair = coupling[i]
            t, row = divmod(i, size // 4)
            coupling_ends[t] = place(coupling_ends[t], pair, row)
            sums.append(jnp.sum(diag[i] * second + pair * lower, axis=0, keepdims=True))
            upward = upward + pair * trial[i : i + 1, :]
        work[pl.ds(chunk * ROWS, ROWS), :] = jnp.concatenate(sums, axis=0)
    upper = jnp.where(lane == count - 1, 0.0, turn(upward, -1))
    defect = rhs[...] - (work[...] + upper)

    for copy in copies[-3:]:
        copy.wait()
    for chunk in range(size // ROWS):
        rows = pl.ds(chunk * ROWS, ROWS)
        sums = []
        for i in range(chunk * ROWS, chunk * ROWS + ROWS):
            t, row = divmod(i, size // 4)
            prolong_ends[t] = place(prolong_ends[t], prolong[i].astype(F32), row)
            sums.append(jnp.sum(inverse[i] * defect, axis=0, keepdims=True))
        twice[rows, :] = trial[rows, :] + jnp.concatenate(sums, axis=0)

    last = count - 1
    named = jnp.broadcast_to(aggregate[...].astype(F32), (size, count))
    after = twice[...]
    both = [(start, 0), (second, 0), (defect, 0), (after, 1), (after, 2), (rhs[...], 0), (rhs[...], 1)]
    both = both + [(named, 0), (named, 1), (named, 2)]
    rows = edge_rows(both, [(column, last - k) for column, k in both], count)
    rows_out[...] = rows
    diag_turned = end_blocks_turned(diag_ends, (1, 2, 3, 4))
    coupling_turned = end_blocks_turned(coupling_ends, (3, 4))
    inverses = end_blocks(inverse_ends, (1, 2, 3, 4))
    couplings = end_blocks(coupling_ends, (1, 2, 3, 4, 5))
    prolongs = end_blocks(prolong_ends, (0, 1, 2, 3, 4, 5))
    turned_diag = [diag_turned[:, k * size : (k + 1) * size] for k in range(4)]
    turned = [coupling_turned[:, k * size : (k + 1) * size] for k in range(2)]
    lasts = (
        (turned_diag[1], inverses[1]), (couplings[1], couplings[0]), (prolongs[2], prolongs[1]),
        (prolongs[0], couplings[4]), (turned_diag[0], inverses[0]),
    )
    firsts = (
        (turned_diag[2], inverses[2]), (couplings[2], couplings[3]), (prolongs[3], prolongs[4]),
        (prolongs[5], couplings[4]), (turned_diag[3], inverses[3]),
    )
    even = even_device()
    for k, (one, other) in enumerate(zip(lasts, firsts)):
        one, other = jnp.concatenate(one, axis=1), jnp.concatenate(other, axis=1)
        at = slice(k * size, (k + 1) * size)
        near[at] = jnp.where(even, one, other).astype(BF16)
        far[at] = jnp.where(even, other, one).astype(BF16)
    high, middle, low = (part.astype(F32) for part in three(rows))
    shares = jnp.concatenate(
        [jnp.concatenate([high, low], axis=1), jnp.concatenate([middle, low], axis=1)], axis=0
    ).astype(BF16)
    near[TILES * size :] = shares
    far[TILES * size :] = shares
    blocks = [turned_diag[1], turned_diag[2]] + inverses
    for k, block in enumerate(blocks + [couplings[1], couplings[2], turned[0], turned[1]]):
        own[k] = block


def beyond_ends(even, near, far, size):
    near, far = near[...].astype(F32), far[...].astype(F32)
    sides, rows = [], []
    for side in (jnp.where(even, far, near), jnp.where(even, near, far)):
        pairs = [side[k * size : (k + 1) * size] for k in range(TILES)]
        sides.append(([(pair[:, :size], pair[:, size:]) for pair in pairs], pairs[1]))
        tail = side[TILES * size :]
        rows.append(tail[:EDGES, :size] + tail[EDGES:, :size] + tail[:EDGES, size:])
    return sides, rows


def columns_from(size):
    shape = (size, size)
    unit = lax.broadcasted_iota(jnp.int32, shape, 0) == lax.broadcasted_iota(jnp.int32, shape, 1)
    return lambda row: jnp.sum(jnp.where(unit, row, 0.0), axis=1, keepdims=True)


def ends(lane, first, last):
    return jnp.where(lane == 0, first, jnp.where(lane == lane.shape[1] - 1, last, 0.0))


def second_kernel(
    group_count, rhs, trial, trial_twice, diag, coupling, own, rows, far, near,
    prolong, aggregate, twice, partial, ghosts, work,
):
    size, count = rhs.shape
    sides, (left, right) = beyond_ends(even_device(), near, far, size)
    (left_blocks, _), (right_blocks, right_pair) = sides
    column = columns_from(size)
    half = EDGE_ROWS
    left_diag, left_inverse = left_blocks[0]
    (right_diag, right_inverse), (right_coupling, _) = right_blocks[:2]
    right_turned = jnp.transpose(right_pair)[:size]
    last_diag, first_diag = own[0], own[1]
    before_inverse, last_inverse, first_inverse, second_inverse = (own[2 + k] for k in range(4))
    last_coupling, first_coupling, first_turned, second_turned = (own[6 + k] for k in range(4))
    first_start, first_trial, last_start, last_trial = (
        column(rows[k : k + 1]) for k in (0, 1, half, half + 1)
    )
    left_start, left_trial = (column(left[half + k : half + k + 1]) for k in (0, 1))
    right_start, right_trial = (column(right[k : k + 1]) for k in (0, 1))
    left_wrong, right_wrong = left[half + 2 : half + 3], right[2:3]

    first_change = -to_column(first_inverse, to_row(first_turned, left_start))
    last_change = -to_column(last_inverse, to_row(right_coupling, right_start))
    left_change = -to_column(left_inverse, to_row(first_coupling, first_start))
    right_change = -to_column(right_inverse, to_row(right_turned, last_start))
    left_once, right_once = left_trial + left_change, right_trial + right_change
    first_added = to_row(first_diag, first_change) + to_row(first_turned, left_once)
    last_added = to_row(last_diag, last_change) + to_row(right_coupling, right_once)
    left_added = to_row(left_diag, left_change)
    left_added = left_added + to_row(first_coupling, first_trial + first_change)
    right_added = to_row(right_diag, right_change)
    right_added = right_added + to_row(right_turned, last_trial + last_change)
    left_twice = left_once + to_column(left_inverse, left_wrong - left_added)
    right_twice = right_once + to_column(right_inverse, right_wrong - right_added)
    second_added = to_row(second_turned, first_change)
    before_added = to_row(last_coupling, last_change)
    lane = lax.broadcasted_iota(jnp.int32, (size, count), 1)
    change = ends(
        lane,
        first_change - to_column(first_inverse, first_added),
        last_change - to_column(last_inverse, last_added),
    )
    change = jnp.where(lane == 1, -to_column(second_inverse, second_added), change)
    change = jnp.where(lane == count - 2, -to_column(before_inverse, before_added), change)
    twice[...] = trial_twice[...] + change
    tile = jnp.zeros((size, count), F32)
    for k, ghost in enumerate((left_twice, left_change, right_twice, right_change)):
        tile = jnp.where(lane == k, ghost, tile)
    ghosts[...] = tile
    added = ends(
        lane,
        column(to_row(first_turned, left_twice)),
        column(to_row(right_coupling, right_twice)),
    )
    work[...] = wrong(rhs, twice, diag, coupling, work) - added
    pieces = apply_transposed(prolong, work)
    picked = [chosen(aggregate, group_count, half) for half in (0, 1)]
    both = product(jnp.concatenate(picked, axis=0), pieces, ((1,), (1,)))
    rows_out = group_count // 2
    partial[...] = jnp.concatenate([both[:rows_out], both[rows_out:]], axis=1)


def chosen(aggregate, group_count, half):
    rows = group_count // 2
    local_index = jnp.broadcast_to(lax.rem(aggregate[...], group_count), (rows, aggregate.shape[1]))
    row = lax.broadcasted_iota(jnp.int32, local_index.shape, 0)
    named = (row // ROWS) * (2 * ROWS) + lax.rem(row, ROWS) + half * ROWS
    return jnp.where(local_index == named, 1.0, 0.0).astype(F32)


def coarse_kernel(shares, coarse_inverse, out):
    size = coarse_inverse.shape[0]
    rows = shares.shape[0] // ROWS
    share = shares[0:ROWS]
    for row in range(1, rows):
        share = share + shares[row * ROWS : (row + 1) * ROWS]
    share = jnp.concatenate([share[:, :size], share[:, size:]], axis=0)
    lane = lanes(share)
    value = jnp.zeros_like(share)
    for i in range(size):
        total = jnp.sum(coarse_inverse[i].astype(F32) * share, axis=1, keepdims=True)
        value = jnp.where(lane == i, total, value)
    value = jnp.concatenate([value[:ROWS], value[ROWS:]], axis=1)
    for row in range(out.shape[0] // ROWS):
        out[row * ROWS : (row + 1) * ROWS] = value


def third_kernel(
    group_count, rhs, twice, values, diag, inverse, coupling, own, near, far, ghosts,
    prolong, aggregate, solution_out, residual, start, once, work,
):
    size, count = rhs.shape
    every = values.shape[0]
    in_group = group_count // 2
    group = pl.ds(pl.multiple_of(lax.axis_index("grp") * in_group, ROWS), in_group)
    mine = three(values[group, :])
    picked = [chosen(aggregate, group_count, half) for half in (0, 1)]
    picked = jnp.concatenate(picked, axis=1).astype(BF16)
    spread = jnp.zeros((size, count), F32)
    for part in mine:
        both = lax.dot_general(part, picked, (((0,), (0,)), ((), ())), preferred_element_type=F32)
        spread = spread + (both[:size, :count] + both[size:, count:])
    apply_blocks(prolong, spread, twice, start)

    sides, (left, right) = beyond_ends(even_device(), near, far, size)
    (left_blocks, left_pair), (right_blocks, right_pair) = sides
    column = columns_from(size)
    lane = lax.broadcasted_iota(jnp.int32, (size, count), 1)
    half = EDGE_ROWS
    blank = jnp.zeros((2, size), F32)
    names = jnp.concatenate([left[half + 7 : half + 10], right[7:10], blank], axis=0)[:, 0:1]
    source = lax.broadcasted_iota(jnp.int32, (ROWS, every), 1)
    first_name = (source // ROWS) * (2 * ROWS) + lax.rem(source, ROWS)
    everything = three(values[...])
    named = [
        jnp.where(names == (first_name + k * ROWS).astype(F32), 1.0, 0.0) for k in (0, 1)
    ]
    named = jnp.concatenate(named, axis=0).astype(BF16)
    coarse = jnp.zeros((ROWS, size), F32)
    for part in everything:
        both = jnp.dot(named, part, preferred_element_type=F32)
        coarse = coarse + (both[:ROWS, :size] + both[ROWS:, size:])

    (left_diag, left_inverse), (left_coupling, _) = left_blocks[:2]
    left_next_diag, left_next_inverse = left_blocks[4]
    left_pair, right_pair = jnp.transpose(left_pair), jnp.transpose(right_pair)
    left_turned, left_next_turned = left_pair[:size], left_pair[size:]
    (right_diag, right_inverse), (right_coupling, right_next_coupling) = right_blocks[:2]
    right_next_diag, right_next_inverse = right_blocks[4]
    right_turned, right_next_turned = right_pair[:size], right_pair[size:]
    right_third_coupling = right_blocks[3][1]
    first_coupling, first_turned = own[7], own[8]
    left_x, left_change, right_x, right_change = (ghosts[:, k : k + 1] for k in range(4))
    left_y, left_z = (column(left[half + k : half + k + 1]) for k in (3, 4))
    right_y, right_z = (column(right[k : k + 1]) for k in (3, 4))
    left_y = left_y - to_column(left_next_inverse, to_row(left_coupling, left_change))
    right_y = right_y - to_column(right_next_inverse, to_row(right_next_turned, right_change))
    prolongs = (left_blocks[2][0], left_blocks[2][1], left_blocks[3][0])
    prolongs = prolongs + (right_blocks[2][0], right_blocks[2][1], right_blocks[3][0])
    known = (left_x, left_y, left_z, right_x, right_y, right_z)
    left_x, left_y, left_z, right_x, right_y, right_z = (
        value + to_column(block, coarse[k : k + 1])
        for k, (value, block) in enumerate(zip(known, prolongs))
    )
    left_rhs, left_next_rhs = left[half + 5 : half + 6], left[half + 6 : half + 7]
    right_rhs, right_next_rhs = right[5:6], right[6:7]

    def added(left_column, right_column):
        return ends(
            lane,
            column(to_row(first_turned, left_column)),
            column(to_row(right_coupling, right_column)),
        )

    def nearest(vector, left_x, left_y, right_x, right_y):
        left_sum = to_row(left_diag, left_x) + to_row(left_turned, left_y)
        left_sum = left_sum + to_row(first_coupling, vector[:, 0:1])
        right_sum = to_row(right_diag, right_x) + to_row(right_turned, vector[:, count - 1 : count])
        right_sum = right_sum + to_row(right_next_coupling, right_y)
        return (
            left_x + to_column(left_inverse, left_rhs - left_sum),
            right_x + to_column(right_inverse, right_rhs - right_sum),
        )

    defect = wrong(rhs, start, diag, coupling, work) - added(left_x, right_x)
    left_once, right_once = nearest(start, left_x, left_y, right_x, right_y)
    left_sum = to_row(left_next_diag, left_y) + to_row(left_next_turned, left_z)
    left_sum = left_sum + to_row(left_coupling, left_x)
    left_y = left_y + to_column(left_next_inverse, left_next_rhs - left_sum)
    right_sum = to_row(right_next_diag, right_y) + to_row(right_next_turned, right_x)
    right_sum = right_sum + to_row(right_third_coupling, right_z)
    right_y = right_y + to_column(right_next_inverse, right_next_rhs - right_sum)
    apply_blocks(inverse, defect, start, once)
    defect = wrong(rhs, once, diag, coupling, work) - added(left_once, right_once)
    left_twice, right_twice = nearest(once, left_once, left_y, right_once, right_y)
    apply_blocks(inverse, defect, once, solution_out)
    defect = wrong(rhs, solution_out, diag, coupling, work)
    residual[...] = defect - added(left_twice, right_twice)


def call(kernel, outs, scratch, *operands, space=pltpu.VMEM):
    inside = pl.BlockSpec(memory_space=pltpu.VMEM)
    if space == pltpu.HBM:
        operands = [pltpu.with_memory_space_constraint(x, space) for x in operands]
    single = not isinstance(outs, tuple)
    return pl.pallas_call(
        kernel,
        out_shape=outs,
        in_specs=[pl.BlockSpec(memory_space=space)] * len(operands),
        out_specs=inside if single else (inside,) * len(outs),
        scratch_shapes=scratch,
        compiler_params=pltpu.CompilerParams(vmem_limit_bytes=24 << 20),
    )(*operands)


def local(rhs, guess, diag_blocks, diag_inverse, coupling, prolong, coarse_inverse, aggregate):
    size, count = rhs.shape
    members = lax.axis_size("row")
    group_count = count * members // AGG
    assert coarse_inverse.shape[2] == 2 * ROWS and 2 * size == count and members % 2 == 0
    aggregate = aggregate.reshape(1, count)
    coarse_inverse = jnp.transpose(coarse_inverse, (0, 2, 1))

    def shape(*sizes, kind=F32):
        return jax.ShapeDtypeStruct(sizes, kind)

    tile = shape(size, count)
    blocks = shape(size, size, count)
    packed = shape(group_count // 2, count)
    edge = shape(TILES * size + 2 * EDGES, count, kind=BF16)
    line = shape(EDGES, size)
    plain = pltpu.VMEM((size, count), F32)
    half = pltpu.VMEM((size, size, count), BF16)
    loads = 2 + 3 * (size // LOAD) + 3
    (
        rhs, diag, inverse, coupling, prolong, coarse_inverse, aggregate,
        trial, trial_twice, near, far, own, rows,
    ) = call(
        first_kernel,
        (
            tile, blocks, blocks, blocks,
            shape(size, size, count, kind=BF16),
            shape(*coarse_inverse.shape, kind=BF16),
            shape(1, count, kind=jnp.int32),
            tile, tile, edge, edge, shape(10, size, size), line,
        ),
        [
            plain, half, half, half, plain,
            pltpu.SemaphoreType.DMA((loads,)),
        ],
        rhs, guess, diag_blocks, diag_inverse, coupling, prolong, coarse_inverse, aggregate,
        space=pltpu.HBM,
    )
    far = swap(far, 1)
    near = swap(near, 0)
    twice, partial, ghosts = call(
        functools.partial(second_kernel, group_count), (tile, packed, tile), [plain],
        rhs, trial, trial_twice, diag, coupling, own, rows, far, near, prolong, aggregate,
    )
    shares = lax.all_to_all(partial, "row", 0, 0, tiled=True)
    corrected = call(
        coarse_kernel, shape(lax.axis_size(BOTH) * ROWS, count), [], shares, coarse_inverse
    )
    values = lax.all_to_all(corrected, BOTH, 0, 0, tiled=True)
    return call(
        functools.partial(third_kernel, group_count), (tile, tile), [plain, plain, plain],
        rhs, twice, values, diag, inverse, coupling, own, near, far, ghosts, prolong, aggregate,
    )


def solution(mesh):
    vector = P(None, BOTH)
    blocks = P(None, None, BOTH)
    return jax.shard_map(
        local,
        mesh=mesh,
        in_specs=(vector, vector, blocks, blocks, blocks, blocks, blocks, P(BOTH)),
        out_specs=(vector, vector),
        check_vma=False,
    )
```

```python
import functools

import jax
import jax.numpy as jnp
from jax import lax
from jax.experimental import pallas as pl
from jax.experimental.pallas import tpu as pltpu
from jax.sharding import PartitionSpec as P

AGG = 8
BOTH = ("grp", "row")
F32 = jnp.float32
BF16 = jnp.bfloat16
ROWS = 8
LOAD = 16
EDGES = 24
EDGE_ROWS = 10
TILES = 5


def swap(block, first):
    pairs = [(i, i + 1) for i in range(first, lax.axis_size(BOTH) - 1, 2)]
    return lax.ppermute(block, BOTH, pairs + [(j, i) for i, j in pairs])


def even_device():
    return lax.rem(lax.axis_index("row"), 2) == 0


def lanes(like):
    return lax.broadcasted_iota(jnp.int32, like.shape, 1)


def turn(tile, shift):
    return pltpu.roll(tile, shift % tile.shape[1], 1)


def three(tile):
    high = tile.astype(BF16)
    rest = tile - high.astype(F32)
    middle = rest.astype(BF16)
    return high, middle, (rest - middle.astype(F32)).astype(BF16)


def product(left, right, dims):
    left = left.astype(BF16)
    parts = [
        lax.dot_general(left, part, (dims, ((), ())), preferred_element_type=F32)
        for part in three(right)
    ]
    return parts[0] + (parts[1] + parts[2])


def stack(rows):
    return jnp.concatenate([part.astype(F32) for part in three(rows)], axis=0)


def to_column(block, row):
    return jnp.sum(block * row, axis=1, keepdims=True)


def to_row(block, column):
    return jnp.sum(block * column, axis=0, keepdims=True)


def operate(diag, coupling, vector_ref, out_ref, lower):
    vector = vector_ref[...]

    def step(chunk, upward):
        start = pl.multiple_of(chunk * ROWS, ROWS)
        own = vector_ref[pl.ds(start, ROWS), :]
        sums = []
        for s in range(ROWS):
            pair = coupling[start + s]
            terms = diag[start + s] * vector + pair * lower
            sums.append(jnp.sum(terms, axis=0, keepdims=True))
            upward = upward + pair * own[s : s + 1, :]
        out_ref[pl.ds(start, ROWS), :] = jnp.concatenate(sums, axis=0)
        return upward

    return loop(vector.shape[0] // ROWS, step, jnp.zeros_like(vector))


def apply_blocks(blocks, vector, base_ref, out_ref):
    def step(chunk, carry):
        start = pl.multiple_of(chunk * ROWS, ROWS)
        sums = [
            jnp.sum(blocks[start + s].astype(F32) * vector, axis=0, keepdims=True)
            for s in range(ROWS)
        ]
        base = base_ref[pl.ds(start, ROWS), :]
        out_ref[pl.ds(start, ROWS), :] = base + jnp.concatenate(sums, axis=0)
        return carry

    loop(vector.shape[0] // ROWS, step, 0)


def apply_transposed(blocks, vector_ref):
    def step(chunk, total):
        start = pl.multiple_of(chunk * ROWS, ROWS)
        own = vector_ref[pl.ds(start, ROWS), :]
        for s in range(ROWS):
            total = total + blocks[start + s].astype(F32) * own[s : s + 1, :]
        return total

    zero = jnp.zeros(vector_ref.shape, F32)
    return loop(vector_ref.shape[0] // ROWS, step, zero)


def loop(count, step, carry):
    return lax.fori_loop(0, count, step, carry, unroll=True)


def place(tile, block, row):
    shape = (tile.shape[0] // ROWS, ROWS, tile.shape[1])
    lane = lax.broadcasted_iota(jnp.int32, (1,) + shape[1:], 2)
    mine = lax.shift_right_logical(lane, 3) == row
    turned = pltpu.roll(block, 8 * row + 3, 1).reshape(shape)
    return jnp.where(mine, turned, tile.reshape(shape)).reshape(tile.shape)


def picker(size, width, ends):
    shape = (size * len(ends), width)
    row = lax.broadcasted_iota(jnp.int32, shape, 0)
    lane = lax.broadcasted_iota(jnp.int32, shape, 1)
    target = 8 * lax.rem(row, size) + row // size + ends[0]
    return jnp.where(lane == target, 1.0, 0.0).astype(BF16)


def end_blocks(tiles, ends):
    packed = jnp.concatenate(tiles, axis=1).astype(BF16)
    size = packed.shape[0]
    blocks = lax.dot_general(
        picker(size, packed.shape[1], ends), packed, (((1,), (1,)), ((), ())),
        preferred_element_type=F32,
    )
    return [blocks[k * size : (k + 1) * size] for k in range(len(ends))]


def end_blocks_turned(tiles, ends):
    packed = jnp.concatenate(tiles, axis=1).astype(BF16)
    return lax.dot_general(
        packed, picker(packed.shape[0], packed.shape[1], ends), (((1,), (1,)), ((), ())),
        preferred_element_type=F32,
    )


def edge_rows(firsts, lasts, count):
    lane = lanes(firsts[0][0])
    tile = jnp.zeros(lane.shape, F32)
    for k, (column, where) in enumerate(firsts + lasts):
        tile = jnp.where(lane == k, turn(column, k - where), tile)
    return jnp.transpose(tile)[:EDGES]


def wrong(rhs_ref, vector_ref, diag, coupling, work):
    vector = vector_ref[...]
    lane = lanes(vector)
    lower = jnp.where(lane == 0, 0.0, turn(vector, 1))
    upward = operate(diag, coupling, vector_ref, work, lower)
    upper = jnp.where(lane == vector.shape[1] - 1, 0.0, turn(upward, -1))
    return rhs_ref[...] - (work[...] + upper)


def first_kernel(
    rhs_in, guess_in, diag_in, inverse_in, coupling_in, prolong_in, coarse_in, aggregate_in,
    rhs, diag, inverse, coupling, prolong, coarse, aggregate,
    trial, twice, near, far, own, rows_out,
    guess, diag_half, inverse_half, coupling_half, work, sems,
):
    size, count = guess.shape
    parts = diag_half.shape[0] // LOAD
    copies = [
        pltpu.make_async_copy(guess_in, guess, sems.at[0]),
        pltpu.make_async_copy(rhs_in, rhs, sems.at[1]),
    ]
    for p in range(parts):
        rows = pl.ds(p * LOAD, LOAD)
        for source, target in ((coupling_in, coupling_half), (diag_in, diag_half)):
            copies.append(
                pltpu.make_async_copy(source.at[rows], target.at[rows], sems.at[len(copies)])
            )
    for p in range(parts):
        rows = pl.ds(p * LOAD, LOAD)
        copies.append(
            pltpu.make_async_copy(inverse_in.at[rows], inverse_half.at[rows], sems.at[len(copies)])
        )
    for source, target in ((prolong_in, prolong), (coarse_in, coarse), (aggregate_in, aggregate)):
        copies.append(pltpu.make_async_copy(source, target, sems.at[len(copies)]))
    for copy in copies:
        copy.start()
    copies[0].wait()

    start = guess[...]
    lane = lanes(start)
    lower = jnp.where(lane == 0, 0.0, turn(start, 1))
    upward = jnp.zeros_like(start)
    diag_ends = [jnp.zeros_like(start) for _ in range(4)]
    inverse_ends, coupling_ends, prolong_ends = list(diag_ends), list(diag_ends), list(diag_ends)
    for chunk in range(size // ROWS):
        if chunk * ROWS % LOAD == 0:
            at = 2 + 2 * (chunk * ROWS // LOAD)
            copies[at].wait()
            copies[at + 1].wait()
        sums = []
        for i in range(chunk * ROWS, chunk * ROWS + ROWS):
            pair = coupling_half[i].astype(F32)
            block = diag_half[i].astype(F32)
            coupling[i] = pair
            diag[i] = block
            t, row = divmod(i, size // 4)
            diag_ends[t] = place(diag_ends[t], block, row)
            sums.append(jnp.sum(block * start + pair * lower, axis=0, keepdims=True))
            upward = upward + pair * guess[i : i + 1, :]
        work[pl.ds(chunk * ROWS, ROWS), :] = jnp.concatenate(sums, axis=0)
    upper = jnp.where(lane == count - 1, 0.0, turn(upward, -1))
    copies[1].wait()
    defect = rhs[...] - (work[...] + upper)

    for chunk in range(size // ROWS):
        if chunk * ROWS % LOAD == 0:
            copies[2 + 2 * parts + chunk * ROWS // LOAD].wait()
        rows = pl.ds(chunk * ROWS, ROWS)
        sums = []
        for i in range(chunk * ROWS, chunk * ROWS + ROWS):
            block = inverse_half[i].astype(F32)
            inverse[i] = block
            t, row = divmod(i, size // 4)
            inverse_ends[t] = place(inverse_ends[t], block, row)
            sums.append(jnp.sum(block * defect, axis=0, keepdims=True))
        trial[rows, :] = guess[rows, :] + jnp.concatenate(sums, axis=0)

    second = trial[...]
    lower = jnp.where(lane == 0, 0.0, turn(second, 1))
    upward = jnp.zeros_like(start)
    for chunk in range(size // ROWS):
        sums = []
        for i in range(chunk * ROWS, chunk * ROWS + ROWS):
            pair = coupling[i]
            t, row = divmod(i, size // 4)
            coupling_ends[t] = place(coupling_ends[t], pair, row)
            sums.append(jnp.sum(diag[i] * second + pair * lower, axis=0, keepdims=True))
            upward = upward + pair * trial[i : i + 1, :]
        work[pl.ds(chunk * ROWS, ROWS), :] = jnp.concatenate(sums, axis=0)
    upper = jnp.where(lane == count - 1, 0.0, turn(upward, -1))
    defect = rhs[...] - (work[...] + upper)

    for copy in copies[-3:]:
        copy.wait()
    for chunk in range(size // ROWS):
        rows = pl.ds(chunk * ROWS, ROWS)
        sums = []
        for i in range(chunk * ROWS, chunk * ROWS + ROWS):
            t, row = divmod(i, size // 4)
            prolong_ends[t] = place(prolong_ends[t], prolong[i].astype(F32), row)
            sums.append(jnp.sum(inverse[i] * defect, axis=0, keepdims=True))
        twice[rows, :] = trial[rows, :] + jnp.concatenate(sums, axis=0)

    last = count - 1
    named = jnp.broadcast_to(aggregate[...].astype(F32), (size, count))
    after = twice[...]
    both = [(start, 0), (second, 0), (defect, 0), (after, 1), (after, 2), (rhs[...], 0), (rhs[...], 1)]
    both = both + [(named, 0), (named, 1), (named, 2)]
    rows = edge_rows(both, [(column, last - k) for column, k in both], count)
    rows_out[...] = rows
    diag_turned = end_blocks_turned(diag_ends, (1, 2, 3, 4))
    coupling_turned = end_blocks_turned(coupling_ends, (2, 3, 4, 5))
    inverses = end_blocks(inverse_ends, (1, 2, 3, 4))
    couplings = end_blocks(coupling_ends, (1, 2, 3, 4, 5))
    prolongs = end_blocks(prolong_ends, (0, 1, 2, 3, 4, 5))
    turned_diag = [diag_turned[:, k * size : (k + 1) * size] for k in range(4)]
    turned = [coupling_turned[:, k * size : (k + 1) * size] for k in range(4)]
    lasts = (
        (turned_diag[1], inverses[1]), (couplings[1], couplings[0]), (prolongs[2], prolongs[1]),
        (prolongs[0], couplings[4]), (turned_diag[0], inverses[0]),
    )
    firsts = (
        (turned_diag[2], inverses[2]), (couplings[2], couplings[3]), (prolongs[3], prolongs[4]),
        (prolongs[5], couplings[4]), (turned_diag[3], inverses[3]),
    )
    even = even_device()
    for k, (one, other) in enumerate(zip(lasts, firsts)):
        one, other = jnp.concatenate(one, axis=1), jnp.concatenate(other, axis=1)
        at = slice(k * size, (k + 1) * size)
        near[at] = jnp.where(even, one, other).astype(BF16)
        far[at] = jnp.where(even, other, one).astype(BF16)
    high, middle, low = (part.astype(F32) for part in three(rows))
    shares = jnp.concatenate(
        [jnp.concatenate([high, low], axis=1), jnp.concatenate([middle, low], axis=1)], axis=0
    ).astype(BF16)
    near[TILES * size :] = shares
    far[TILES * size :] = shares
    blocks = [turned_diag[1], turned_diag[2]] + inverses
    blocks = blocks + [couplings[1], couplings[2], turned[1], turned[2]]
    blocks = blocks + [turned_diag[0], turned_diag[3], couplings[0], couplings[3]]
    for k, block in enumerate(blocks + [turned[0], turned[3]] + prolongs):
        own[k] = block


def beyond_ends(even, near, far, size):
    near, far = near[...].astype(F32), far[...].astype(F32)
    sides, rows = [], []
    for side in (jnp.where(even, far, near), jnp.where(even, near, far)):
        pairs = [side[k * size : (k + 1) * size] for k in range(TILES)]
        sides.append(([(pair[:, :size], pair[:, size:]) for pair in pairs], pairs[1]))
        tail = side[TILES * size :]
        rows.append(tail[:EDGES, :size] + tail[EDGES:, :size] + tail[:EDGES, size:])
    return sides, rows


def columns_from(size):
    shape = (size, size)
    unit = lax.broadcasted_iota(jnp.int32, shape, 0) == lax.broadcasted_iota(jnp.int32, shape, 1)
    return lambda row: jnp.sum(jnp.where(unit, row, 0.0), axis=1, keepdims=True)


def ends(lane, first, last):
    return jnp.where(lane == 0, first, jnp.where(lane == lane.shape[1] - 1, last, 0.0))


def trial_kernel(
    group_count, rhs, trial_twice, diag, coupling, prolong, aggregate, partial, work,
):
    work[...] = wrong(rhs, trial_twice, diag, coupling, work)
    pieces = apply_transposed(prolong, work)
    picked = [chosen(aggregate, group_count, half) for half in (0, 1)]
    both = product(jnp.concatenate(picked, axis=0), pieces, ((1,), (1,)))
    rows_out = group_count // 2
    partial[...] = jnp.concatenate([both[:rows_out], both[rows_out:]], axis=1)


def second_kernel(
    group_count, trial_partial, trial_twice, own, rows, near, far, twice, partial, ghosts,
):
    size, count = trial_twice.shape
    sides, (left, right) = beyond_ends(even_device(), near, far, size)
    (left_blocks, _), (right_blocks, right_pair) = sides
    column = columns_from(size)
    half = EDGE_ROWS
    left_diag, left_inverse = left_blocks[0]
    (right_diag, right_inverse), (right_coupling, _) = right_blocks[:2]
    right_turned = jnp.transpose(right_pair)[:size]
    last_diag, first_diag = own[0], own[1]
    before_inverse, last_inverse, first_inverse, second_inverse = (own[2 + k] for k in range(4))
    last_coupling, first_coupling, first_turned, second_turned = (own[6 + k] for k in range(4))
    first_start, first_trial, last_start, last_trial = (
        column(rows[k : k + 1]) for k in (0, 1, half, half + 1)
    )
    left_start, left_trial = (column(left[half + k : half + k + 1]) for k in (0, 1))
    right_start, right_trial = (column(right[k : k + 1]) for k in (0, 1))
    left_wrong, right_wrong = left[half + 2 : half + 3], right[2:3]

    first_change = -to_column(first_inverse, to_row(first_turned, left_start))
    last_change = -to_column(last_inverse, to_row(right_coupling, right_start))
    left_change = -to_column(left_inverse, to_row(first_coupling, first_start))
    right_change = -to_column(right_inverse, to_row(right_turned, last_start))
    left_once, right_once = left_trial + left_change, right_trial + right_change
    first_added = to_row(first_diag, first_change) + to_row(first_turned, left_once)
    last_added = to_row(last_diag, last_change) + to_row(right_coupling, right_once)
    left_added = to_row(left_diag, left_change)
    left_added = left_added + to_row(first_coupling, first_trial + first_change)
    right_added = to_row(right_diag, right_change)
    right_added = right_added + to_row(right_turned, last_trial + last_change)
    left_twice = left_once + to_column(left_inverse, left_wrong - left_added)
    right_twice = right_once + to_column(right_inverse, right_wrong - right_added)
    second_added = to_row(second_turned, first_change)
    before_added = to_row(last_coupling, last_change)
    lane = lax.broadcasted_iota(jnp.int32, (size, count), 1)
    first_new = first_change - to_column(first_inverse, first_added)
    second_new = -to_column(second_inverse, second_added)
    before_new = -to_column(before_inverse, before_added)
    last_new = last_change - to_column(last_inverse, last_added)
    change = ends(lane, first_new, last_new)
    change = jnp.where(lane == 1, second_new, change)
    change = jnp.where(lane == count - 2, before_new, change)
    twice[...] = trial_twice[...] + change
    tile = jnp.zeros((size, count), F32)
    for k, ghost in enumerate((left_twice, left_change, right_twice, right_change)):
        tile = jnp.where(lane == k, ghost, tile)
    ghosts[...] = tile
    before_diag, second_diag, before_coupling, second_coupling = (own[10 + k] for k in range(4))
    last_turned, third_turned = own[14], own[15]
    prolongs = [own[16 + k] for k in range(6)]
    added = (
        to_row(before_coupling, before_new),
        to_row(before_diag, before_new) + to_row(last_coupling, last_new),
        to_row(last_diag, last_new) + to_row(last_turned, before_new)
        + to_row(right_coupling, right_twice),
        to_row(first_diag, first_new) + to_row(second_coupling, second_new)
        + to_row(first_turned, left_twice),
        to_row(second_diag, second_new) + to_row(second_turned, first_new),
        to_row(third_turned, second_new),
    )
    pieces = [to_row(block, column(row)) for block, row in zip(prolongs, added)]
    order = (half + 9, half + 8, half + 7, 7, 8, 9)
    names = [rows[k : k + 1] for k in order]
    blank = jnp.zeros((ROWS - 6, size), F32)
    pieces = jnp.concatenate(pieces + [blank], axis=0)
    names = jnp.concatenate(names + [blank], axis=0)[:, 0:1]
    rows_out = group_count // 2
    start = (lax.axis_index("grp") * group_count).astype(F32)
    row = lax.broadcasted_iota(jnp.int32, (ROWS, 2 * rows_out), 1)
    half_row = lax.rem(row, rows_out)
    named = (half_row // ROWS) * (2 * ROWS) + lax.rem(row, ROWS) + (row // rows_out) * ROWS
    mine = jnp.where(names - start == named.astype(F32), 1.0, 0.0)
    both = product(mine, pieces, ((0,), (0,)))
    both = jnp.concatenate([both[:rows_out], both[rows_out:]], axis=1)
    partial[...] = trial_partial[...] - both


def chosen(aggregate, group_count, half):
    rows = group_count // 2
    local_index = jnp.broadcast_to(lax.rem(aggregate[...], group_count), (rows, aggregate.shape[1]))
    row = lax.broadcasted_iota(jnp.int32, local_index.shape, 0)
    named = (row // ROWS) * (2 * ROWS) + lax.rem(row, ROWS) + half * ROWS
    return jnp.where(local_index == named, 1.0, 0.0).astype(F32)


def coarse_kernel(shares, coarse_inverse, out):
    size = coarse_inverse.shape[0]
    rows = shares.shape[0] // ROWS
    share = shares[0:ROWS]
    for row in range(1, rows):
        share = share + shares[row * ROWS : (row + 1) * ROWS]
    share = jnp.concatenate([share[:, :size], share[:, size:]], axis=0)
    lane = lanes(share)
    value = jnp.zeros_like(share)
    for i in range(size):
        total = jnp.sum(coarse_inverse[i].astype(F32) * share, axis=1, keepdims=True)
        value = jnp.where(lane == i, total, value)
    value = jnp.concatenate([value[:ROWS], value[ROWS:]], axis=1)
    for row in range(out.shape[0] // ROWS):
        out[row * ROWS : (row + 1) * ROWS] = value


def third_kernel(
    group_count, rhs, twice, values, diag, inverse, coupling, own, near, far, ghosts,
    prolong, aggregate, solution_out, residual, start, once, work,
):
    size, count = rhs.shape
    every = values.shape[0]
    in_group = group_count // 2
    group = pl.ds(pl.multiple_of(lax.axis_index("grp") * in_group, ROWS), in_group)
    mine = three(values[group, :])
    picked = [chosen(aggregate, group_count, half) for half in (0, 1)]
    picked = jnp.concatenate(picked, axis=1).astype(BF16)
    spread = jnp.zeros((size, count), F32)
    for part in mine:
        both = lax.dot_general(part, picked, (((0,), (0,)), ((), ())), preferred_element_type=F32)
        spread = spread + (both[:size, :count] + both[size:, count:])
    apply_blocks(prolong, spread, twice, start)

    sides, (left, right) = beyond_ends(even_device(), near, far, size)
    (left_blocks, left_pair), (right_blocks, right_pair) = sides
    column = columns_from(size)
    lane = lax.broadcasted_iota(jnp.int32, (size, count), 1)
    half = EDGE_ROWS
    blank = jnp.zeros((2, size), F32)
    names = jnp.concatenate([left[half + 7 : half + 10], right[7:10], blank], axis=0)[:, 0:1]
    source = lax.broadcasted_iota(jnp.int32, (ROWS, every), 1)
    first_name = (source // ROWS) * (2 * ROWS) + lax.rem(source, ROWS)
    everything = three(values[...])
    named = [
        jnp.where(names == (first_name + k * ROWS).astype(F32), 1.0, 0.0) for k in (0, 1)
    ]
    named = jnp.concatenate(named, axis=0).astype(BF16)
    coarse = jnp.zeros((ROWS, size), F32)
    for part in everything:
        both = jnp.dot(named, part, preferred_element_type=F32)
        coarse = coarse + (both[:ROWS, :size] + both[ROWS:, size:])

    (left_diag, left_inverse), (left_coupling, _) = left_blocks[:2]
    left_next_diag, left_next_inverse = left_blocks[4]
    left_pair, right_pair = jnp.transpose(left_pair), jnp.transpose(right_pair)
    left_turned, left_next_turned = left_pair[:size], left_pair[size:]
    (right_diag, right_inverse), (right_coupling, right_next_coupling) = right_blocks[:2]
    right_next_diag, right_next_inverse = right_blocks[4]
    right_turned, right_next_turned = right_pair[:size], right_pair[size:]
    right_third_coupling = right_blocks[3][1]
    first_coupling, first_turned = own[7], own[8]
    left_x, left_change, right_x, right_change = (ghosts[:, k : k + 1] for k in range(4))
    left_y, left_z = (column(left[half + k : half + k + 1]) for k in (3, 4))
    right_y, right_z = (column(right[k : k + 1]) for k in (3, 4))
    left_y = left_y - to_column(left_next_inverse, to_row(left_coupling, left_change))
    right_y = right_y - to_column(right_next_inverse, to_row(right_next_turned, right_change))
    prolongs = (left_blocks[2][0], left_blocks[2][1], left_blocks[3][0])
    prolongs = prolongs + (right_blocks[2][0], right_blocks[2][1], right_blocks[3][0])
    known = (left_x, left_y, left_z, right_x, right_y, right_z)
    left_x, left_y, left_z, right_x, right_y, right_z = (
        value + to_column(block, coarse[k : k + 1])
        for k, (value, block) in enumerate(zip(known, prolongs))
    )
    left_rhs, left_next_rhs = left[half + 5 : half + 6], left[half + 6 : half + 7]
    right_rhs, right_next_rhs = right[5:6], right[6:7]

    def added(left_column, right_column):
        return ends(
            lane,
            column(to_row(first_turned, left_column)),
            column(to_row(right_coupling, right_column)),
        )

    def nearest(vector, left_x, left_y, right_x, right_y):
        left_sum = to_row(left_diag, left_x) + to_row(left_turned, left_y)
        left_sum = left_sum + to_row(first_coupling, vector[:, 0:1])
        right_sum = to_row(right_diag, right_x) + to_row(right_turned, vector[:, count - 1 : count])
        right_sum = right_sum + to_row(right_next_coupling, right_y)
        return (
            left_x + to_column(left_inverse, left_rhs - left_sum),
            right_x + to_column(right_inverse, right_rhs - right_sum),
        )

    defect = wrong(rhs, start, diag, coupling, work) - added(left_x, right_x)
    left_once, right_once = nearest(start, left_x, left_y, right_x, right_y)
    left_sum = to_row(left_next_diag, left_y) + to_row(left_next_turned, left_z)
    left_sum = left_sum + to_row(left_coupling, left_x)
    left_y = left_y + to_column(left_next_inverse, left_next_rhs - left_sum)
    right_sum = to_row(right_next_diag, right_y) + to_row(right_next_turned, right_x)
    right_sum = right_sum + to_row(right_third_coupling, right_z)
    right_y = right_y + to_column(right_next_inverse, right_next_rhs - right_sum)
    apply_blocks(inverse, defect, start, once)
    defect = wrong(rhs, once, diag, coupling, work) - added(left_once, right_once)
    left_twice, right_twice = nearest(once, left_once, left_y, right_once, right_y)
    apply_blocks(inverse, defect, once, solution_out)
    defect = wrong(rhs, solution_out, diag, coupling, work)
    residual[...] = defect - added(left_twice, right_twice)


def call(kernel, outs, scratch, *operands, space=pltpu.VMEM, cost=None):
    inside = pl.BlockSpec(memory_space=pltpu.VMEM)
    if space == pltpu.HBM:
        operands = [pltpu.with_memory_space_constraint(x, space) for x in operands]
    single = not isinstance(outs, tuple)
    return pl.pallas_call(
        kernel,
        out_shape=outs,
        in_specs=[pl.BlockSpec(memory_space=space)] * len(operands),
        out_specs=inside if single else (inside,) * len(outs),
        scratch_shapes=scratch,
        cost_estimate=cost,
        compiler_params=pltpu.CompilerParams(vmem_limit_bytes=24 << 20),
    )(*operands)


def local(rhs, guess, diag_blocks, diag_inverse, coupling, prolong, coarse_inverse, aggregate):
    size, count = rhs.shape
    members = lax.axis_size("row")
    group_count = count * members // AGG
    assert coarse_inverse.shape[2] == 2 * ROWS and 2 * size == count and members % 2 == 0
    aggregate = aggregate.reshape(1, count)
    coarse_inverse = jnp.transpose(coarse_inverse, (0, 2, 1))

    def shape(*sizes, kind=F32):
        return jax.ShapeDtypeStruct(sizes, kind)

    tile = shape(size, count)
    blocks = shape(size, size, count)
    packed = shape(group_count // 2, count)
    edge = shape(TILES * size + 2 * EDGES, count, kind=BF16)
    line = shape(EDGES, size)
    plain = pltpu.VMEM((size, count), F32)
    half = pltpu.VMEM((size, size, count), BF16)
    loads = 2 + 3 * (size // LOAD) + 3
    (
        rhs, diag, inverse, coupling, prolong, coarse_inverse, aggregate,
        trial, trial_twice, near, far, own, rows,
    ) = call(
        first_kernel,
        (
            tile, blocks, blocks, blocks,
            shape(size, size, count, kind=BF16),
            shape(*coarse_inverse.shape, kind=BF16),
            shape(1, count, kind=jnp.int32),
            tile, tile, edge, edge, shape(22, size, size), line,
        ),
        [
            plain, half, half, half, plain,
            pltpu.SemaphoreType.DMA((loads,)),
        ],
        rhs, guess, diag_blocks, diag_inverse, coupling, prolong, coarse_inverse, aggregate,
        space=pltpu.HBM,
    )
    far = swap(far, 1)
    near = swap(near, 0)
    trial_partial = call(
        functools.partial(trial_kernel, group_count), packed, [plain],
        rhs, trial_twice, diag, coupling, prolong, aggregate,
        cost=pl.CostEstimate(flops=8 * size**2 * count, bytes_accessed=8 * size**2 * count, transcendentals=0),
    )
    twice, partial, ghosts = call(
        functools.partial(second_kernel, group_count), (tile, packed, tile), [],
        trial_partial, trial_twice, own, rows, near, far,
    )
    shares = lax.all_to_all(partial, "row", 0, 0, tiled=True)
    corrected = call(
        coarse_kernel, shape(lax.axis_size(BOTH) * ROWS, count), [], shares, coarse_inverse
    )
    values = lax.all_to_all(corrected, BOTH, 0, 0, tiled=True)
    return call(
        functools.partial(third_kernel, group_count), (tile, tile), [plain, plain, plain],
        rhs, twice, values, diag, inverse, coupling, own, near, far, ghosts, prolong, aggregate,
    )


def solution(mesh):
    vector = P(None, BOTH)
    blocks = P(None, None, BOTH)
    return jax.shard_map(
        local,
        mesh=mesh,
        in_specs=(vector, vector, blocks, blocks, blocks, blocks, blocks, P(BOTH)),
        out_specs=(vector, vector),
        check_vma=False,
    )
```

```python
import functools

import jax
import jax.numpy as jnp
from jax import lax
from jax.experimental import pallas as pl
from jax.experimental.pallas import tpu as pltpu
from jax.sharding import PartitionSpec as P

AGG = 8
BOTH = ("grp", "row")
F32 = jnp.float32
BF16 = jnp.bfloat16
ROWS = 8
LOAD = 16
EDGES = 24
EDGE_ROWS = 10
TILES = 5


def swap(block, first):
    pairs = [(i, i + 1) for i in range(first, lax.axis_size(BOTH) - 1, 2)]
    return lax.ppermute(block, BOTH, pairs + [(j, i) for i, j in pairs])


def even_device():
    return lax.rem(lax.axis_index("row"), 2) == 0


def lanes(like):
    return lax.broadcasted_iota(jnp.int32, like.shape, 1)


def turn(tile, shift):
    return pltpu.roll(tile, shift % tile.shape[1], 1)


def three(tile):
    high = tile.astype(BF16)
    rest = tile - high.astype(F32)
    middle = rest.astype(BF16)
    return high, middle, (rest - middle.astype(F32)).astype(BF16)


def product(left, right, dims):
    left = left.astype(BF16)
    parts = [
        lax.dot_general(left, part, (dims, ((), ())), preferred_element_type=F32)
        for part in three(right)
    ]
    return parts[0] + (parts[1] + parts[2])


def stack(rows):
    return jnp.concatenate([part.astype(F32) for part in three(rows)], axis=0)


def to_column(block, row):
    return jnp.sum(block * row, axis=1, keepdims=True)


def to_row(block, column):
    return jnp.sum(block * column, axis=0, keepdims=True)


def operate(diag, coupling, vector_ref, out_ref, lower):
    vector = vector_ref[...]

    def step(chunk, upward):
        start = pl.multiple_of(chunk * ROWS, ROWS)
        own = vector_ref[pl.ds(start, ROWS), :]
        sums = []
        for s in range(ROWS):
            pair = coupling[start + s]
            terms = diag[start + s] * vector + pair * lower
            sums.append(jnp.sum(terms, axis=0, keepdims=True))
            upward = upward + pair * own[s : s + 1, :]
        out_ref[pl.ds(start, ROWS), :] = jnp.concatenate(sums, axis=0)
        return upward

    return loop(vector.shape[0] // ROWS, step, jnp.zeros_like(vector))


def apply_blocks(blocks, vector, base_ref, out_ref):
    def step(chunk, carry):
        start = pl.multiple_of(chunk * ROWS, ROWS)
        sums = [
            jnp.sum(blocks[start + s].astype(F32) * vector, axis=0, keepdims=True)
            for s in range(ROWS)
        ]
        base = base_ref[pl.ds(start, ROWS), :]
        out_ref[pl.ds(start, ROWS), :] = base + jnp.concatenate(sums, axis=0)
        return carry

    loop(vector.shape[0] // ROWS, step, 0)


def apply_transposed(blocks, vector_ref):
    def step(chunk, total):
        start = pl.multiple_of(chunk * ROWS, ROWS)
        own = vector_ref[pl.ds(start, ROWS), :]
        for s in range(ROWS):
            total = total + blocks[start + s].astype(F32) * own[s : s + 1, :]
        return total

    zero = jnp.zeros(vector_ref.shape, F32)
    return loop(vector_ref.shape[0] // ROWS, step, zero)


def loop(count, step, carry):
    return lax.fori_loop(0, count, step, carry, unroll=True)


def place(tile, block, row):
    shape = (tile.shape[0] // ROWS, ROWS, tile.shape[1])
    lane = lax.broadcasted_iota(jnp.int32, (1,) + shape[1:], 2)
    mine = lax.shift_right_logical(lane, 3) == row
    turned = pltpu.roll(block, 8 * row + 3, 1).reshape(shape)
    return jnp.where(mine, turned, tile.reshape(shape)).reshape(tile.shape)


def picker(size, width, ends):
    shape = (size * len(ends), width)
    row = lax.broadcasted_iota(jnp.int32, shape, 0)
    lane = lax.broadcasted_iota(jnp.int32, shape, 1)
    target = 8 * lax.rem(row, size) + row // size + ends[0]
    return jnp.where(lane == target, 1.0, 0.0).astype(BF16)


def end_blocks(tiles, ends):
    packed = jnp.concatenate(tiles, axis=1).astype(BF16)
    size = packed.shape[0]
    blocks = lax.dot_general(
        picker(size, packed.shape[1], ends), packed, (((1,), (1,)), ((), ())),
        preferred_element_type=F32,
    )
    return [blocks[k * size : (k + 1) * size] for k in range(len(ends))]


def end_blocks_turned(tiles, ends):
    packed = jnp.concatenate(tiles, axis=1).astype(BF16)
    return lax.dot_general(
        packed, picker(packed.shape[0], packed.shape[1], ends), (((1,), (1,)), ((), ())),
        preferred_element_type=F32,
    )


def edge_rows(firsts, lasts, count):
    lane = lanes(firsts[0][0])
    tile = jnp.zeros(lane.shape, F32)
    for k, (column, where) in enumerate(firsts + lasts):
        tile = jnp.where(lane == k, turn(column, k - where), tile)
    return jnp.transpose(tile)[:EDGES]


def wrong(rhs_ref, vector_ref, diag, coupling, work):
    vector = vector_ref[...]
    lane = lanes(vector)
    lower = jnp.where(lane == 0, 0.0, turn(vector, 1))
    upward = operate(diag, coupling, vector_ref, work, lower)
    upper = jnp.where(lane == vector.shape[1] - 1, 0.0, turn(upward, -1))
    return rhs_ref[...] - (work[...] + upper)


def first_kernel(
    rhs_in, guess_in, diag_in, inverse_in, coupling_in, prolong_in, coarse_in, aggregate_in,
    rhs, diag, inverse, coupling, prolong, coarse, aggregate,
    trial, twice, near, far, rows_out,
    guess, diag_half, inverse_half, coupling_half, work, sems,
):
    size, count = guess.shape
    parts = diag_half.shape[0] // LOAD
    copies = [
        pltpu.make_async_copy(guess_in, guess, sems.at[0]),
        pltpu.make_async_copy(rhs_in, rhs, sems.at[1]),
    ]
    for p in range(parts):
        rows = pl.ds(p * LOAD, LOAD)
        for source, target in ((coupling_in, coupling_half), (diag_in, diag_half)):
            copies.append(
                pltpu.make_async_copy(source.at[rows], target.at[rows], sems.at[len(copies)])
            )
    for p in range(parts):
        rows = pl.ds(p * LOAD, LOAD)
        copies.append(
            pltpu.make_async_copy(inverse_in.at[rows], inverse_half.at[rows], sems.at[len(copies)])
        )
    for source, target in ((prolong_in, prolong), (coarse_in, coarse), (aggregate_in, aggregate)):
        copies.append(pltpu.make_async_copy(source, target, sems.at[len(copies)]))
    for copy in copies:
        copy.start()
    copies[0].wait()

    start = guess[...]
    lane = lanes(start)
    lower = jnp.where(lane == 0, 0.0, turn(start, 1))
    upward = jnp.zeros_like(start)
    diag_ends = [jnp.zeros_like(start) for _ in range(4)]
    inverse_ends, coupling_ends, prolong_ends = list(diag_ends), list(diag_ends), list(diag_ends)
    for chunk in range(size // ROWS):
        if chunk * ROWS % LOAD == 0:
            at = 2 + 2 * (chunk * ROWS // LOAD)
            copies[at].wait()
            copies[at + 1].wait()
        sums = []
        for i in range(chunk * ROWS, chunk * ROWS + ROWS):
            pair = coupling_half[i].astype(F32)
            block = diag_half[i].astype(F32)
            coupling[i] = pair
            diag[i] = block
            t, row = divmod(i, size // 4)
            diag_ends[t] = place(diag_ends[t], block, row)
            sums.append(jnp.sum(block * start + pair * lower, axis=0, keepdims=True))
            upward = upward + pair * guess[i : i + 1, :]
        work[pl.ds(chunk * ROWS, ROWS), :] = jnp.concatenate(sums, axis=0)
    upper = jnp.where(lane == count - 1, 0.0, turn(upward, -1))
    copies[1].wait()
    defect = rhs[...] - (work[...] + upper)

    for chunk in range(size // ROWS):
        if chunk * ROWS % LOAD == 0:
            copies[2 + 2 * parts + chunk * ROWS // LOAD].wait()
        rows = pl.ds(chunk * ROWS, ROWS)
        sums = []
        for i in range(chunk * ROWS, chunk * ROWS + ROWS):
            block = inverse_half[i].astype(F32)
            inverse[i] = block
            t, row = divmod(i, size // 4)
            inverse_ends[t] = place(inverse_ends[t], block, row)
            sums.append(jnp.sum(block * defect, axis=0, keepdims=True))
        trial[rows, :] = guess[rows, :] + jnp.concatenate(sums, axis=0)

    second = trial[...]
    lower = jnp.where(lane == 0, 0.0, turn(second, 1))
    upward = jnp.zeros_like(start)
    for chunk in range(size // ROWS):
        sums = []
        for i in range(chunk * ROWS, chunk * ROWS + ROWS):
            pair = coupling[i]
            t, row = divmod(i, size // 4)
            coupling_ends[t] = place(coupling_ends[t], pair, row)
            sums.append(jnp.sum(diag[i] * second + pair * lower, axis=0, keepdims=True))
            upward = upward + pair * trial[i : i + 1, :]
        work[pl.ds(chunk * ROWS, ROWS), :] = jnp.concatenate(sums, axis=0)
    upper = jnp.where(lane == count - 1, 0.0, turn(upward, -1))
    defect = rhs[...] - (work[...] + upper)

    for copy in copies[-3:]:
        copy.wait()
    for chunk in range(size // ROWS):
        rows = pl.ds(chunk * ROWS, ROWS)
        sums = []
        for i in range(chunk * ROWS, chunk * ROWS + ROWS):
            t, row = divmod(i, size // 4)
            prolong_ends[t] = place(prolong_ends[t], prolong[i].astype(F32), row)
            sums.append(jnp.sum(inverse[i] * defect, axis=0, keepdims=True))
        twice[rows, :] = trial[rows, :] + jnp.concatenate(sums, axis=0)

    last = count - 1
    named = jnp.broadcast_to(aggregate[...].astype(F32), (size, count))
    after = twice[...]
    both = [(start, 0), (second, 0), (defect, 0), (after, 1), (after, 2), (rhs[...], 0), (rhs[...], 1)]
    both = both + [(named, 0), (named, 1), (named, 2)]
    rows = edge_rows(both, [(column, last - k) for column, k in both], count)
    rows_out[...] = rows
    diag_turned = end_blocks_turned(diag_ends, (1, 2, 3, 4))
    inverses = end_blocks(inverse_ends, (1, 2, 3, 4))
    couplings = end_blocks(coupling_ends, (1, 2, 3, 4, 5))
    prolongs = end_blocks(prolong_ends, (0, 1, 2, 3, 4, 5))
    turned_diag = [diag_turned[:, k * size : (k + 1) * size] for k in range(4)]
    lasts = (
        (turned_diag[1], inverses[1]), (couplings[1], couplings[0]), (prolongs[2], prolongs[1]),
        (prolongs[0], couplings[4]), (turned_diag[0], inverses[0]),
    )
    firsts = (
        (turned_diag[2], inverses[2]), (couplings[2], couplings[3]), (prolongs[3], prolongs[4]),
        (prolongs[5], couplings[4]), (turned_diag[3], inverses[3]),
    )
    even = even_device()
    for k, (one, other) in enumerate(zip(lasts, firsts)):
        one, other = jnp.concatenate(one, axis=1), jnp.concatenate(other, axis=1)
        at = slice(k * size, (k + 1) * size)
        near[at] = jnp.where(even, one, other).astype(BF16)
        far[at] = jnp.where(even, other, one).astype(BF16)
    high, middle, low = (part.astype(F32) for part in three(rows))
    shares = jnp.concatenate(
        [jnp.concatenate([high, low], axis=1), jnp.concatenate([middle, low], axis=1)], axis=0
    ).astype(BF16)
    near[TILES * size :] = shares
    far[TILES * size :] = shares

def beyond_ends(even, near, far, size):
    near, far = near[...].astype(F32), far[...].astype(F32)
    sides, rows = [], []
    for side in (jnp.where(even, far, near), jnp.where(even, near, far)):
        pairs = [side[k * size : (k + 1) * size] for k in range(TILES)]
        sides.append(([(pair[:, :size], pair[:, size:]) for pair in pairs], pairs[1]))
        tail = side[TILES * size :]
        rows.append(tail[:EDGES, :size] + tail[EDGES:, :size] + tail[:EDGES, size:])
    return sides, rows


def columns_from(size):
    shape = (size, size)
    unit = lax.broadcasted_iota(jnp.int32, shape, 0) == lax.broadcasted_iota(jnp.int32, shape, 1)
    return lambda row: jnp.sum(jnp.where(unit, row, 0.0), axis=1, keepdims=True)


def ends(lane, first, last):
    return jnp.where(lane == 0, first, jnp.where(lane == lane.shape[1] - 1, last, 0.0))


def trial_kernel(
    group_count, rhs, trial_twice, diag, coupling, prolong, aggregate, near, far,
    partial, own, work,
):
    work[...] = wrong(rhs, trial_twice, diag, coupling, work)
    pieces = apply_transposed(prolong, work)
    picked = [chosen(aggregate, group_count, half) for half in (0, 1)]
    both = product(jnp.concatenate(picked, axis=0), pieces, ((1,), (1,)))
    rows_out = group_count // 2
    partial[...] = jnp.concatenate([both[:rows_out], both[rows_out:]], axis=1)

    size = rhs.shape[0]
    even = even_device()
    near, far = near[: TILES * size].astype(F32), far[: TILES * size].astype(F32)
    lasts, firsts = (
        [side[k * size : (k + 1) * size] for k in range(TILES)]
        for side in (jnp.where(even, near, far), jnp.where(even, far, near))
    )
    turned_last, turned_first = jnp.transpose(lasts[1]), jnp.transpose(firsts[1])
    turned_third = jnp.transpose(firsts[3])[size:]
    lasts = [(tile[:, :size], tile[:, size:]) for tile in lasts]
    firsts = [(tile[:, :size], tile[:, size:]) for tile in firsts]
    blocks = (
        lasts[0][0], firsts[0][0], lasts[4][1], lasts[0][1], firsts[0][1], firsts[4][1],
        lasts[1][0], firsts[1][0], turned_first[:size], turned_first[size:],
        lasts[4][0], firsts[4][0], lasts[1][1], firsts[1][1], turned_last[:size], turned_third,
        lasts[3][0], lasts[2][1], lasts[2][0], firsts[2][0], firsts[2][1], firsts[3][0],
    )
    for k, block in enumerate(blocks):
        own[k] = block


def second_kernel(
    group_count, trial_partial, trial_twice, own, rows, near, far, twice, partial, ghosts,
):
    size, count = trial_twice.shape
    sides, (left, right) = beyond_ends(even_device(), near, far, size)
    (left_blocks, _), (right_blocks, right_pair) = sides
    column = columns_from(size)
    half = EDGE_ROWS
    left_diag, left_inverse = left_blocks[0]
    (right_diag, right_inverse), (right_coupling, _) = right_blocks[:2]
    right_turned = jnp.transpose(right_pair)[:size]
    last_diag, first_diag = own[0], own[1]
    before_inverse, last_inverse, first_inverse, second_inverse = (own[2 + k] for k in range(4))
    last_coupling, first_coupling, first_turned, second_turned = (own[6 + k] for k in range(4))
    first_start, first_trial, last_start, last_trial = (
        column(rows[k : k + 1]) for k in (0, 1, half, half + 1)
    )
    left_start, left_trial = (column(left[half + k : half + k + 1]) for k in (0, 1))
    right_start, right_trial = (column(right[k : k + 1]) for k in (0, 1))
    left_wrong, right_wrong = left[half + 2 : half + 3], right[2:3]

    first_change = -to_column(first_inverse, to_row(first_turned, left_start))
    last_change = -to_column(last_inverse, to_row(right_coupling, right_start))
    left_change = -to_column(left_inverse, to_row(first_coupling, first_start))
    right_change = -to_column(right_inverse, to_row(right_turned, last_start))
    left_once, right_once = left_trial + left_change, right_trial + right_change
    first_added = to_row(first_diag, first_change) + to_row(first_turned, left_once)
    last_added = to_row(last_diag, last_change) + to_row(right_coupling, right_once)
    left_added = to_row(left_diag, left_change)
    left_added = left_added + to_row(first_coupling, first_trial + first_change)
    right_added = to_row(right_diag, right_change)
    right_added = right_added + to_row(right_turned, last_trial + last_change)
    left_twice = left_once + to_column(left_inverse, left_wrong - left_added)
    right_twice = right_once + to_column(right_inverse, right_wrong - right_added)
    second_added = to_row(second_turned, first_change)
    before_added = to_row(last_coupling, last_change)
    lane = lax.broadcasted_iota(jnp.int32, (size, count), 1)
    first_new = first_change - to_column(first_inverse, first_added)
    second_new = -to_column(second_inverse, second_added)
    before_new = -to_column(before_inverse, before_added)
    last_new = last_change - to_column(last_inverse, last_added)
    change = ends(lane, first_new, last_new)
    change = jnp.where(lane == 1, second_new, change)
    change = jnp.where(lane == count - 2, before_new, change)
    twice[...] = trial_twice[...] + change
    tile = jnp.zeros((size, count), F32)
    for k, ghost in enumerate((left_twice, left_change, right_twice, right_change)):
        tile = jnp.where(lane == k, ghost, tile)
    ghosts[...] = tile
    before_diag, second_diag, before_coupling, second_coupling = (own[10 + k] for k in range(4))
    last_turned, third_turned = own[14], own[15]
    prolongs = [own[16 + k] for k in range(6)]
    added = (
        to_row(before_coupling, before_new),
        to_row(before_diag, before_new) + to_row(last_coupling, last_new),
        to_row(last_diag, last_new) + to_row(last_turned, before_new)
        + to_row(right_coupling, right_twice),
        to_row(first_diag, first_new) + to_row(second_coupling, second_new)
        + to_row(first_turned, left_twice),
        to_row(second_diag, second_new) + to_row(second_turned, first_new),
        to_row(third_turned, second_new),
    )
    pieces = [to_row(block, column(row)) for block, row in zip(prolongs, added)]
    order = (half + 9, half + 8, half + 7, 7, 8, 9)
    names = [rows[k : k + 1] for k in order]
    blank = jnp.zeros((ROWS - 6, size), F32)
    pieces = jnp.concatenate(pieces + [blank], axis=0)
    names = jnp.concatenate(names + [blank], axis=0)[:, 0:1]
    rows_out = group_count // 2
    start = (lax.axis_index("grp") * group_count).astype(F32)
    row = lax.broadcasted_iota(jnp.int32, (ROWS, 2 * rows_out), 1)
    half_row = lax.rem(row, rows_out)
    named = (half_row // ROWS) * (2 * ROWS) + lax.rem(row, ROWS) + (row // rows_out) * ROWS
    mine = jnp.where(names - start == named.astype(F32), 1.0, 0.0)
    both = product(mine, pieces, ((0,), (0,)))
    both = jnp.concatenate([both[:rows_out], both[rows_out:]], axis=1)
    partial[...] = trial_partial[...] - both


def chosen(aggregate, group_count, half):
    rows = group_count // 2
    local_index = jnp.broadcast_to(lax.rem(aggregate[...], group_count), (rows, aggregate.shape[1]))
    row = lax.broadcasted_iota(jnp.int32, local_index.shape, 0)
    named = (row // ROWS) * (2 * ROWS) + lax.rem(row, ROWS) + half * ROWS
    return jnp.where(local_index == named, 1.0, 0.0).astype(F32)


def coarse_kernel(shares, coarse_inverse, out):
    size = coarse_inverse.shape[0]
    rows = shares.shape[0] // ROWS
    share = shares[0:ROWS]
    for row in range(1, rows):
        share = share + shares[row * ROWS : (row + 1) * ROWS]
    share = jnp.concatenate([share[:, :size], share[:, size:]], axis=0)
    lane = lanes(share)
    value = jnp.zeros_like(share)
    for i in range(size):
        total = jnp.sum(coarse_inverse[i].astype(F32) * share, axis=1, keepdims=True)
        value = jnp.where(lane == i, total, value)
    value = jnp.concatenate([value[:ROWS], value[ROWS:]], axis=1)
    for row in range(out.shape[0] // ROWS):
        out[row * ROWS : (row + 1) * ROWS] = value


def third_kernel(
    group_count, rhs, twice, values, diag, inverse, coupling, own, near, far, ghosts,
    prolong, aggregate, solution_out, residual, start, once, work,
):
    size, count = rhs.shape
    every = values.shape[0]
    in_group = group_count // 2
    group = pl.ds(pl.multiple_of(lax.axis_index("grp") * in_group, ROWS), in_group)
    mine = three(values[group, :])
    picked = [chosen(aggregate, group_count, half) for half in (0, 1)]
    picked = jnp.concatenate(picked, axis=1).astype(BF16)
    spread = jnp.zeros((size, count), F32)
    for part in mine:
        both = lax.dot_general(part, picked, (((0,), (0,)), ((), ())), preferred_element_type=F32)
        spread = spread + (both[:size, :count] + both[size:, count:])
    apply_blocks(prolong, spread, twice, start)

    sides, (left, right) = beyond_ends(even_device(), near, far, size)
    (left_blocks, left_pair), (right_blocks, right_pair) = sides
    column = columns_from(size)
    lane = lax.broadcasted_iota(jnp.int32, (size, count), 1)
    half = EDGE_ROWS
    blank = jnp.zeros((2, size), F32)
    names = jnp.concatenate([left[half + 7 : half + 10], right[7:10], blank], axis=0)[:, 0:1]
    source = lax.broadcasted_iota(jnp.int32, (ROWS, every), 1)
    first_name = (source // ROWS) * (2 * ROWS) + lax.rem(source, ROWS)
    everything = three(values[...])
    named = [
        jnp.where(names == (first_name + k * ROWS).astype(F32), 1.0, 0.0) for k in (0, 1)
    ]
    named = jnp.concatenate(named, axis=0).astype(BF16)
    coarse = jnp.zeros((ROWS, size), F32)
    for part in everything:
        both = jnp.dot(named, part, preferred_element_type=F32)
        coarse = coarse + (both[:ROWS, :size] + both[ROWS:, size:])

    (left_diag, left_inverse), (left_coupling, _) = left_blocks[:2]
    left_next_diag, left_next_inverse = left_blocks[4]
    left_pair, right_pair = jnp.transpose(left_pair), jnp.transpose(right_pair)
    left_turned, left_next_turned = left_pair[:size], left_pair[size:]
    (right_diag, right_inverse), (right_coupling, right_next_coupling) = right_blocks[:2]
    right_next_diag, right_next_inverse = right_blocks[4]
    right_turned, right_next_turned = right_pair[:size], right_pair[size:]
    right_third_coupling = right_blocks[3][1]
    first_coupling, first_turned = own[7], own[8]
    left_x, left_change, right_x, right_change = (ghosts[:, k : k + 1] for k in range(4))
    left_y, left_z = (column(left[half + k : half + k + 1]) for k in (3, 4))
    right_y, right_z = (column(right[k : k + 1]) for k in (3, 4))
    left_y = left_y - to_column(left_next_inverse, to_row(left_coupling, left_change))
    right_y = right_y - to_column(right_next_inverse, to_row(right_next_turned, right_change))
    prolongs = (left_blocks[2][0], left_blocks[2][1], left_blocks[3][0])
    prolongs = prolongs + (right_blocks[2][0], right_blocks[2][1], right_blocks[3][0])
    known = (left_x, left_y, left_z, right_x, right_y, right_z)
    left_x, left_y, left_z, right_x, right_y, right_z = (
        value + to_column(block, coarse[k : k + 1])
        for k, (value, block) in enumerate(zip(known, prolongs))
    )
    left_rhs, left_next_rhs = left[half + 5 : half + 6], left[half + 6 : half + 7]
    right_rhs, right_next_rhs = right[5:6], right[6:7]

    def added(left_column, right_column):
        return ends(
            lane,
            column(to_row(first_turned, left_column)),
            column(to_row(right_coupling, right_column)),
        )

    def nearest(vector, left_x, left_y, right_x, right_y):
        left_sum = to_row(left_diag, left_x) + to_row(left_turned, left_y)
        left_sum = left_sum + to_row(first_coupling, vector[:, 0:1])
        right_sum = to_row(right_diag, right_x) + to_row(right_turned, vector[:, count - 1 : count])
        right_sum = right_sum + to_row(right_next_coupling, right_y)
        return (
            left_x + to_column(left_inverse, left_rhs - left_sum),
            right_x + to_column(right_inverse, right_rhs - right_sum),
        )

    defect = wrong(rhs, start, diag, coupling, work) - added(left_x, right_x)
    left_once, right_once = nearest(start, left_x, left_y, right_x, right_y)
    left_sum = to_row(left_next_diag, left_y) + to_row(left_next_turned, left_z)
    left_sum = left_sum + to_row(left_coupling, left_x)
    left_y = left_y + to_column(left_next_inverse, left_next_rhs - left_sum)
    right_sum = to_row(right_next_diag, right_y) + to_row(right_next_turned, right_x)
    right_sum = right_sum + to_row(right_third_coupling, right_z)
    right_y = right_y + to_column(right_next_inverse, right_next_rhs - right_sum)
    apply_blocks(inverse, defect, start, once)
    defect = wrong(rhs, once, diag, coupling, work) - added(left_once, right_once)
    left_twice, right_twice = nearest(once, left_once, left_y, right_once, right_y)
    apply_blocks(inverse, defect, once, solution_out)
    defect = wrong(rhs, solution_out, diag, coupling, work)
    residual[...] = defect - added(left_twice, right_twice)


def call(kernel, outs, scratch, *operands, space=pltpu.VMEM, cost=None):
    inside = pl.BlockSpec(memory_space=pltpu.VMEM)
    if space == pltpu.HBM:
        operands = [pltpu.with_memory_space_constraint(x, space) for x in operands]
    single = not isinstance(outs, tuple)
    return pl.pallas_call(
        kernel,
        out_shape=outs,
        in_specs=[pl.BlockSpec(memory_space=space)] * len(operands),
        out_specs=inside if single else (inside,) * len(outs),
        scratch_shapes=scratch,
        cost_estimate=cost,
        compiler_params=pltpu.CompilerParams(vmem_limit_bytes=24 << 20),
    )(*operands)


def local(rhs, guess, diag_blocks, diag_inverse, coupling, prolong, coarse_inverse, aggregate):
    size, count = rhs.shape
    members = lax.axis_size("row")
    group_count = count * members // AGG
    assert coarse_inverse.shape[2] == 2 * ROWS and 2 * size == count and members % 2 == 0
    aggregate = aggregate.reshape(1, count)
    coarse_inverse = jnp.transpose(coarse_inverse, (0, 2, 1))

    def shape(*sizes, kind=F32):
        return jax.ShapeDtypeStruct(sizes, kind)

    tile = shape(size, count)
    blocks = shape(size, size, count)
    packed = shape(group_count // 2, count)
    edge = shape(TILES * size + 2 * EDGES, count, kind=BF16)
    line = shape(EDGES, size)
    plain = pltpu.VMEM((size, count), F32)
    half = pltpu.VMEM((size, size, count), BF16)
    loads = 2 + 3 * (size // LOAD) + 3
    (
        rhs, diag, inverse, coupling, prolong, coarse_inverse, aggregate,
        trial, trial_twice, near, far, rows,
    ) = call(
        first_kernel,
        (
            tile, blocks, blocks, blocks,
            shape(size, size, count, kind=BF16),
            shape(*coarse_inverse.shape, kind=BF16),
            shape(1, count, kind=jnp.int32),
            tile, tile, edge, edge, line,
        ),
        [
            plain, half, half, half, plain,
            pltpu.SemaphoreType.DMA((loads,)),
        ],
        rhs, guess, diag_blocks, diag_inverse, coupling, prolong, coarse_inverse, aggregate,
        space=pltpu.HBM,
    )
    trial_partial, own = call(
        functools.partial(trial_kernel, group_count), (packed, shape(22, size, size)), [plain],
        rhs, trial_twice, diag, coupling, prolong, aggregate, near, far,
        cost=pl.CostEstimate(flops=8 * size**2 * count, bytes_accessed=8 * size**2 * count, transcendentals=0),
    )
    far = swap(far, 1)
    near = swap(near, 0)
    twice, partial, ghosts = call(
        functools.partial(second_kernel, group_count), (tile, packed, tile), [],
        trial_partial, trial_twice, own, rows, near, far,
    )
    shares = lax.all_to_all(partial, "row", 0, 0, tiled=True)
    corrected = call(
        coarse_kernel, shape(lax.axis_size(BOTH) * ROWS, count), [], shares, coarse_inverse
    )
    values = lax.all_to_all(corrected, BOTH, 0, 0, tiled=True)
    return call(
        functools.partial(third_kernel, group_count), (tile, tile), [plain, plain, plain],
        rhs, twice, values, diag, inverse, coupling, own, near, far, ghosts, prolong, aggregate,
    )


def solution(mesh):
    vector = P(None, BOTH)
    blocks = P(None, None, BOTH)
    return jax.shard_map(
        local,
        mesh=mesh,
        in_specs=(vector, vector, blocks, blocks, blocks, blocks, blocks, P(BOTH)),
        out_specs=(vector, vector),
        check_vma=False,
    )
```

```python
import functools

import jax
import jax.numpy as jnp
from jax import lax
from jax.experimental import pallas as pl
from jax.experimental.pallas import tpu as pltpu
from jax.sharding import PartitionSpec as P

AGG = 8
BOTH = ("grp", "row")
F32 = jnp.float32
BF16 = jnp.bfloat16
ROWS = 8
LOAD = 16
EDGES = 24
EDGE_ROWS = 10
TILES = 5


def swap(block, first):
    pairs = [(i, i + 1) for i in range(first, lax.axis_size(BOTH) - 1, 2)]
    return lax.ppermute(block, BOTH, pairs + [(j, i) for i, j in pairs])


def even_device():
    return lax.rem(lax.axis_index("row"), 2) == 0


def lanes(like):
    return lax.broadcasted_iota(jnp.int32, like.shape, 1)


def turn(tile, shift):
    return pltpu.roll(tile, shift % tile.shape[1], 1)


def three(tile):
    high = tile.astype(BF16)
    rest = tile - high.astype(F32)
    middle = rest.astype(BF16)
    return high, middle, (rest - middle.astype(F32)).astype(BF16)


def product(left, right, dims):
    left = left.astype(BF16)
    parts = [
        lax.dot_general(left, part, (dims, ((), ())), preferred_element_type=F32)
        for part in three(right)
    ]
    return parts[0] + (parts[1] + parts[2])


def stack(rows):
    return jnp.concatenate([part.astype(F32) for part in three(rows)], axis=0)


def to_column(block, row):
    return jnp.sum(block * row, axis=1, keepdims=True)


def to_row(block, column):
    return jnp.sum(block * column, axis=0, keepdims=True)


def operate(diag, coupling, vector_ref, out_ref, lower):
    vector = vector_ref[...]

    def step(chunk, upward):
        start = pl.multiple_of(chunk * ROWS, ROWS)
        own = vector_ref[pl.ds(start, ROWS), :]
        sums = []
        for s in range(ROWS):
            pair = coupling[start + s]
            terms = diag[start + s] * vector + pair * lower
            sums.append(jnp.sum(terms, axis=0, keepdims=True))
            upward = upward + pair * own[s : s + 1, :]
        out_ref[pl.ds(start, ROWS), :] = jnp.concatenate(sums, axis=0)
        return upward

    return loop(vector.shape[0] // ROWS, step, jnp.zeros_like(vector))


def apply_blocks(blocks, vector, base_ref, out_ref):
    def step(chunk, carry):
        start = pl.multiple_of(chunk * ROWS, ROWS)
        sums = [
            jnp.sum(blocks[start + s].astype(F32) * vector, axis=0, keepdims=True)
            for s in range(ROWS)
        ]
        base = base_ref[pl.ds(start, ROWS), :]
        out_ref[pl.ds(start, ROWS), :] = base + jnp.concatenate(sums, axis=0)
        return carry

    loop(vector.shape[0] // ROWS, step, 0)


def apply_transposed(blocks, vector_ref):
    def step(chunk, total):
        start = pl.multiple_of(chunk * ROWS, ROWS)
        own = vector_ref[pl.ds(start, ROWS), :]
        for s in range(ROWS):
            total = total + blocks[start + s].astype(F32) * own[s : s + 1, :]
        return total

    zero = jnp.zeros(vector_ref.shape, F32)
    return loop(vector_ref.shape[0] // ROWS, step, zero)


def loop(count, step, carry):
    return lax.fori_loop(0, count, step, carry, unroll=True)


def place(tile, block, row):
    shape = (tile.shape[0] // ROWS, ROWS, tile.shape[1])
    lane = lax.broadcasted_iota(jnp.int32, (1,) + shape[1:], 2)
    mine = lax.shift_right_logical(lane, 3) == row
    turned = pltpu.roll(block, 8 * row + 3, 1).reshape(shape)
    return jnp.where(mine, turned, tile.reshape(shape)).reshape(tile.shape)


def picker(size, width, ends):
    shape = (size * len(ends), width)
    row = lax.broadcasted_iota(jnp.int32, shape, 0)
    lane = lax.broadcasted_iota(jnp.int32, shape, 1)
    target = 8 * lax.rem(row, size) + row // size + ends[0]
    return jnp.where(lane == target, 1.0, 0.0).astype(BF16)


def end_blocks(tiles, ends):
    packed = jnp.concatenate(tiles, axis=1).astype(BF16)
    size = packed.shape[0]
    blocks = lax.dot_general(
        picker(size, packed.shape[1], ends), packed, (((1,), (1,)), ((), ())),
        preferred_element_type=F32,
    )
    return [blocks[k * size : (k + 1) * size] for k in range(len(ends))]


def end_blocks_turned(tiles, ends):
    packed = jnp.concatenate(tiles, axis=1).astype(BF16)
    return lax.dot_general(
        packed, picker(packed.shape[0], packed.shape[1], ends), (((1,), (1,)), ((), ())),
        preferred_element_type=F32,
    )


def edge_rows(firsts, lasts, count):
    lane = lanes(firsts[0][0])
    tile = jnp.zeros(lane.shape, F32)
    for k, (column, where) in enumerate(firsts + lasts):
        tile = jnp.where(lane == k, turn(column, k - where), tile)
    return jnp.transpose(tile)[:EDGES]


def wrong(rhs_ref, vector_ref, diag, coupling, work):
    vector = vector_ref[...]
    lane = lanes(vector)
    lower = jnp.where(lane == 0, 0.0, turn(vector, 1))
    upward = operate(diag, coupling, vector_ref, work, lower)
    upper = jnp.where(lane == vector.shape[1] - 1, 0.0, turn(upward, -1))
    return rhs_ref[...] - (work[...] + upper)


def first_kernel(
    rhs_in, guess_in, diag_in, inverse_in, coupling_in, prolong_in, coarse_in, aggregate_in,
    rhs, diag, inverse, coupling, prolong, coarse, aggregate,
    twice, near, far, rows_out,
    trial, guess, diag_half, inverse_half, coupling_half, work, sems,
):
    size, count = guess.shape
    parts = diag_half.shape[0] // LOAD
    copies = [
        pltpu.make_async_copy(guess_in, guess, sems.at[0]),
        pltpu.make_async_copy(rhs_in, rhs, sems.at[1]),
    ]
    for p in range(parts):
        rows = pl.ds(p * LOAD, LOAD)
        for source, target in ((coupling_in, coupling_half), (diag_in, diag_half)):
            copies.append(
                pltpu.make_async_copy(source.at[rows], target.at[rows], sems.at[len(copies)])
            )
    for p in range(parts):
        rows = pl.ds(p * LOAD, LOAD)
        copies.append(
            pltpu.make_async_copy(inverse_in.at[rows], inverse_half.at[rows], sems.at[len(copies)])
        )
    for source, target in ((prolong_in, prolong), (coarse_in, coarse), (aggregate_in, aggregate)):
        copies.append(pltpu.make_async_copy(source, target, sems.at[len(copies)]))
    for copy in copies:
        copy.start()
    copies[0].wait()

    start = guess[...]
    lane = lanes(start)
    lower = jnp.where(lane == 0, 0.0, turn(start, 1))
    upward = jnp.zeros_like(start)
    diag_ends = [jnp.zeros_like(start) for _ in range(4)]
    inverse_ends, coupling_ends, prolong_ends = list(diag_ends), list(diag_ends), list(diag_ends)
    for chunk in range(size // ROWS):
        if chunk * ROWS % LOAD == 0:
            at = 2 + 2 * (chunk * ROWS // LOAD)
            copies[at].wait()
            copies[at + 1].wait()
        sums = []
        for i in range(chunk * ROWS, chunk * ROWS + ROWS):
            pair = coupling_half[i].astype(F32)
            block = diag_half[i].astype(F32)
            coupling[i] = pair
            diag[i] = block
            t, row = divmod(i, size // 4)
            diag_ends[t] = place(diag_ends[t], block, row)
            sums.append(jnp.sum(block * start + pair * lower, axis=0, keepdims=True))
            upward = upward + pair * guess[i : i + 1, :]
        work[pl.ds(chunk * ROWS, ROWS), :] = jnp.concatenate(sums, axis=0)
    upper = jnp.where(lane == count - 1, 0.0, turn(upward, -1))
    copies[1].wait()
    defect = rhs[...] - (work[...] + upper)

    for chunk in range(size // ROWS):
        if chunk * ROWS % LOAD == 0:
            copies[2 + 2 * parts + chunk * ROWS // LOAD].wait()
        rows = pl.ds(chunk * ROWS, ROWS)
        sums = []
        for i in range(chunk * ROWS, chunk * ROWS + ROWS):
            block = inverse_half[i].astype(F32)
            inverse[i] = block
            t, row = divmod(i, size // 4)
            inverse_ends[t] = place(inverse_ends[t], block, row)
            sums.append(jnp.sum(block * defect, axis=0, keepdims=True))
        trial[rows, :] = guess[rows, :] + jnp.concatenate(sums, axis=0)

    second = trial[...]
    lower = jnp.where(lane == 0, 0.0, turn(second, 1))
    upward = jnp.zeros_like(start)
    for chunk in range(size // ROWS):
        sums = []
        for i in range(chunk * ROWS, chunk * ROWS + ROWS):
            pair = coupling[i]
            t, row = divmod(i, size // 4)
            coupling_ends[t] = place(coupling_ends[t], pair, row)
            sums.append(jnp.sum(diag[i] * second + pair * lower, axis=0, keepdims=True))
            upward = upward + pair * trial[i : i + 1, :]
        work[pl.ds(chunk * ROWS, ROWS), :] = jnp.concatenate(sums, axis=0)
    upper = jnp.where(lane == count - 1, 0.0, turn(upward, -1))
    defect = rhs[...] - (work[...] + upper)

    for copy in copies[-3:]:
        copy.wait()
    for chunk in range(size // ROWS):
        rows = pl.ds(chunk * ROWS, ROWS)
        sums = []
        for i in range(chunk * ROWS, chunk * ROWS + ROWS):
            t, row = divmod(i, size // 4)
            prolong_ends[t] = place(prolong_ends[t], prolong[i].astype(F32), row)
            sums.append(jnp.sum(inverse[i] * defect, axis=0, keepdims=True))
        twice[rows, :] = trial[rows, :] + jnp.concatenate(sums, axis=0)

    last = count - 1
    named = jnp.broadcast_to(aggregate[...].astype(F32), (size, count))
    after = twice[...]
    both = [(start, 0), (second, 0), (defect, 0), (after, 1), (after, 2), (rhs[...], 0), (rhs[...], 1)]
    both = both + [(named, 0), (named, 1), (named, 2)]
    rows = edge_rows(both, [(column, last - k) for column, k in both], count)
    rows_out[...] = rows
    diag_turned = end_blocks_turned(diag_ends, (1, 2, 3, 4))
    inverses = end_blocks(inverse_ends, (1, 2, 3, 4))
    couplings = end_blocks(coupling_ends, (1, 2, 3, 4, 5))
    prolongs = end_blocks(prolong_ends, (0, 1, 2, 3, 4, 5))
    turned_diag = [diag_turned[:, k * size : (k + 1) * size] for k in range(4)]
    lasts = (
        (turned_diag[1], inverses[1]), (couplings[1], couplings[0]), (prolongs[2], prolongs[1]),
        (prolongs[0], couplings[4]), (turned_diag[0], inverses[0]),
    )
    firsts = (
        (turned_diag[2], inverses[2]), (couplings[2], couplings[3]), (prolongs[3], prolongs[4]),
        (prolongs[5], couplings[4]), (turned_diag[3], inverses[3]),
    )
    even = even_device()
    for k, (one, other) in enumerate(zip(lasts, firsts)):
        one, other = jnp.concatenate(one, axis=1), jnp.concatenate(other, axis=1)
        at = slice(k * size, (k + 1) * size)
        near[at] = jnp.where(even, one, other).astype(BF16)
        far[at] = jnp.where(even, other, one).astype(BF16)
    high, middle, low = (part.astype(F32) for part in three(rows))
    shares = jnp.concatenate(
        [jnp.concatenate([high, low], axis=1), jnp.concatenate([middle, low], axis=1)], axis=0
    ).astype(BF16)
    near[TILES * size :] = shares
    far[TILES * size :] = shares

def beyond_ends(even, near, far, size):
    near, far = near[...].astype(F32), far[...].astype(F32)
    sides, rows = [], []
    for side in (jnp.where(even, far, near), jnp.where(even, near, far)):
        pairs = [side[k * size : (k + 1) * size] for k in range(TILES)]
        sides.append(([(pair[:, :size], pair[:, size:]) for pair in pairs], pairs[1]))
        tail = side[TILES * size :]
        rows.append(tail[:EDGES, :size] + tail[EDGES:, :size] + tail[:EDGES, size:])
    return sides, rows


def columns_from(size):
    shape = (size, size)
    unit = lax.broadcasted_iota(jnp.int32, shape, 0) == lax.broadcasted_iota(jnp.int32, shape, 1)
    return lambda row: jnp.sum(jnp.where(unit, row, 0.0), axis=1, keepdims=True)


def ends(lane, first, last):
    return jnp.where(lane == 0, first, jnp.where(lane == lane.shape[1] - 1, last, 0.0))


def trial_kernel(
    group_count, rhs, trial_twice, diag, coupling, prolong, aggregate, near, far,
    partial, own, work,
):
    work[...] = wrong(rhs, trial_twice, diag, coupling, work)
    pieces = apply_transposed(prolong, work)
    picked = [chosen(aggregate, group_count, half) for half in (0, 1)]
    both = product(jnp.concatenate(picked, axis=0), pieces, ((1,), (1,)))
    rows_out = group_count // 2
    partial[...] = jnp.concatenate([both[:rows_out], both[rows_out:]], axis=1)

    size = rhs.shape[0]
    even = even_device()
    near, far = near[: TILES * size].astype(F32), far[: TILES * size].astype(F32)
    lasts, firsts = (
        [side[k * size : (k + 1) * size] for k in range(TILES)]
        for side in (jnp.where(even, near, far), jnp.where(even, far, near))
    )
    turned_last, turned_first = jnp.transpose(lasts[1]), jnp.transpose(firsts[1])
    turned_third = jnp.transpose(firsts[3])[size:]
    lasts = [(tile[:, :size], tile[:, size:]) for tile in lasts]
    firsts = [(tile[:, :size], tile[:, size:]) for tile in firsts]
    blocks = (
        lasts[0][0], firsts[0][0], lasts[4][1], lasts[0][1], firsts[0][1], firsts[4][1],
        lasts[1][0], firsts[1][0], turned_first[:size], turned_first[size:],
        lasts[4][0], firsts[4][0], lasts[1][1], firsts[1][1], turned_last[:size], turned_third,
        lasts[3][0], lasts[2][1], lasts[2][0], firsts[2][0], firsts[2][1], firsts[3][0],
    )
    for k, block in enumerate(blocks):
        own[k] = block


def second_kernel(
    group_count, trial_partial, trial_twice, own, rows, near, far, twice, partial, ghosts,
):
    size, count = trial_twice.shape
    sides, (left, right) = beyond_ends(even_device(), near, far, size)
    (left_blocks, _), (right_blocks, right_pair) = sides
    column = columns_from(size)
    half = EDGE_ROWS
    left_diag, left_inverse = left_blocks[0]
    (right_diag, right_inverse), (right_coupling, _) = right_blocks[:2]
    right_turned = jnp.transpose(right_pair)[:size]
    last_diag, first_diag = own[0], own[1]
    before_inverse, last_inverse, first_inverse, second_inverse = (own[2 + k] for k in range(4))
    last_coupling, first_coupling, first_turned, second_turned = (own[6 + k] for k in range(4))
    first_start, first_trial, last_start, last_trial = (
        column(rows[k : k + 1]) for k in (0, 1, half, half + 1)
    )
    left_start, left_trial = (column(left[half + k : half + k + 1]) for k in (0, 1))
    right_start, right_trial = (column(right[k : k + 1]) for k in (0, 1))
    left_wrong, right_wrong = left[half + 2 : half + 3], right[2:3]

    first_change = -to_column(first_inverse, to_row(first_turned, left_start))
    last_change = -to_column(last_inverse, to_row(right_coupling, right_start))
    left_change = -to_column(left_inverse, to_row(first_coupling, first_start))
    right_change = -to_column(right_inverse, to_row(right_turned, last_start))
    left_once, right_once = left_trial + left_change, right_trial + right_change
    first_added = to_row(first_diag, first_change) + to_row(first_turned, left_once)
    last_added = to_row(last_diag, last_change) + to_row(right_coupling, right_once)
    left_added = to_row(left_diag, left_change)
    left_added = left_added + to_row(first_coupling, first_trial + first_change)
    right_added = to_row(right_diag, right_change)
    right_added = right_added + to_row(right_turned, last_trial + last_change)
    left_twice = left_once + to_column(left_inverse, left_wrong - left_added)
    right_twice = right_once + to_column(right_inverse, right_wrong - right_added)
    second_added = to_row(second_turned, first_change)
    before_added = to_row(last_coupling, last_change)
    lane = lax.broadcasted_iota(jnp.int32, (size, count), 1)
    first_new = first_change - to_column(first_inverse, first_added)
    second_new = -to_column(second_inverse, second_added)
    before_new = -to_column(before_inverse, before_added)
    last_new = last_change - to_column(last_inverse, last_added)
    change = ends(lane, first_new, last_new)
    change = jnp.where(lane == 1, second_new, change)
    change = jnp.where(lane == count - 2, before_new, change)
    twice[...] = trial_twice[...] + change
    tile = jnp.zeros((size, count), F32)
    for k, ghost in enumerate((left_twice, left_change, right_twice, right_change)):
        tile = jnp.where(lane == k, ghost, tile)
    ghosts[...] = tile
    before_diag, second_diag, before_coupling, second_coupling = (own[10 + k] for k in range(4))
    last_turned, third_turned = own[14], own[15]
    prolongs = [own[16 + k] for k in range(6)]
    added = (
        to_row(before_coupling, before_new),
        to_row(before_diag, before_new) + to_row(last_coupling, last_new),
        to_row(last_diag, last_new) + to_row(last_turned, before_new)
        + to_row(right_coupling, right_twice),
        to_row(first_diag, first_new) + to_row(second_coupling, second_new)
        + to_row(first_turned, left_twice),
        to_row(second_diag, second_new) + to_row(second_turned, first_new),
        to_row(third_turned, second_new),
    )
    pieces = [to_row(block, column(row)) for block, row in zip(prolongs, added)]
    order = (half + 9, half + 8, half + 7, 7, 8, 9)
    names = [rows[k : k + 1] for k in order]
    blank = jnp.zeros((ROWS - 6, size), F32)
    pieces = jnp.concatenate(pieces + [blank], axis=0)
    names = jnp.concatenate(names + [blank], axis=0)[:, 0:1]
    rows_out = group_count // 2
    start = (lax.axis_index("grp") * group_count).astype(F32)
    row = lax.broadcasted_iota(jnp.int32, (ROWS, 2 * rows_out), 1)
    half_row = lax.rem(row, rows_out)
    named = (half_row // ROWS) * (2 * ROWS) + lax.rem(row, ROWS) + (row // rows_out) * ROWS
    mine = jnp.where(names - start == named.astype(F32), 1.0, 0.0)
    both = product(mine, pieces, ((0,), (0,)))
    both = jnp.concatenate([both[:rows_out], both[rows_out:]], axis=1)
    partial[...] = trial_partial[...] - both


def chosen(aggregate, group_count, half):
    rows = group_count // 2
    local_index = jnp.broadcast_to(lax.rem(aggregate[...], group_count), (rows, aggregate.shape[1]))
    row = lax.broadcasted_iota(jnp.int32, local_index.shape, 0)
    named = (row // ROWS) * (2 * ROWS) + lax.rem(row, ROWS) + half * ROWS
    return jnp.where(local_index == named, 1.0, 0.0).astype(F32)


def coarse_kernel(shares, coarse_inverse, out):
    size = coarse_inverse.shape[0]
    rows = shares.shape[0] // ROWS
    share = shares[0:ROWS]
    for row in range(1, rows):
        share = share + shares[row * ROWS : (row + 1) * ROWS]
    share = jnp.concatenate([share[:, :size], share[:, size:]], axis=0)
    lane = lanes(share)
    value = jnp.zeros_like(share)
    for i in range(size):
        total = jnp.sum(coarse_inverse[i].astype(F32) * share, axis=1, keepdims=True)
        value = jnp.where(lane == i, total, value)
    value = jnp.concatenate([value[:ROWS], value[ROWS:]], axis=1)
    for row in range(out.shape[0] // ROWS):
        out[row * ROWS : (row + 1) * ROWS] = value


def third_kernel(
    group_count, rhs, twice, values, diag, inverse, coupling, own, near, far, ghosts,
    prolong, aggregate, solution_out, residual, start, once, work,
):
    size, count = rhs.shape
    every = values.shape[0]
    in_group = group_count // 2
    group = pl.ds(pl.multiple_of(lax.axis_index("grp") * in_group, ROWS), in_group)
    mine = three(values[group, :])
    picked = [chosen(aggregate, group_count, half) for half in (0, 1)]
    picked = jnp.concatenate(picked, axis=1).astype(BF16)
    spread = jnp.zeros((size, count), F32)
    for part in mine:
        both = lax.dot_general(part, picked, (((0,), (0,)), ((), ())), preferred_element_type=F32)
        spread = spread + (both[:size, :count] + both[size:, count:])
    apply_blocks(prolong, spread, twice, start)

    sides, (left, right) = beyond_ends(even_device(), near, far, size)
    (left_blocks, left_pair), (right_blocks, right_pair) = sides
    column = columns_from(size)
    lane = lax.broadcasted_iota(jnp.int32, (size, count), 1)
    half = EDGE_ROWS
    blank = jnp.zeros((2, size), F32)
    names = jnp.concatenate([left[half + 7 : half + 10], right[7:10], blank], axis=0)[:, 0:1]
    source = lax.broadcasted_iota(jnp.int32, (ROWS, every), 1)
    first_name = (source // ROWS) * (2 * ROWS) + lax.rem(source, ROWS)
    everything = three(values[...])
    named = [
        jnp.where(names == (first_name + k * ROWS).astype(F32), 1.0, 0.0) for k in (0, 1)
    ]
    named = jnp.concatenate(named, axis=0).astype(BF16)
    coarse = jnp.zeros((ROWS, size), F32)
    for part in everything:
        both = jnp.dot(named, part, preferred_element_type=F32)
        coarse = coarse + (both[:ROWS, :size] + both[ROWS:, size:])

    (left_diag, left_inverse), (left_coupling, _) = left_blocks[:2]
    left_next_diag, left_next_inverse = left_blocks[4]
    left_pair, right_pair = jnp.transpose(left_pair), jnp.transpose(right_pair)
    left_turned, left_next_turned = left_pair[:size], left_pair[size:]
    (right_diag, right_inverse), (right_coupling, right_next_coupling) = right_blocks[:2]
    right_next_diag, right_next_inverse = right_blocks[4]
    right_turned, right_next_turned = right_pair[:size], right_pair[size:]
    right_third_coupling = right_blocks[3][1]
    first_coupling, first_turned = own[7], own[8]
    left_x, left_change, right_x, right_change = (ghosts[:, k : k + 1] for k in range(4))
    left_y, left_z = (column(left[half + k : half + k + 1]) for k in (3, 4))
    right_y, right_z = (column(right[k : k + 1]) for k in (3, 4))
    left_y = left_y - to_column(left_next_inverse, to_row(left_coupling, left_change))
    right_y = right_y - to_column(right_next_inverse, to_row(right_next_turned, right_change))
    prolongs = (left_blocks[2][0], left_blocks[2][1], left_blocks[3][0])
    prolongs = prolongs + (right_blocks[2][0], right_blocks[2][1], right_blocks[3][0])
    known = (left_x, left_y, left_z, right_x, right_y, right_z)
    left_x, left_y, left_z, right_x, right_y, right_z = (
        value + to_column(block, coarse[k : k + 1])
        for k, (value, block) in enumerate(zip(known, prolongs))
    )
    left_rhs, left_next_rhs = left[half + 5 : half + 6], left[half + 6 : half + 7]
    right_rhs, right_next_rhs = right[5:6], right[6:7]

    def added(left_column, right_column):
        return ends(
            lane,
            column(to_row(first_turned, left_column)),
            column(to_row(right_coupling, right_column)),
        )

    def nearest(vector, left_x, left_y, right_x, right_y):
        left_sum = to_row(left_diag, left_x) + to_row(left_turned, left_y)
        left_sum = left_sum + to_row(first_coupling, vector[:, 0:1])
        right_sum = to_row(right_diag, right_x) + to_row(right_turned, vector[:, count - 1 : count])
        right_sum = right_sum + to_row(right_next_coupling, right_y)
        return (
            left_x + to_column(left_inverse, left_rhs - left_sum),
            right_x + to_column(right_inverse, right_rhs - right_sum),
        )

    defect = wrong(rhs, start, diag, coupling, work) - added(left_x, right_x)
    left_once, right_once = nearest(start, left_x, left_y, right_x, right_y)
    left_sum = to_row(left_next_diag, left_y) + to_row(left_next_turned, left_z)
    left_sum = left_sum + to_row(left_coupling, left_x)
    left_y = left_y + to_column(left_next_inverse, left_next_rhs - left_sum)
    right_sum = to_row(right_next_diag, right_y) + to_row(right_next_turned, right_x)
    right_sum = right_sum + to_row(right_third_coupling, right_z)
    right_y = right_y + to_column(right_next_inverse, right_next_rhs - right_sum)
    apply_blocks(inverse, defect, start, once)
    defect = wrong(rhs, once, diag, coupling, work) - added(left_once, right_once)
    left_twice, right_twice = nearest(once, left_once, left_y, right_once, right_y)
    apply_blocks(inverse, defect, once, solution_out)
    defect = wrong(rhs, solution_out, diag, coupling, work)
    residual[...] = defect - added(left_twice, right_twice)


def call(kernel, outs, scratch, *operands, space=pltpu.VMEM, cost=None):
    inside = pl.BlockSpec(memory_space=pltpu.VMEM)
    if space == pltpu.HBM:
        operands = [pltpu.with_memory_space_constraint(x, space) for x in operands]
    single = not isinstance(outs, tuple)
    return pl.pallas_call(
        kernel,
        out_shape=outs,
        in_specs=[pl.BlockSpec(memory_space=space)] * len(operands),
        out_specs=inside if single else (inside,) * len(outs),
        scratch_shapes=scratch,
        cost_estimate=cost,
        compiler_params=pltpu.CompilerParams(vmem_limit_bytes=24 << 20),
    )(*operands)


def local(rhs, guess, diag_blocks, diag_inverse, coupling, prolong, coarse_inverse, aggregate):
    size, count = rhs.shape
    members = lax.axis_size("row")
    group_count = count * members // AGG
    assert coarse_inverse.shape[2] == 2 * ROWS and 2 * size == count and members % 2 == 0
    aggregate = aggregate.reshape(1, count)
    coarse_inverse = jnp.transpose(coarse_inverse, (0, 2, 1))

    def shape(*sizes, kind=F32):
        return jax.ShapeDtypeStruct(sizes, kind)

    tile = shape(size, count)
    blocks = shape(size, size, count)
    packed = shape(group_count // 2, count)
    edge = shape(TILES * size + 2 * EDGES, count, kind=BF16)
    line = shape(EDGES, size)
    plain = pltpu.VMEM((size, count), F32)
    half = pltpu.VMEM((size, size, count), BF16)
    loads = 2 + 3 * (size // LOAD) + 3
    (
        rhs, diag, inverse, coupling, prolong, coarse_inverse, aggregate,
        trial_twice, near, far, rows,
    ) = call(
        first_kernel,
        (
            tile, blocks, blocks, blocks,
            shape(size, size, count, kind=BF16),
            shape(*coarse_inverse.shape, kind=BF16),
            shape(1, count, kind=jnp.int32),
            tile, edge, edge, line,
        ),
        [
            plain, plain, half, half, half, plain,
            pltpu.SemaphoreType.DMA((loads,)),
        ],
        rhs, guess, diag_blocks, diag_inverse, coupling, prolong, coarse_inverse, aggregate,
        space=pltpu.HBM,
    )
    trial_partial, own = call(
        functools.partial(trial_kernel, group_count), (packed, shape(22, size, size)), [plain],
        rhs, trial_twice, diag, coupling, prolong, aggregate, near, far,
        cost=pl.CostEstimate(flops=8 * size**2 * count, bytes_accessed=8 * size**2 * count, transcendentals=0),
    )
    far = swap(far, 1)
    near = swap(near, 0)
    twice, partial, ghosts = call(
        functools.partial(second_kernel, group_count), (tile, packed, tile), [],
        trial_partial, trial_twice, own, rows, near, far,
    )
    shares = lax.all_to_all(partial, "row", 0, 0, tiled=True)
    corrected = call(
        coarse_kernel, shape(lax.axis_size(BOTH) * ROWS, count), [], shares, coarse_inverse
    )
    values = lax.all_to_all(corrected, BOTH, 0, 0, tiled=True)
    return call(
        functools.partial(third_kernel, group_count), (tile, tile), [plain, plain, plain],
        rhs, twice, values, diag, inverse, coupling, own, near, far, ghosts, prolong, aggregate,
    )


def solution(mesh):
    vector = P(None, BOTH)
    blocks = P(None, None, BOTH)
    return jax.shard_map(
        local,
        mesh=mesh,
        in_specs=(vector, vector, blocks, blocks, blocks, blocks, blocks, P(BOTH)),
        out_specs=(vector, vector),
        check_vma=False,
    )
```

```python
import functools

import jax
import jax.numpy as jnp
from jax import lax
from jax.experimental import pallas as pl
from jax.experimental.pallas import tpu as pltpu
from jax.sharding import PartitionSpec as P

AGG = 8
BOTH = ("grp", "row")
F32 = jnp.float32
BF16 = jnp.bfloat16
ROWS = 8
LOAD = 16
EDGES = 24
EDGE_ROWS = 10
TILES = 5


def swap(block, first):
    pairs = [(i, i + 1) for i in range(first, lax.axis_size(BOTH) - 1, 2)]
    return lax.ppermute(block, BOTH, pairs + [(j, i) for i, j in pairs])


def even_device():
    return lax.rem(lax.axis_index("row"), 2) == 0


def lanes(like):
    return lax.broadcasted_iota(jnp.int32, like.shape, 1)


def turn(tile, shift):
    return pltpu.roll(tile, shift % tile.shape[1], 1)


def three(tile):
    high = tile.astype(BF16)
    rest = tile - high.astype(F32)
    middle = rest.astype(BF16)
    return high, middle, (rest - middle.astype(F32)).astype(BF16)


def product(left, right, dims):
    left = left.astype(BF16)
    parts = [
        lax.dot_general(left, part, (dims, ((), ())), preferred_element_type=F32)
        for part in three(right)
    ]
    return parts[0] + (parts[1] + parts[2])


def stack(rows):
    return jnp.concatenate([part.astype(F32) for part in three(rows)], axis=0)


def to_column(block, row):
    return jnp.sum(block * row, axis=1, keepdims=True)


def to_row(block, column):
    return jnp.sum(block * column, axis=0, keepdims=True)


def operate(diag, coupling, vector_ref, out_ref, lower):
    vector = vector_ref[...]

    def step(chunk, upward):
        start = pl.multiple_of(chunk * ROWS, ROWS)
        own = vector_ref[pl.ds(start, ROWS), :]
        sums = []
        for s in range(ROWS):
            pair = coupling[start + s]
            terms = diag[start + s] * vector + pair * lower
            sums.append(jnp.sum(terms, axis=0, keepdims=True))
            upward = upward + pair * own[s : s + 1, :]
        out_ref[pl.ds(start, ROWS), :] = jnp.concatenate(sums, axis=0)
        return upward

    return loop(vector.shape[0] // ROWS, step, jnp.zeros_like(vector))


def apply_blocks(blocks, vector, base_ref, out_ref):
    def step(chunk, carry):
        start = pl.multiple_of(chunk * ROWS, ROWS)
        sums = [
            jnp.sum(blocks[start + s].astype(F32) * vector, axis=0, keepdims=True)
            for s in range(ROWS)
        ]
        base = base_ref[pl.ds(start, ROWS), :]
        out_ref[pl.ds(start, ROWS), :] = base + jnp.concatenate(sums, axis=0)
        return carry

    loop(vector.shape[0] // ROWS, step, 0)


def apply_transposed(blocks, vector_ref):
    def step(chunk, total):
        start = pl.multiple_of(chunk * ROWS, ROWS)
        own = vector_ref[pl.ds(start, ROWS), :]
        for s in range(ROWS):
            total = total + blocks[start + s].astype(F32) * own[s : s + 1, :]
        return total

    zero = jnp.zeros(vector_ref.shape, F32)
    return loop(vector_ref.shape[0] // ROWS, step, zero)


def loop(count, step, carry):
    return lax.fori_loop(0, count, step, carry, unroll=True)


def place(tile, block, row):
    shape = (tile.shape[0] // ROWS, ROWS, tile.shape[1])
    lane = lax.broadcasted_iota(jnp.int32, (1,) + shape[1:], 2)
    mine = lax.shift_right_logical(lane, 3) == row
    turned = pltpu.roll(block, 8 * row + 3, 1).reshape(shape)
    return jnp.where(mine, turned, tile.reshape(shape)).reshape(tile.shape)


def picker(size, width, ends):
    shape = (size * len(ends), width)
    row = lax.broadcasted_iota(jnp.int32, shape, 0)
    lane = lax.broadcasted_iota(jnp.int32, shape, 1)
    target = 8 * lax.rem(row, size) + row // size + ends[0]
    return jnp.where(lane == target, 1.0, 0.0).astype(BF16)


def end_blocks(tiles, ends):
    packed = jnp.concatenate(tiles, axis=1).astype(BF16)
    size = packed.shape[0]
    blocks = lax.dot_general(
        picker(size, packed.shape[1], ends), packed, (((1,), (1,)), ((), ())),
        preferred_element_type=F32,
    )
    return [blocks[k * size : (k + 1) * size] for k in range(len(ends))]


def end_blocks_turned(tiles, ends):
    packed = jnp.concatenate(tiles, axis=1).astype(BF16)
    return lax.dot_general(
        packed, picker(packed.shape[0], packed.shape[1], ends), (((1,), (1,)), ((), ())),
        preferred_element_type=F32,
    )


def edge_rows(firsts, lasts, count):
    lane = lanes(firsts[0][0])
    tile = jnp.zeros(lane.shape, F32)
    for k, (column, where) in enumerate(firsts + lasts):
        tile = jnp.where(lane == k, turn(column, k - where), tile)
    return jnp.transpose(tile)[:EDGES]


def wrong(rhs_ref, vector_ref, diag, coupling, work):
    vector = vector_ref[...]
    lane = lanes(vector)
    lower = jnp.where(lane == 0, 0.0, turn(vector, 1))
    upward = operate(diag, coupling, vector_ref, work, lower)
    upper = jnp.where(lane == vector.shape[1] - 1, 0.0, turn(upward, -1))
    return rhs_ref[...] - (work[...] + upper)


def first_kernel(
    rhs_in, guess_in, diag_in, inverse_in, coupling_in, prolong_in, coarse_in, aggregate_in,
    rhs, diag, inverse, coupling, prolong, coarse, aggregate,
    twice, near, far, rows_out,
    trial, guess, diag_half, inverse_half, coupling_half, work, sems,
):
    size, count = guess.shape
    parts = diag_half.shape[0] // LOAD
    copies = [
        pltpu.make_async_copy(guess_in, guess, sems.at[0]),
        pltpu.make_async_copy(rhs_in, rhs, sems.at[1]),
    ]
    for p in range(parts):
        rows = pl.ds(p * LOAD, LOAD)
        for source, target in ((coupling_in, coupling_half), (diag_in, diag_half)):
            copies.append(
                pltpu.make_async_copy(source.at[rows], target.at[rows], sems.at[len(copies)])
            )
    for p in range(parts):
        rows = pl.ds(p * LOAD, LOAD)
        copies.append(
            pltpu.make_async_copy(inverse_in.at[rows], inverse_half.at[rows], sems.at[len(copies)])
        )
    for source, target in ((prolong_in, prolong), (coarse_in, coarse), (aggregate_in, aggregate)):
        copies.append(pltpu.make_async_copy(source, target, sems.at[len(copies)]))
    for copy in copies:
        copy.start()
    copies[0].wait()

    start = guess[...]
    lane = lanes(start)
    lower = jnp.where(lane == 0, 0.0, turn(start, 1))
    upward = jnp.zeros_like(start)
    diag_ends = [jnp.zeros_like(start) for _ in range(4)]
    inverse_ends, coupling_ends, prolong_ends = list(diag_ends), list(diag_ends), list(diag_ends)
    for chunk in range(size // ROWS):
        if chunk * ROWS % LOAD == 0:
            at = 2 + 2 * (chunk * ROWS // LOAD)
            copies[at].wait()
            copies[at + 1].wait()
        sums = []
        for i in range(chunk * ROWS, chunk * ROWS + ROWS):
            pair = coupling_half[i].astype(F32)
            block = diag_half[i].astype(F32)
            coupling[i] = pair
            diag[i] = block
            t, row = divmod(i, size // 4)
            diag_ends[t] = place(diag_ends[t], block, row)
            sums.append(jnp.sum(block * start + pair * lower, axis=0, keepdims=True))
            upward = upward + pair * guess[i : i + 1, :]
        work[pl.ds(chunk * ROWS, ROWS), :] = jnp.concatenate(sums, axis=0)
    upper = jnp.where(lane == count - 1, 0.0, turn(upward, -1))
    copies[1].wait()
    defect = rhs[...] - (work[...] + upper)

    for chunk in range(size // ROWS):
        if chunk * ROWS % LOAD == 0:
            copies[2 + 2 * parts + chunk * ROWS // LOAD].wait()
        rows = pl.ds(chunk * ROWS, ROWS)
        sums = []
        for i in range(chunk * ROWS, chunk * ROWS + ROWS):
            block = inverse_half[i].astype(F32)
            inverse[i] = block
            t, row = divmod(i, size // 4)
            inverse_ends[t] = place(inverse_ends[t], block, row)
            sums.append(jnp.sum(block * defect, axis=0, keepdims=True))
        trial[rows, :] = guess[rows, :] + jnp.concatenate(sums, axis=0)

    second = trial[...]
    lower = jnp.where(lane == 0, 0.0, turn(second, 1))
    upward = jnp.zeros_like(start)
    for chunk in range(size // ROWS):
        sums = []
        for i in range(chunk * ROWS, chunk * ROWS + ROWS):
            pair = coupling[i]
            t, row = divmod(i, size // 4)
            coupling_ends[t] = place(coupling_ends[t], pair, row)
            sums.append(jnp.sum(diag[i] * second + pair * lower, axis=0, keepdims=True))
            upward = upward + pair * trial[i : i + 1, :]
        work[pl.ds(chunk * ROWS, ROWS), :] = jnp.concatenate(sums, axis=0)
    upper = jnp.where(lane == count - 1, 0.0, turn(upward, -1))
    defect = rhs[...] - (work[...] + upper)

    for copy in copies[-3:]:
        copy.wait()
    for chunk in range(size // ROWS):
        rows = pl.ds(chunk * ROWS, ROWS)
        sums = []
        for i in range(chunk * ROWS, chunk * ROWS + ROWS):
            t, row = divmod(i, size // 4)
            prolong_ends[t] = place(prolong_ends[t], prolong[i].astype(F32), row)
            sums.append(jnp.sum(inverse[i] * defect, axis=0, keepdims=True))
        twice[rows, :] = trial[rows, :] + jnp.concatenate(sums, axis=0)

    last = count - 1
    named = jnp.broadcast_to(aggregate[...].astype(F32), (size, count))
    after = twice[...]
    both = [(start, 0), (second, 0), (defect, 0), (after, 1), (after, 2), (rhs[...], 0), (rhs[...], 1)]
    both = both + [(named, 0), (named, 1), (named, 2)]
    rows = edge_rows(both, [(column, last - k) for column, k in both], count)
    rows_out[...] = rows
    diag_turned = end_blocks_turned(diag_ends, (1, 2, 3, 4))
    inverses = end_blocks(inverse_ends, (1, 2, 3, 4))
    couplings = end_blocks(coupling_ends, (1, 2, 3, 4, 5))
    prolongs = end_blocks(prolong_ends, (0, 1, 2, 3, 4, 5))
    turned_diag = [diag_turned[:, k * size : (k + 1) * size] for k in range(4)]
    lasts = (
        (turned_diag[1], inverses[1]), (couplings[1], couplings[0]), (prolongs[2], prolongs[1]),
        (prolongs[0], couplings[4]), (turned_diag[0], inverses[0]),
    )
    firsts = (
        (turned_diag[2], inverses[2]), (couplings[2], couplings[3]), (prolongs[3], prolongs[4]),
        (prolongs[5], couplings[4]), (turned_diag[3], inverses[3]),
    )
    even = even_device()
    for k, (one, other) in enumerate(zip(lasts, firsts)):
        one, other = jnp.concatenate(one, axis=1), jnp.concatenate(other, axis=1)
        at = slice(k * size, (k + 1) * size)
        near[at] = jnp.where(even, one, other).astype(BF16)
        far[at] = jnp.where(even, other, one).astype(BF16)
    high, middle, low = (part.astype(F32) for part in three(rows))
    shares = jnp.concatenate(
        [jnp.concatenate([high, low], axis=1), jnp.concatenate([middle, low], axis=1)], axis=0
    ).astype(BF16)
    near[TILES * size :] = shares
    far[TILES * size :] = shares

def beyond_ends(even, near, far, size):
    near, far = near[...].astype(F32), far[...].astype(F32)
    sides, rows = [], []
    for side in (jnp.where(even, far, near), jnp.where(even, near, far)):
        pairs = [side[k * size : (k + 1) * size] for k in range(TILES)]
        sides.append(([(pair[:, :size], pair[:, size:]) for pair in pairs], pairs[1]))
        tail = side[TILES * size :]
        rows.append(tail[:EDGES, :size] + tail[EDGES:, :size] + tail[:EDGES, size:])
    return sides, rows


def columns_from(size):
    shape = (size, size)
    unit = lax.broadcasted_iota(jnp.int32, shape, 0) == lax.broadcasted_iota(jnp.int32, shape, 1)
    return lambda row: jnp.sum(jnp.where(unit, row, 0.0), axis=1, keepdims=True)


def ends(lane, first, last):
    return jnp.where(lane == 0, first, jnp.where(lane == lane.shape[1] - 1, last, 0.0))


def trial_kernel(
    group_count, rhs, trial_twice, diag, coupling, prolong, aggregate, near, far,
    partial, own, work,
):
    work[...] = wrong(rhs, trial_twice, diag, coupling, work)
    pieces = apply_transposed(prolong, work)
    picked = [chosen(aggregate, group_count, half) for half in (0, 1)]
    both = product(jnp.concatenate(picked, axis=0), pieces, ((1,), (1,)))
    rows_out = group_count // 2
    partial[...] = jnp.concatenate([both[:rows_out], both[rows_out:]], axis=1)

    size = rhs.shape[0]
    even = even_device()
    near, far = near[: TILES * size].astype(F32), far[: TILES * size].astype(F32)
    lasts, firsts = (
        [side[k * size : (k + 1) * size] for k in range(TILES)]
        for side in (jnp.where(even, near, far), jnp.where(even, far, near))
    )
    turned_last, turned_first = jnp.transpose(lasts[1]), jnp.transpose(firsts[1])
    turned_third = jnp.transpose(firsts[3])[size:]
    lasts = [(tile[:, :size], tile[:, size:]) for tile in lasts]
    firsts = [(tile[:, :size], tile[:, size:]) for tile in firsts]
    blocks = (
        lasts[0][0], firsts[0][0], lasts[4][1], lasts[0][1], firsts[0][1], firsts[4][1],
        lasts[1][0], firsts[1][0], turned_first[:size], turned_first[size:],
        lasts[4][0], firsts[4][0], lasts[1][1], firsts[1][1], turned_last[:size], turned_third,
        lasts[3][0], lasts[2][1], lasts[2][0], firsts[2][0], firsts[2][1], firsts[3][0],
    )
    for k, block in enumerate(blocks):
        own[k] = block


def second_kernel(
    group_count, trial_partial, trial_twice, own, rows, far, near, twice, partial, ghosts,
):
    size, count = trial_twice.shape
    sides, (left, right) = beyond_ends(even_device(), near, far, size)
    (left_blocks, _), (right_blocks, right_pair) = sides
    column = columns_from(size)
    half = EDGE_ROWS
    left_diag, left_inverse = left_blocks[0]
    (right_diag, right_inverse), (right_coupling, _) = right_blocks[:2]
    right_turned = jnp.transpose(right_pair)[:size]
    last_diag, first_diag = own[0], own[1]
    before_inverse, last_inverse, first_inverse, second_inverse = (own[2 + k] for k in range(4))
    last_coupling, first_coupling, first_turned, second_turned = (own[6 + k] for k in range(4))
    first_start, first_trial, last_start, last_trial = (
        column(rows[k : k + 1]) for k in (0, 1, half, half + 1)
    )
    left_start, left_trial = (column(left[half + k : half + k + 1]) for k in (0, 1))
    right_start, right_trial = (column(right[k : k + 1]) for k in (0, 1))
    left_wrong, right_wrong = left[half + 2 : half + 3], right[2:3]

    first_change = -to_column(first_inverse, to_row(first_turned, left_start))
    last_change = -to_column(last_inverse, to_row(right_coupling, right_start))
    left_change = -to_column(left_inverse, to_row(first_coupling, first_start))
    right_change = -to_column(right_inverse, to_row(right_turned, last_start))
    left_once, right_once = left_trial + left_change, right_trial + right_change
    first_added = to_row(first_diag, first_change) + to_row(first_turned, left_once)
    last_added = to_row(last_diag, last_change) + to_row(right_coupling, right_once)
    left_added = to_row(left_diag, left_change)
    left_added = left_added + to_row(first_coupling, first_trial + first_change)
    right_added = to_row(right_diag, right_change)
    right_added = right_added + to_row(right_turned, last_trial + last_change)
    left_twice = left_once + to_column(left_inverse, left_wrong - left_added)
    right_twice = right_once + to_column(right_inverse, right_wrong - right_added)
    second_added = to_row(second_turned, first_change)
    before_added = to_row(last_coupling, last_change)
    lane = lax.broadcasted_iota(jnp.int32, (size, count), 1)
    first_new = first_change - to_column(first_inverse, first_added)
    second_new = -to_column(second_inverse, second_added)
    before_new = -to_column(before_inverse, before_added)
    last_new = last_change - to_column(last_inverse, last_added)
    change = ends(lane, first_new, last_new)
    change = jnp.where(lane == 1, second_new, change)
    change = jnp.where(lane == count - 2, before_new, change)
    twice[...] = trial_twice[...] + change
    tile = jnp.zeros((size, count), F32)
    for k, ghost in enumerate((left_twice, left_change, right_twice, right_change)):
        tile = jnp.where(lane == k, ghost, tile)
    ghosts[...] = tile
    before_diag, second_diag, before_coupling, second_coupling = (own[10 + k] for k in range(4))
    last_turned, third_turned = own[14], own[15]
    prolongs = [own[16 + k] for k in range(6)]
    added = (
        to_row(before_coupling, before_new),
        to_row(before_diag, before_new) + to_row(last_coupling, last_new),
        to_row(last_diag, last_new) + to_row(last_turned, before_new)
        + to_row(right_coupling, right_twice),
        to_row(first_diag, first_new) + to_row(second_coupling, second_new)
        + to_row(first_turned, left_twice),
        to_row(second_diag, second_new) + to_row(second_turned, first_new),
        to_row(third_turned, second_new),
    )
    pieces = [to_row(block, column(row)) for block, row in zip(prolongs, added)]
    order = (half + 9, half + 8, half + 7, 7, 8, 9)
    names = [rows[k : k + 1] for k in order]
    blank = jnp.zeros((ROWS - 6, size), F32)
    pieces = jnp.concatenate(pieces + [blank], axis=0)
    names = jnp.concatenate(names + [blank], axis=0)[:, 0:1]
    rows_out = group_count // 2
    start = (lax.axis_index("grp") * group_count).astype(F32)
    row = lax.broadcasted_iota(jnp.int32, (ROWS, 2 * rows_out), 1)
    half_row = lax.rem(row, rows_out)
    named = (half_row // ROWS) * (2 * ROWS) + lax.rem(row, ROWS) + (row // rows_out) * ROWS
    mine = jnp.where(names - start == named.astype(F32), 1.0, 0.0)
    both = product(mine, pieces, ((0,), (0,)))
    both = jnp.concatenate([both[:rows_out], both[rows_out:]], axis=1)
    partial[...] = trial_partial[...] - both


def chosen(aggregate, group_count, half):
    rows = group_count // 2
    local_index = jnp.broadcast_to(lax.rem(aggregate[...], group_count), (rows, aggregate.shape[1]))
    row = lax.broadcasted_iota(jnp.int32, local_index.shape, 0)
    named = (row // ROWS) * (2 * ROWS) + lax.rem(row, ROWS) + half * ROWS
    return jnp.where(local_index == named, 1.0, 0.0).astype(F32)


def coarse_kernel(shares, coarse_inverse, out):
    size = coarse_inverse.shape[0]
    rows = shares.shape[0] // ROWS
    share = shares[0:ROWS]
    for row in range(1, rows):
        share = share + shares[row * ROWS : (row + 1) * ROWS]
    share = jnp.concatenate([share[:, :size], share[:, size:]], axis=0)
    lane = lanes(share)
    value = jnp.zeros_like(share)
    for i in range(size):
        total = jnp.sum(coarse_inverse[i].astype(F32) * share, axis=1, keepdims=True)
        value = jnp.where(lane == i, total, value)
    value = jnp.concatenate([value[:ROWS], value[ROWS:]], axis=1)
    for row in range(out.shape[0] // ROWS):
        out[row * ROWS : (row + 1) * ROWS] = value


def third_kernel(
    group_count, rhs, twice, values, diag, inverse, coupling, own, near, far, ghosts,
    prolong, aggregate, solution_out, residual, start, once, work,
):
    size, count = rhs.shape
    every = values.shape[0]
    in_group = group_count // 2
    group = pl.ds(pl.multiple_of(lax.axis_index("grp") * in_group, ROWS), in_group)
    mine = three(values[group, :])
    picked = [chosen(aggregate, group_count, half) for half in (0, 1)]
    picked = jnp.concatenate(picked, axis=1).astype(BF16)
    spread = jnp.zeros((size, count), F32)
    for part in mine:
        both = lax.dot_general(part, picked, (((0,), (0,)), ((), ())), preferred_element_type=F32)
        spread = spread + (both[:size, :count] + both[size:, count:])
    apply_blocks(prolong, spread, twice, start)

    sides, (left, right) = beyond_ends(even_device(), near, far, size)
    (left_blocks, left_pair), (right_blocks, right_pair) = sides
    column = columns_from(size)
    lane = lax.broadcasted_iota(jnp.int32, (size, count), 1)
    half = EDGE_ROWS
    blank = jnp.zeros((2, size), F32)
    names = jnp.concatenate([left[half + 7 : half + 10], right[7:10], blank], axis=0)[:, 0:1]
    source = lax.broadcasted_iota(jnp.int32, (ROWS, every), 1)
    first_name = (source // ROWS) * (2 * ROWS) + lax.rem(source, ROWS)
    everything = three(values[...])
    named = [
        jnp.where(names == (first_name + k * ROWS).astype(F32), 1.0, 0.0) for k in (0, 1)
    ]
    named = jnp.concatenate(named, axis=0).astype(BF16)
    coarse = jnp.zeros((ROWS, size), F32)
    for part in everything:
        both = jnp.dot(named, part, preferred_element_type=F32)
        coarse = coarse + (both[:ROWS, :size] + both[ROWS:, size:])

    (left_diag, left_inverse), (left_coupling, _) = left_blocks[:2]
    left_next_diag, left_next_inverse = left_blocks[4]
    left_pair, right_pair = jnp.transpose(left_pair), jnp.transpose(right_pair)
    left_turned, left_next_turned = left_pair[:size], left_pair[size:]
    (right_diag, right_inverse), (right_coupling, right_next_coupling) = right_blocks[:2]
    right_next_diag, right_next_inverse = right_blocks[4]
    right_turned, right_next_turned = right_pair[:size], right_pair[size:]
    right_third_coupling = right_blocks[3][1]
    first_coupling, first_turned = own[7], own[8]
    left_x, left_change, right_x, right_change = (ghosts[:, k : k + 1] for k in range(4))
    left_y, left_z = (column(left[half + k : half + k + 1]) for k in (3, 4))
    right_y, right_z = (column(right[k : k + 1]) for k in (3, 4))
    left_y = left_y - to_column(left_next_inverse, to_row(left_coupling, left_change))
    right_y = right_y - to_column(right_next_inverse, to_row(right_next_turned, right_change))
    prolongs = (left_blocks[2][0], left_blocks[2][1], left_blocks[3][0])
    prolongs = prolongs + (right_blocks[2][0], right_blocks[2][1], right_blocks[3][0])
    known = (left_x, left_y, left_z, right_x, right_y, right_z)
    left_x, left_y, left_z, right_x, right_y, right_z = (
        value + to_column(block, coarse[k : k + 1])
        for k, (value, block) in enumerate(zip(known, prolongs))
    )
    left_rhs, left_next_rhs = left[half + 5 : half + 6], left[half + 6 : half + 7]
    right_rhs, right_next_rhs = right[5:6], right[6:7]

    def added(left_column, right_column):
        return ends(
            lane,
            column(to_row(first_turned, left_column)),
            column(to_row(right_coupling, right_column)),
        )

    def nearest(vector, left_x, left_y, right_x, right_y):
        left_sum = to_row(left_diag, left_x) + to_row(left_turned, left_y)
        left_sum = left_sum + to_row(first_coupling, vector[:, 0:1])
        right_sum = to_row(right_diag, right_x) + to_row(right_turned, vector[:, count - 1 : count])
        right_sum = right_sum + to_row(right_next_coupling, right_y)
        return (
            left_x + to_column(left_inverse, left_rhs - left_sum),
            right_x + to_column(right_inverse, right_rhs - right_sum),
        )

    defect = wrong(rhs, start, diag, coupling, work) - added(left_x, right_x)
    left_once, right_once = nearest(start, left_x, left_y, right_x, right_y)
    left_sum = to_row(left_next_diag, left_y) + to_row(left_next_turned, left_z)
    left_sum = left_sum + to_row(left_coupling, left_x)
    left_y = left_y + to_column(left_next_inverse, left_next_rhs - left_sum)
    right_sum = to_row(right_next_diag, right_y) + to_row(right_next_turned, right_x)
    right_sum = right_sum + to_row(right_third_coupling, right_z)
    right_y = right_y + to_column(right_next_inverse, right_next_rhs - right_sum)
    apply_blocks(inverse, defect, start, once)
    defect = wrong(rhs, once, diag, coupling, work) - added(left_once, right_once)
    left_twice, right_twice = nearest(once, left_once, left_y, right_once, right_y)
    apply_blocks(inverse, defect, once, solution_out)
    defect = wrong(rhs, solution_out, diag, coupling, work)
    residual[...] = defect - added(left_twice, right_twice)


def call(kernel, outs, scratch, *operands, space=pltpu.VMEM, cost=None):
    inside = pl.BlockSpec(memory_space=pltpu.VMEM)
    if space == pltpu.HBM:
        operands = [pltpu.with_memory_space_constraint(x, space) for x in operands]
    single = not isinstance(outs, tuple)
    return pl.pallas_call(
        kernel,
        out_shape=outs,
        in_specs=[pl.BlockSpec(memory_space=space)] * len(operands),
        out_specs=inside if single else (inside,) * len(outs),
        scratch_shapes=scratch,
        cost_estimate=cost,
        compiler_params=pltpu.CompilerParams(vmem_limit_bytes=24 << 20),
    )(*operands)


def local(rhs, guess, diag_blocks, diag_inverse, coupling, prolong, coarse_inverse, aggregate):
    size, count = rhs.shape
    members = lax.axis_size("row")
    group_count = count * members // AGG
    assert coarse_inverse.shape[2] == 2 * ROWS and 2 * size == count and members % 2 == 0
    aggregate = aggregate.reshape(1, count)
    coarse_inverse = jnp.transpose(coarse_inverse, (0, 2, 1))

    def shape(*sizes, kind=F32):
        return jax.ShapeDtypeStruct(sizes, kind)

    tile = shape(size, count)
    blocks = shape(size, size, count)
    packed = shape(group_count // 2, count)
    edge = shape(TILES * size + 2 * EDGES, count, kind=BF16)
    line = shape(EDGES, size)
    plain = pltpu.VMEM((size, count), F32)
    half = pltpu.VMEM((size, size, count), BF16)
    loads = 2 + 3 * (size // LOAD) + 3
    (
        rhs, diag, inverse, coupling, prolong, coarse_inverse, aggregate,
        trial_twice, near, far, rows,
    ) = call(
        first_kernel,
        (
            tile, blocks, blocks, blocks,
            shape(size, size, count, kind=BF16),
            shape(*coarse_inverse.shape, kind=BF16),
            shape(1, count, kind=jnp.int32),
            tile, edge, edge, line,
        ),
        [
            plain, plain, half, half, half, plain,
            pltpu.SemaphoreType.DMA((loads,)),
        ],
        rhs, guess, diag_blocks, diag_inverse, coupling, prolong, coarse_inverse, aggregate,
        space=pltpu.HBM,
    )
    trial_partial, own = call(
        functools.partial(trial_kernel, group_count), (packed, shape(22, size, size)), [plain],
        rhs, trial_twice, diag, coupling, prolong, aggregate, near, far,
        cost=pl.CostEstimate(flops=8 * size**2 * count, bytes_accessed=8 * size**2 * count, transcendentals=0),
    )
    far = swap(far, 1)
    near = swap(near, 0)
    twice, partial, ghosts = call(
        functools.partial(second_kernel, group_count), (tile, packed, tile), [],
        trial_partial, trial_twice, own, rows, far, near,
    )
    shares = lax.all_to_all(partial, "row", 0, 0, tiled=True)
    corrected = call(
        coarse_kernel, shape(lax.axis_size(BOTH) * ROWS, count), [], shares, coarse_inverse
    )
    values = lax.all_to_all(corrected, BOTH, 0, 0, tiled=True)
    return call(
        functools.partial(third_kernel, group_count), (tile, tile), [plain, plain, plain],
        rhs, twice, values, diag, inverse, coupling, own, near, far, ghosts, prolong, aggregate,
    )


def solution(mesh):
    vector = P(None, BOTH)
    blocks = P(None, None, BOTH)
    return jax.shard_map(
        local,
        mesh=mesh,
        in_specs=(vector, vector, blocks, blocks, blocks, blocks, blocks, P(BOTH)),
        out_specs=(vector, vector),
        check_vma=False,
    )
```

```python
import functools

import jax
import jax.numpy as jnp
from jax import lax
from jax.experimental import pallas as pl
from jax.experimental.pallas import tpu as pltpu
from jax.sharding import PartitionSpec as P

AGG = 8
BOTH = ("grp", "row")
F32 = jnp.float32
BF16 = jnp.bfloat16
ROWS = 8
LOAD = 16
EDGES = 24
EDGE_ROWS = 10
TILES = 5


def swap(block, first):
    pairs = [(i, i + 1) for i in range(first, lax.axis_size(BOTH) - 1, 2)]
    return lax.ppermute(block, BOTH, pairs + [(j, i) for i, j in pairs])


def even_device():
    return lax.rem(lax.axis_index("row"), 2) == 0


def lanes(like):
    return lax.broadcasted_iota(jnp.int32, like.shape, 1)


def turn(tile, shift):
    return pltpu.roll(tile, shift % tile.shape[1], 1)


def three(tile):
    high = tile.astype(BF16)
    rest = tile - high.astype(F32)
    middle = rest.astype(BF16)
    return high, middle, (rest - middle.astype(F32)).astype(BF16)


def product(left, right, dims):
    left = left.astype(BF16)
    parts = [
        lax.dot_general(left, part, (dims, ((), ())), preferred_element_type=F32)
        for part in three(right)
    ]
    return parts[0] + (parts[1] + parts[2])


def stack(rows):
    return jnp.concatenate([part.astype(F32) for part in three(rows)], axis=0)


def to_column(block, row):
    return jnp.sum(block * row, axis=1, keepdims=True)


def to_row(block, column):
    return jnp.sum(block * column, axis=0, keepdims=True)


def operate(diag, coupling, vector_ref, out_ref, lower):
    vector = vector_ref[...]

    def step(chunk, upward):
        start = pl.multiple_of(chunk * ROWS, ROWS)
        own = vector_ref[pl.ds(start, ROWS), :]
        sums = []
        for s in range(ROWS):
            pair = coupling[start + s]
            terms = diag[start + s] * vector + pair * lower
            sums.append(jnp.sum(terms, axis=0, keepdims=True))
            upward = upward + pair * own[s : s + 1, :]
        out_ref[pl.ds(start, ROWS), :] = jnp.concatenate(sums, axis=0)
        return upward

    return loop(vector.shape[0] // ROWS, step, jnp.zeros_like(vector))


def apply_blocks(blocks, vector, base_ref, out_ref):
    def step(chunk, carry):
        start = pl.multiple_of(chunk * ROWS, ROWS)
        sums = [
            jnp.sum(blocks[start + s].astype(F32) * vector, axis=0, keepdims=True)
            for s in range(ROWS)
        ]
        base = base_ref[pl.ds(start, ROWS), :]
        out_ref[pl.ds(start, ROWS), :] = base + jnp.concatenate(sums, axis=0)
        return carry

    loop(vector.shape[0] // ROWS, step, 0)


def apply_transposed(blocks, vector_ref):
    def step(chunk, total):
        start = pl.multiple_of(chunk * ROWS, ROWS)
        own = vector_ref[pl.ds(start, ROWS), :]
        for s in range(ROWS):
            total = total + blocks[start + s].astype(F32) * own[s : s + 1, :]
        return total

    zero = jnp.zeros(vector_ref.shape, F32)
    return loop(vector_ref.shape[0] // ROWS, step, zero)


def loop(count, step, carry):
    return lax.fori_loop(0, count, step, carry, unroll=True)


def place(tile, block, row):
    shape = (tile.shape[0] // ROWS, ROWS, tile.shape[1])
    lane = lax.broadcasted_iota(jnp.int32, (1,) + shape[1:], 2)
    mine = lax.shift_right_logical(lane, 3) == row
    turned = pltpu.roll(block, 8 * row + 4, 1).reshape(shape)
    return jnp.where(mine, turned, tile.reshape(shape)).reshape(tile.shape)


def picker(size, width, ends):
    shape = (size * len(ends), width)
    row = lax.broadcasted_iota(jnp.int32, shape, 0)
    lane = lax.broadcasted_iota(jnp.int32, shape, 1)
    target = 8 * lax.rem(row, size) + row // size + ends[0]
    return jnp.where(lane == target, 1.0, 0.0).astype(BF16)


def end_blocks(tiles, ends):
    packed = jnp.concatenate(tiles, axis=1).astype(BF16)
    size = packed.shape[0]
    blocks = lax.dot_general(
        picker(size, packed.shape[1], ends), packed, (((1,), (1,)), ((), ())),
        preferred_element_type=F32,
    )
    return [blocks[k * size : (k + 1) * size] for k in range(len(ends))]


def end_blocks_turned(tiles, ends):
    packed = jnp.concatenate(tiles, axis=1).astype(BF16)
    return lax.dot_general(
        packed, picker(packed.shape[0], packed.shape[1], ends), (((1,), (1,)), ((), ())),
        preferred_element_type=F32,
    )


def edge_rows(firsts, lasts, count):
    lane = lanes(firsts[0][0])
    tile = jnp.zeros(lane.shape, F32)
    for k, (column, where) in enumerate(firsts + lasts):
        tile = jnp.where(lane == k, turn(column, k - where), tile)
    return jnp.transpose(tile)[:EDGES]


def wrong(rhs_ref, vector_ref, diag, coupling, work):
    vector = vector_ref[...]
    lane = lanes(vector)
    lower = jnp.where(lane == 0, 0.0, turn(vector, 1))
    upward = operate(diag, coupling, vector_ref, work, lower)
    upper = jnp.where(lane == vector.shape[1] - 1, 0.0, turn(upward, -1))
    return rhs_ref[...] - (work[...] + upper)


def first_kernel(
    rhs_in, guess_in, diag_in, inverse_in, coupling_in, prolong_in, coarse_in, aggregate_in,
    rhs, diag, inverse, coupling, prolong, coarse, aggregate,
    trial, near, far, rows_out,
    guess, diag_half, inverse_half, coupling_half, work, sems,
):
    size, count = guess.shape
    parts = diag_half.shape[0] // LOAD
    copies = [
        pltpu.make_async_copy(guess_in, guess, sems.at[0]),
        pltpu.make_async_copy(rhs_in, rhs, sems.at[1]),
    ]
    for p in range(parts):
        rows = pl.ds(p * LOAD, LOAD)
        for source, target in ((coupling_in, coupling_half), (diag_in, diag_half)):
            copies.append(
                pltpu.make_async_copy(source.at[rows], target.at[rows], sems.at[len(copies)])
            )
    for p in range(parts):
        rows = pl.ds(p * LOAD, LOAD)
        copies.append(
            pltpu.make_async_copy(inverse_in.at[rows], inverse_half.at[rows], sems.at[len(copies)])
        )
    for source, target in ((prolong_in, prolong), (coarse_in, coarse), (aggregate_in, aggregate)):
        copies.append(pltpu.make_async_copy(source, target, sems.at[len(copies)]))
    for copy in copies:
        copy.start()
    copies[0].wait()

    start = guess[...]
    lane = lanes(start)
    lower = jnp.where(lane == 0, 0.0, turn(start, 1))
    upward = jnp.zeros_like(start)
    diag_ends = [jnp.zeros_like(start) for _ in range(4)]
    inverse_ends, coupling_ends, prolong_ends = list(diag_ends), list(diag_ends), list(diag_ends)
    for chunk in range(size // ROWS):
        if chunk * ROWS % LOAD == 0:
            at = 2 + 2 * (chunk * ROWS // LOAD)
            copies[at].wait()
            copies[at + 1].wait()
        sums = []
        for i in range(chunk * ROWS, chunk * ROWS + ROWS):
            pair = coupling_half[i].astype(F32)
            block = diag_half[i].astype(F32)
            coupling[i] = pair
            diag[i] = block
            t, row = divmod(i, size // 4)
            diag_ends[t] = place(diag_ends[t], block, row)
            coupling_ends[t] = place(coupling_ends[t], pair, row)
            sums.append(jnp.sum(block * start + pair * lower, axis=0, keepdims=True))
            upward = upward + pair * guess[i : i + 1, :]
        work[pl.ds(chunk * ROWS, ROWS), :] = jnp.concatenate(sums, axis=0)
    upper = jnp.where(lane == count - 1, 0.0, turn(upward, -1))
    copies[1].wait()
    defect = rhs[...] - (work[...] + upper)

    for chunk in range(size // ROWS):
        if chunk * ROWS % LOAD == 0:
            copies[2 + 2 * parts + chunk * ROWS // LOAD].wait()
        rows = pl.ds(chunk * ROWS, ROWS)
        sums = []
        for i in range(chunk * ROWS, chunk * ROWS + ROWS):
            block = inverse_half[i].astype(F32)
            inverse[i] = block
            t, row = divmod(i, size // 4)
            inverse_ends[t] = place(inverse_ends[t], block, row)
            sums.append(jnp.sum(block * defect, axis=0, keepdims=True))
        trial[rows, :] = guess[rows, :] + jnp.concatenate(sums, axis=0)

    for copy in copies[-3:]:
        copy.wait()
    for i in range(size):
        t, row = divmod(i, size // 4)
        prolong_ends[t] = place(prolong_ends[t], prolong[i].astype(F32), row)
    diag_turned = end_blocks_turned(diag_ends, (1, 2, 3, 4, 5, 6))
    coupling_turned = end_blocks_turned(coupling_ends, (1, 2, 3, 4, 5, 6))
    inverses = end_blocks(inverse_ends, (1, 2, 3, 4, 5, 6))
    couplings = end_blocks(coupling_ends, (2, 3, 4, 5, 6, 7))
    prolongs = end_blocks(prolong_ends, (1, 2, 3, 4, 5, 6))
    turned_diag = [diag_turned[:, k * size : (k + 1) * size] for k in range(6)]
    turned = [coupling_turned[:, k * size : (k + 1) * size] for k in range(6)]

    second = trial[...]
    last = count - 1
    named = jnp.broadcast_to(aggregate[...].astype(F32), (size, count))
    both = [(start, 0)] + [(second, k) for k in range(3)] + [(rhs[...], k) for k in range(3)]
    both = both + [(named, k) for k in range(3)]
    known = edge_rows(both, [(column, last - k) for column, k in both], count)
    shape = (size, size)
    unit = lax.broadcasted_iota(jnp.int32, shape, 0) == lax.broadcasted_iota(jnp.int32, shape, 1)
    defects, after = [], []
    for k in range(6):
        own_row = (k - 3) if k > 2 else EDGE_ROWS + (2 - k)
        lane_of = (k - 3) if k > 2 else last - (2 - k)
        total = to_row(turned_diag[k], trial[:, lane_of : lane_of + 1])
        if k != 3:
            total = total + to_row(turned[k], trial[:, lane_of - 1 : lane_of])
        if k != 2:
            total = total + to_row(couplings[k], trial[:, lane_of + 1 : lane_of + 2])
        defect_row = known[own_row + 4 : own_row + 5] - total
        step = to_column(inverses[k], defect_row)
        step = jnp.sum(jnp.where(unit, step, 0.0), axis=0, keepdims=True)
        defects.append(defect_row)
        after.append(known[own_row + 1 : own_row + 2] + step)
    rows = []
    for base, nearest, next_one, third in ((0, 3, 4, 5), (EDGE_ROWS, 2, 1, 0)):
        rows = rows + [
            known[base : base + 2], defects[nearest], after[next_one], after[third],
            known[base + 4 : base + 6], known[base + 7 : base + 10],
        ]
    rows = rows + [jnp.zeros((EDGES - 2 * EDGE_ROWS, size), F32)]
    rows = jnp.concatenate(rows, axis=0)
    rows_out[...] = rows
    lasts = (
        (turned_diag[2], inverses[2]), (couplings[1], couplings[0]), (prolongs[2], prolongs[1]),
        (prolongs[0], couplings[4]), (turned_diag[1], inverses[1]),
    )
    firsts = (
        (turned_diag[3], inverses[3]), (couplings[2], couplings[3]), (prolongs[3], prolongs[4]),
        (prolongs[5], couplings[4]), (turned_diag[4], inverses[4]),
    )
    even = even_device()
    for k, (one, other) in enumerate(zip(lasts, firsts)):
        one, other = jnp.concatenate(one, axis=1), jnp.concatenate(other, axis=1)
        at = slice(k * size, (k + 1) * size)
        near[at] = jnp.where(even, one, other).astype(BF16)
        far[at] = jnp.where(even, other, one).astype(BF16)
    high, middle, low = (part.astype(F32) for part in three(rows))
    shares = jnp.concatenate(
        [jnp.concatenate([high, low], axis=1), jnp.concatenate([middle, low], axis=1)], axis=0
    ).astype(BF16)
    near[TILES * size :] = shares
    far[TILES * size :] = shares

def beyond_ends(even, near, far, size):
    near, far = near[...].astype(F32), far[...].astype(F32)
    sides, rows = [], []
    for side in (jnp.where(even, far, near), jnp.where(even, near, far)):
        pairs = [side[k * size : (k + 1) * size] for k in range(TILES)]
        sides.append(([(pair[:, :size], pair[:, size:]) for pair in pairs], pairs[1]))
        tail = side[TILES * size :]
        rows.append(tail[:EDGES, :size] + tail[EDGES:, :size] + tail[:EDGES, size:])
    return sides, rows


def columns_from(size):
    shape = (size, size)
    unit = lax.broadcasted_iota(jnp.int32, shape, 0) == lax.broadcasted_iota(jnp.int32, shape, 1)
    return lambda row: jnp.sum(jnp.where(unit, row, 0.0), axis=1, keepdims=True)


def ends(lane, first, last):
    return jnp.where(lane == 0, first, jnp.where(lane == lane.shape[1] - 1, last, 0.0))


def trial_kernel(
    group_count, rhs, trial, diag, inverse, coupling, prolong, aggregate, near, far,
    trial_twice, partial, own, work,
):
    apply_blocks(inverse, wrong(rhs, trial, diag, coupling, work), trial, trial_twice)
    work[...] = wrong(rhs, trial_twice, diag, coupling, work)
    pieces = apply_transposed(prolong, work)
    picked = [chosen(aggregate, group_count, half) for half in (0, 1)]
    both = product(jnp.concatenate(picked, axis=0), pieces, ((1,), (1,)))
    rows_out = group_count // 2
    partial[...] = jnp.concatenate([both[:rows_out], both[rows_out:]], axis=1)

    size = rhs.shape[0]
    even = even_device()
    near, far = near[: TILES * size].astype(F32), far[: TILES * size].astype(F32)
    lasts, firsts = (
        [side[k * size : (k + 1) * size] for k in range(TILES)]
        for side in (jnp.where(even, near, far), jnp.where(even, far, near))
    )
    turned_last, turned_first = jnp.transpose(lasts[1]), jnp.transpose(firsts[1])
    turned_third = jnp.transpose(firsts[3])[size:]
    lasts = [(tile[:, :size], tile[:, size:]) for tile in lasts]
    firsts = [(tile[:, :size], tile[:, size:]) for tile in firsts]
    blocks = (
        lasts[0][0], firsts[0][0], lasts[4][1], lasts[0][1], firsts[0][1], firsts[4][1],
        lasts[1][0], firsts[1][0], turned_first[:size], turned_first[size:],
        lasts[4][0], firsts[4][0], lasts[1][1], firsts[1][1], turned_last[:size], turned_third,
        lasts[3][0], lasts[2][1], lasts[2][0], firsts[2][0], firsts[2][1], firsts[3][0],
    )
    for k, block in enumerate(blocks):
        own[k] = block


def second_kernel(
    group_count, trial_partial, trial_twice, own, rows, far, near, twice, partial, ghosts,
):
    size, count = trial_twice.shape
    sides, (left, right) = beyond_ends(even_device(), near, far, size)
    (left_blocks, _), (right_blocks, right_pair) = sides
    column = columns_from(size)
    half = EDGE_ROWS
    left_diag, left_inverse = left_blocks[0]
    (right_diag, right_inverse), (right_coupling, _) = right_blocks[:2]
    right_turned = jnp.transpose(right_pair)[:size]
    last_diag, first_diag = own[0], own[1]
    before_inverse, last_inverse, first_inverse, second_inverse = (own[2 + k] for k in range(4))
    last_coupling, first_coupling, first_turned, second_turned = (own[6 + k] for k in range(4))
    first_start, first_trial, last_start, last_trial = (
        column(rows[k : k + 1]) for k in (0, 1, half, half + 1)
    )
    left_start, left_trial = (column(left[half + k : half + k + 1]) for k in (0, 1))
    right_start, right_trial = (column(right[k : k + 1]) for k in (0, 1))
    left_wrong, right_wrong = left[half + 2 : half + 3], right[2:3]

    first_change = -to_column(first_inverse, to_row(first_turned, left_start))
    last_change = -to_column(last_inverse, to_row(right_coupling, right_start))
    left_change = -to_column(left_inverse, to_row(first_coupling, first_start))
    right_change = -to_column(right_inverse, to_row(right_turned, last_start))
    left_once, right_once = left_trial + left_change, right_trial + right_change
    first_added = to_row(first_diag, first_change) + to_row(first_turned, left_once)
    last_added = to_row(last_diag, last_change) + to_row(right_coupling, right_once)
    left_added = to_row(left_diag, left_change)
    left_added = left_added + to_row(first_coupling, first_trial + first_change)
    right_added = to_row(right_diag, right_change)
    right_added = right_added + to_row(right_turned, last_trial + last_change)
    left_twice = left_once + to_column(left_inverse, left_wrong - left_added)
    right_twice = right_once + to_column(right_inverse, right_wrong - right_added)
    second_added = to_row(second_turned, first_change)
    before_added = to_row(last_coupling, last_change)
    lane = lax.broadcasted_iota(jnp.int32, (size, count), 1)
    first_new = first_change - to_column(first_inverse, first_added)
    second_new = -to_column(second_inverse, second_added)
    before_new = -to_column(before_inverse, before_added)
    last_new = last_change - to_column(last_inverse, last_added)
    change = ends(lane, first_new, last_new)
    change = jnp.where(lane == 1, second_new, change)
    change = jnp.where(lane == count - 2, before_new, change)
    twice[...] = trial_twice[...] + change
    tile = jnp.zeros((size, count), F32)
    for k, ghost in enumerate((left_twice, left_change, right_twice, right_change)):
        tile = jnp.where(lane == k, ghost, tile)
    ghosts[...] = tile
    before_diag, second_diag, before_coupling, second_coupling = (own[10 + k] for k in range(4))
    last_turned, third_turned = own[14], own[15]
    prolongs = [own[16 + k] for k in range(6)]
    added = (
        to_row(before_coupling, before_new),
        to_row(before_diag, before_new) + to_row(last_coupling, last_new),
        to_row(last_diag, last_new) + to_row(last_turned, before_new)
        + to_row(right_coupling, right_twice),
        to_row(first_diag, first_new) + to_row(second_coupling, second_new)
        + to_row(first_turned, left_twice),
        to_row(second_diag, second_new) + to_row(second_turned, first_new),
        to_row(third_turned, second_new),
    )
    pieces = [to_row(block, column(row)) for block, row in zip(prolongs, added)]
    order = (half + 9, half + 8, half + 7, 7, 8, 9)
    names = [rows[k : k + 1] for k in order]
    blank = jnp.zeros((ROWS - 6, size), F32)
    pieces = jnp.concatenate(pieces + [blank], axis=0)
    names = jnp.concatenate(names + [blank], axis=0)[:, 0:1]
    rows_out = group_count // 2
    start = (lax.axis_index("grp") * group_count).astype(F32)
    row = lax.broadcasted_iota(jnp.int32, (ROWS, 2 * rows_out), 1)
    half_row = lax.rem(row, rows_out)
    named = (half_row // ROWS) * (2 * ROWS) + lax.rem(row, ROWS) + (row // rows_out) * ROWS
    mine = jnp.where(names - start == named.astype(F32), 1.0, 0.0)
    both = product(mine, pieces, ((0,), (0,)))
    both = jnp.concatenate([both[:rows_out], both[rows_out:]], axis=1)
    partial[...] = trial_partial[...] - both


def chosen(aggregate, group_count, half):
    rows = group_count // 2
    local_index = jnp.broadcast_to(lax.rem(aggregate[...], group_count), (rows, aggregate.shape[1]))
    row = lax.broadcasted_iota(jnp.int32, local_index.shape, 0)
    named = (row // ROWS) * (2 * ROWS) + lax.rem(row, ROWS) + half * ROWS
    return jnp.where(local_index == named, 1.0, 0.0).astype(F32)


def coarse_kernel(shares, coarse_inverse, out):
    size = coarse_inverse.shape[0]
    rows = shares.shape[0] // ROWS
    share = shares[0:ROWS]
    for row in range(1, rows):
        share = share + shares[row * ROWS : (row + 1) * ROWS]
    share = jnp.concatenate([share[:, :size], share[:, size:]], axis=0)
    lane = lanes(share)
    value = jnp.zeros_like(share)
    for i in range(size):
        total = jnp.sum(coarse_inverse[i].astype(F32) * share, axis=1, keepdims=True)
        value = jnp.where(lane == i, total, value)
    value = jnp.concatenate([value[:ROWS], value[ROWS:]], axis=1)
    for row in range(out.shape[0] // ROWS):
        out[row * ROWS : (row + 1) * ROWS] = value


def third_kernel(
    group_count, rhs, twice, values, diag, inverse, coupling, own, near, far, ghosts,
    prolong, aggregate, solution_out, residual, start, once, work,
):
    size, count = rhs.shape
    every = values.shape[0]
    in_group = group_count // 2
    group = pl.ds(pl.multiple_of(lax.axis_index("grp") * in_group, ROWS), in_group)
    mine = three(values[group, :])
    picked = [chosen(aggregate, group_count, half) for half in (0, 1)]
    picked = jnp.concatenate(picked, axis=1).astype(BF16)
    spread = jnp.zeros((size, count), F32)
    for part in mine:
        both = lax.dot_general(part, picked, (((0,), (0,)), ((), ())), preferred_element_type=F32)
        spread = spread + (both[:size, :count] + both[size:, count:])
    apply_blocks(prolong, spread, twice, start)

    sides, (left, right) = beyond_ends(even_device(), near, far, size)
    (left_blocks, left_pair), (right_blocks, right_pair) = sides
    column = columns_from(size)
    lane = lax.broadcasted_iota(jnp.int32, (size, count), 1)
    half = EDGE_ROWS
    blank = jnp.zeros((2, size), F32)
    names = jnp.concatenate([left[half + 7 : half + 10], right[7:10], blank], axis=0)[:, 0:1]
    source = lax.broadcasted_iota(jnp.int32, (ROWS, every), 1)
    first_name = (source // ROWS) * (2 * ROWS) + lax.rem(source, ROWS)
    everything = three(values[...])
    named = [
        jnp.where(names == (first_name + k * ROWS).astype(F32), 1.0, 0.0) for k in (0, 1)
    ]
    named = jnp.concatenate(named, axis=0).astype(BF16)
    coarse = jnp.zeros((ROWS, size), F32)
    for part in everything:
        both = jnp.dot(named, part, preferred_element_type=F32)
        coarse = coarse + (both[:ROWS, :size] + both[ROWS:, size:])

    (left_diag, left_inverse), (left_coupling, _) = left_blocks[:2]
    left_next_diag, left_next_inverse = left_blocks[4]
    left_pair, right_pair = jnp.transpose(left_pair), jnp.transpose(right_pair)
    left_turned, left_next_turned = left_pair[:size], left_pair[size:]
    (right_diag, right_inverse), (right_coupling, right_next_coupling) = right_blocks[:2]
    right_next_diag, right_next_inverse = right_blocks[4]
    right_turned, right_next_turned = right_pair[:size], right_pair[size:]
    right_third_coupling = right_blocks[3][1]
    first_coupling, first_turned = own[7], own[8]
    left_x, left_change, right_x, right_change = (ghosts[:, k : k + 1] for k in range(4))
    left_y, left_z = (column(left[half + k : half + k + 1]) for k in (3, 4))
    right_y, right_z = (column(right[k : k + 1]) for k in (3, 4))
    left_y = left_y - to_column(left_next_inverse, to_row(left_coupling, left_change))
    right_y = right_y - to_column(right_next_inverse, to_row(right_next_turned, right_change))
    prolongs = (left_blocks[2][0], left_blocks[2][1], left_blocks[3][0])
    prolongs = prolongs + (right_blocks[2][0], right_blocks[2][1], right_blocks[3][0])
    known = (left_x, left_y, left_z, right_x, right_y, right_z)
    left_x, left_y, left_z, right_x, right_y, right_z = (
        value + to_column(block, coarse[k : k + 1])
        for k, (value, block) in enumerate(zip(known, prolongs))
    )
    left_rhs, left_next_rhs = left[half + 5 : half + 6], left[half + 6 : half + 7]
    right_rhs, right_next_rhs = right[5:6], right[6:7]

    def added(left_column, right_column):
        return ends(
            lane,
            column(to_row(first_turned, left_column)),
            column(to_row(right_coupling, right_column)),
        )

    def nearest(vector, left_x, left_y, right_x, right_y):
        left_sum = to_row(left_diag, left_x) + to_row(left_turned, left_y)
        left_sum = left_sum + to_row(first_coupling, vector[:, 0:1])
        right_sum = to_row(right_diag, right_x) + to_row(right_turned, vector[:, count - 1 : count])
        right_sum = right_sum + to_row(right_next_coupling, right_y)
        return (
            left_x + to_column(left_inverse, left_rhs - left_sum),
            right_x + to_column(right_inverse, right_rhs - right_sum),
        )

    defect = wrong(rhs, start, diag, coupling, work) - added(left_x, right_x)
    left_once, right_once = nearest(start, left_x, left_y, right_x, right_y)
    left_sum = to_row(left_next_diag, left_y) + to_row(left_next_turned, left_z)
    left_sum = left_sum + to_row(left_coupling, left_x)
    left_y = left_y + to_column(left_next_inverse, left_next_rhs - left_sum)
    right_sum = to_row(right_next_diag, right_y) + to_row(right_next_turned, right_x)
    right_sum = right_sum + to_row(right_third_coupling, right_z)
    right_y = right_y + to_column(right_next_inverse, right_next_rhs - right_sum)
    apply_blocks(inverse, defect, start, once)
    defect = wrong(rhs, once, diag, coupling, work) - added(left_once, right_once)
    left_twice, right_twice = nearest(once, left_once, left_y, right_once, right_y)
    apply_blocks(inverse, defect, once, solution_out)
    defect = wrong(rhs, solution_out, diag, coupling, work)
    residual[...] = defect - added(left_twice, right_twice)


def call(kernel, outs, scratch, *operands, space=pltpu.VMEM, cost=None):
    inside = pl.BlockSpec(memory_space=pltpu.VMEM)
    if space == pltpu.HBM:
        operands = [pltpu.with_memory_space_constraint(x, space) for x in operands]
    single = not isinstance(outs, tuple)
    return pl.pallas_call(
        kernel,
        out_shape=outs,
        in_specs=[pl.BlockSpec(memory_space=space)] * len(operands),
        out_specs=inside if single else (inside,) * len(outs),
        scratch_shapes=scratch,
        cost_estimate=cost,
        compiler_params=pltpu.CompilerParams(vmem_limit_bytes=24 << 20),
    )(*operands)


def local(rhs, guess, diag_blocks, diag_inverse, coupling, prolong, coarse_inverse, aggregate):
    size, count = rhs.shape
    members = lax.axis_size("row")
    group_count = count * members // AGG
    assert coarse_inverse.shape[2] == 2 * ROWS and 2 * size == count and members % 2 == 0
    aggregate = aggregate.reshape(1, count)
    coarse_inverse = jnp.transpose(coarse_inverse, (0, 2, 1))

    def shape(*sizes, kind=F32):
        return jax.ShapeDtypeStruct(sizes, kind)

    tile = shape(size, count)
    blocks = shape(size, size, count)
    packed = shape(group_count // 2, count)
    edge = shape(TILES * size + 2 * EDGES, count, kind=BF16)
    line = shape(EDGES, size)
    plain = pltpu.VMEM((size, count), F32)
    half = pltpu.VMEM((size, size, count), BF16)
    loads = 2 + 3 * (size // LOAD) + 3
    (
        rhs, diag, inverse, coupling, prolong, coarse_inverse, aggregate,
        trial, near, far, rows,
    ) = call(
        first_kernel,
        (
            tile, blocks, blocks, blocks,
            shape(size, size, count, kind=BF16),
            shape(*coarse_inverse.shape, kind=BF16),
            shape(1, count, kind=jnp.int32),
            tile, edge, edge, line,
        ),
        [
            plain, half, half, half, plain,
            pltpu.SemaphoreType.DMA((loads,)),
        ],
        rhs, guess, diag_blocks, diag_inverse, coupling, prolong, coarse_inverse, aggregate,
        space=pltpu.HBM,
    )
    trial_twice, trial_partial, own = call(
        functools.partial(trial_kernel, group_count), (tile, packed, shape(22, size, size)), [plain],
        rhs, trial, diag, inverse, coupling, prolong, aggregate, near, far,
        cost=pl.CostEstimate(flops=8 * size**2 * count, bytes_accessed=8 * size**2 * count, transcendentals=0),
    )
    far = swap(far, 1)
    near = swap(near, 0)
    twice, partial, ghosts = call(
        functools.partial(second_kernel, group_count), (tile, packed, tile), [],
        trial_partial, trial_twice, own, rows, far, near,
    )
    shares = lax.all_to_all(partial, "row", 0, 0, tiled=True)
    corrected = call(
        coarse_kernel, shape(lax.axis_size(BOTH) * ROWS, count), [], shares, coarse_inverse
    )
    values = lax.all_to_all(corrected, BOTH, 0, 0, tiled=True)
    return call(
        functools.partial(third_kernel, group_count), (tile, tile), [plain, plain, plain],
        rhs, twice, values, diag, inverse, coupling, own, near, far, ghosts, prolong, aggregate,
    )


def solution(mesh):
    vector = P(None, BOTH)
    blocks = P(None, None, BOTH)
    return jax.shard_map(
        local,
        mesh=mesh,
        in_specs=(vector, vector, blocks, blocks, blocks, blocks, blocks, P(BOTH)),
        out_specs=(vector, vector),
        check_vma=False,
    )
```

```python
import functools

import jax
import jax.numpy as jnp
from jax import lax
from jax.experimental import pallas as pl
from jax.experimental.pallas import tpu as pltpu
from jax.sharding import PartitionSpec as P

AGG = 8
BOTH = ("grp", "row")
F32 = jnp.float32
BF16 = jnp.bfloat16
ROWS = 8
LOAD = 16
EDGES = 24
EDGE_ROWS = 10
TILES = 5


def swap(block, first):
    pairs = [(i, i + 1) for i in range(first, lax.axis_size(BOTH) - 1, 2)]
    return lax.ppermute(block, BOTH, pairs + [(j, i) for i, j in pairs])


def even_device():
    return lax.rem(lax.axis_index("row"), 2) == 0


def lanes(like):
    return lax.broadcasted_iota(jnp.int32, like.shape, 1)


def turn(tile, shift):
    return pltpu.roll(tile, shift % tile.shape[1], 1)


def three(tile):
    high = tile.astype(BF16)
    rest = tile - high.astype(F32)
    middle = rest.astype(BF16)
    return high, middle, (rest - middle.astype(F32)).astype(BF16)


def product(left, right, dims):
    left = left.astype(BF16)
    parts = [
        lax.dot_general(left, part, (dims, ((), ())), preferred_element_type=F32)
        for part in three(right)
    ]
    return parts[0] + (parts[1] + parts[2])


def stack(rows):
    return jnp.concatenate([part.astype(F32) for part in three(rows)], axis=0)


def to_column(block, row):
    return jnp.sum(block * row, axis=1, keepdims=True)


def to_row(block, column):
    return jnp.sum(block * column, axis=0, keepdims=True)


def operate(diag, coupling, vector_ref, out_ref, lower):
    vector = vector_ref[...]

    def step(chunk, upward):
        start = pl.multiple_of(chunk * ROWS, ROWS)
        own = vector_ref[pl.ds(start, ROWS), :]
        sums = []
        for s in range(ROWS):
            pair = coupling[start + s]
            terms = diag[start + s] * vector + pair * lower
            sums.append(jnp.sum(terms, axis=0, keepdims=True))
            upward = upward + pair * own[s : s + 1, :]
        out_ref[pl.ds(start, ROWS), :] = jnp.concatenate(sums, axis=0)
        return upward

    return loop(vector.shape[0] // ROWS, step, jnp.zeros_like(vector))


def apply_blocks(blocks, vector, base_ref, out_ref):
    def step(chunk, carry):
        start = pl.multiple_of(chunk * ROWS, ROWS)
        sums = [
            jnp.sum(blocks[start + s].astype(F32) * vector, axis=0, keepdims=True)
            for s in range(ROWS)
        ]
        base = base_ref[pl.ds(start, ROWS), :]
        out_ref[pl.ds(start, ROWS), :] = base + jnp.concatenate(sums, axis=0)
        return carry

    loop(vector.shape[0] // ROWS, step, 0)


def apply_transposed(blocks, vector_ref):
    def step(chunk, total):
        start = pl.multiple_of(chunk * ROWS, ROWS)
        own = vector_ref[pl.ds(start, ROWS), :]
        for s in range(ROWS):
            total = total + blocks[start + s].astype(F32) * own[s : s + 1, :]
        return total

    zero = jnp.zeros(vector_ref.shape, F32)
    return loop(vector_ref.shape[0] // ROWS, step, zero)


def loop(count, step, carry):
    return lax.fori_loop(0, count, step, carry, unroll=True)


def place(tile, block, row):
    shape = (tile.shape[0] // ROWS, ROWS, tile.shape[1])
    lane = lax.broadcasted_iota(jnp.int32, (1,) + shape[1:], 2)
    mine = lax.shift_right_logical(lane, 3) == row
    turned = pltpu.roll(block, 8 * row + 4, 1).reshape(shape)
    return jnp.where(mine, turned, tile.reshape(shape)).reshape(tile.shape)


def picker(size, width, ends):
    shape = (size * len(ends), width)
    row = lax.broadcasted_iota(jnp.int32, shape, 0)
    lane = lax.broadcasted_iota(jnp.int32, shape, 1)
    target = 8 * lax.rem(row, size) + row // size + ends[0]
    return jnp.where(lane == target, 1.0, 0.0).astype(BF16)


def end_blocks(tiles, ends):
    packed = jnp.concatenate(tiles, axis=1).astype(BF16)
    size = packed.shape[0]
    blocks = lax.dot_general(
        picker(size, packed.shape[1], ends), packed, (((1,), (1,)), ((), ())),
        preferred_element_type=F32,
    )
    return [blocks[k * size : (k + 1) * size] for k in range(len(ends))]


def end_blocks_turned(tiles, ends):
    packed = jnp.concatenate(tiles, axis=1).astype(BF16)
    return lax.dot_general(
        packed, picker(packed.shape[0], packed.shape[1], ends), (((1,), (1,)), ((), ())),
        preferred_element_type=F32,
    )


def edge_rows(firsts, lasts, count):
    lane = lanes(firsts[0][0])
    tile = jnp.zeros(lane.shape, F32)
    for k, (column, where) in enumerate(firsts + lasts):
        tile = jnp.where(lane == k, turn(column, k - where), tile)
    return jnp.transpose(tile)[:EDGES]


def wrong(rhs_ref, vector_ref, diag, coupling, work):
    vector = vector_ref[...]
    lane = lanes(vector)
    lower = jnp.where(lane == 0, 0.0, turn(vector, 1))
    upward = operate(diag, coupling, vector_ref, work, lower)
    upper = jnp.where(lane == vector.shape[1] - 1, 0.0, turn(upward, -1))
    return rhs_ref[...] - (work[...] + upper)


def first_kernel(
    rhs_in, guess_in, diag_in, inverse_in, coupling_in, prolong_in, coarse_in, aggregate_in,
    rhs, diag, inverse, coupling, prolong, coarse, aggregate,
    trial, near, far, rows_out,
    guess, diag_half, inverse_half, coupling_half, work, sems,
):
    size, count = guess.shape
    parts = diag_half.shape[0] // LOAD
    copies = [
        pltpu.make_async_copy(guess_in, guess, sems.at[0]),
        pltpu.make_async_copy(rhs_in, rhs, sems.at[1]),
    ]
    for p in range(parts):
        rows = pl.ds(p * LOAD, LOAD)
        for source, target in ((coupling_in, coupling_half), (diag_in, diag_half)):
            copies.append(
                pltpu.make_async_copy(source.at[rows], target.at[rows], sems.at[len(copies)])
            )
    for p in range(parts):
        rows = pl.ds(p * LOAD, LOAD)
        copies.append(
            pltpu.make_async_copy(inverse_in.at[rows], inverse_half.at[rows], sems.at[len(copies)])
        )
    for source, target in ((prolong_in, prolong), (coarse_in, coarse), (aggregate_in, aggregate)):
        copies.append(pltpu.make_async_copy(source, target, sems.at[len(copies)]))
    for copy in copies:
        copy.start()
    copies[0].wait()

    start = guess[...]
    lane = lanes(start)
    lower = jnp.where(lane == 0, 0.0, turn(start, 1))
    upward = jnp.zeros_like(start)
    diag_ends = [jnp.zeros_like(start) for _ in range(4)]
    inverse_ends, coupling_ends, prolong_ends = list(diag_ends), list(diag_ends), list(diag_ends)
    for chunk in range(size // ROWS):
        if chunk * ROWS % LOAD == 0:
            at = 2 + 2 * (chunk * ROWS // LOAD)
            copies[at].wait()
            copies[at + 1].wait()
        sums = []
        for i in range(chunk * ROWS, chunk * ROWS + ROWS):
            pair = coupling_half[i].astype(F32)
            block = diag_half[i].astype(F32)
            coupling[i] = pair
            diag[i] = block
            t, row = divmod(i, size // 4)
            diag_ends[t] = place(diag_ends[t], block, row)
            coupling_ends[t] = place(coupling_ends[t], pair, row)
            sums.append(jnp.sum(block * start + pair * lower, axis=0, keepdims=True))
            upward = upward + pair * guess[i : i + 1, :]
        work[pl.ds(chunk * ROWS, ROWS), :] = jnp.concatenate(sums, axis=0)
    upper = jnp.where(lane == count - 1, 0.0, turn(upward, -1))
    copies[1].wait()
    defect = rhs[...] - (work[...] + upper)

    for chunk in range(size // ROWS):
        if chunk * ROWS % LOAD == 0:
            copies[2 + 2 * parts + chunk * ROWS // LOAD].wait()
        rows = pl.ds(chunk * ROWS, ROWS)
        sums = []
        for i in range(chunk * ROWS, chunk * ROWS + ROWS):
            block = inverse_half[i].astype(F32)
            inverse[i] = block
            t, row = divmod(i, size // 4)
            inverse_ends[t] = place(inverse_ends[t], block, row)
            sums.append(jnp.sum(block * defect, axis=0, keepdims=True))
        trial[rows, :] = guess[rows, :] + jnp.concatenate(sums, axis=0)

    for copy in copies[-3:]:
        copy.wait()
    for i in range(size):
        t, row = divmod(i, size // 4)
        prolong_ends[t] = place(prolong_ends[t], prolong[i].astype(F32), row)
    diag_turned = end_blocks_turned(diag_ends, (1, 2, 3, 4, 5, 6))
    coupling_turned = end_blocks_turned(coupling_ends, (1, 2, 3, 4, 5, 6))
    inverses = end_blocks(inverse_ends, (1, 2, 3, 4, 5, 6))
    couplings = end_blocks(coupling_ends, (2, 3, 4, 5, 6, 7))
    prolongs = end_blocks(prolong_ends, (1, 2, 3, 4, 5, 6))
    turned_diag = [diag_turned[:, k * size : (k + 1) * size] for k in range(6)]
    turned = [coupling_turned[:, k * size : (k + 1) * size] for k in range(6)]

    second = trial[...]
    last = count - 1
    named = jnp.broadcast_to(aggregate[...].astype(F32), (size, count))
    both = [(start, 0)] + [(second, k) for k in range(3)] + [(rhs[...], k) for k in range(3)]
    both = both + [(named, k) for k in range(3)]
    known = edge_rows(both, [(column, last - k) for column, k in both], count)
    shape = (size, size)
    unit = lax.broadcasted_iota(jnp.int32, shape, 0) == lax.broadcasted_iota(jnp.int32, shape, 1)
    defects, after = [], []
    for k in range(6):
        own_row = (k - 3) if k > 2 else EDGE_ROWS + (2 - k)
        lane_of = (k - 3) if k > 2 else last - (2 - k)
        total = to_row(turned_diag[k], trial[:, lane_of : lane_of + 1])
        if k != 3:
            total = total + to_row(turned[k], trial[:, lane_of - 1 : lane_of])
        if k != 2:
            total = total + to_row(couplings[k], trial[:, lane_of + 1 : lane_of + 2])
        defect_row = known[own_row + 4 : own_row + 5] - total
        step = to_column(inverses[k], defect_row)
        step = jnp.sum(jnp.where(unit, step, 0.0), axis=0, keepdims=True)
        defects.append(defect_row)
        after.append(known[own_row + 1 : own_row + 2] + step)
    rows = []
    for base, nearest, next_one, third in ((0, 3, 4, 5), (EDGE_ROWS, 2, 1, 0)):
        rows = rows + [
            known[base : base + 2], defects[nearest], after[next_one], after[third],
            known[base + 4 : base + 6], known[base + 7 : base + 10],
        ]
    rows = rows + [jnp.zeros((EDGES - 2 * EDGE_ROWS, size), F32)]
    rows = jnp.concatenate(rows, axis=0)
    rows_out[...] = rows
    lasts = (
        (turned_diag[2], inverses[2]), (couplings[1], couplings[0]), (prolongs[2], prolongs[1]),
        (prolongs[0], couplings[4]), (turned_diag[1], inverses[1]),
    )
    firsts = (
        (turned_diag[3], inverses[3]), (couplings[2], couplings[3]), (prolongs[3], prolongs[4]),
        (prolongs[5], couplings[4]), (turned_diag[4], inverses[4]),
    )
    even = even_device()
    for k, (one, other) in enumerate(zip(lasts, firsts)):
        one, other = jnp.concatenate(one, axis=1), jnp.concatenate(other, axis=1)
        at = slice(k * size, (k + 1) * size)
        near[at] = jnp.where(even, one, other).astype(BF16)
        far[at] = jnp.where(even, other, one).astype(BF16)
    high, middle, low = (part.astype(F32) for part in three(rows))
    shares = jnp.concatenate(
        [jnp.concatenate([high, low], axis=1), jnp.concatenate([middle, low], axis=1)], axis=0
    ).astype(BF16)
    near[TILES * size :] = shares
    far[TILES * size :] = shares

def beyond_ends(even, near, far, size):
    near, far = near[...].astype(F32), far[...].astype(F32)
    sides, rows = [], []
    for side in (jnp.where(even, far, near), jnp.where(even, near, far)):
        pairs = [side[k * size : (k + 1) * size] for k in range(TILES)]
        sides.append(([(pair[:, :size], pair[:, size:]) for pair in pairs], pairs[1]))
        tail = side[TILES * size :]
        rows.append(tail[:EDGES, :size] + tail[EDGES:, :size] + tail[:EDGES, size:])
    return sides, rows


def columns_from(size):
    shape = (size, size)
    unit = lax.broadcasted_iota(jnp.int32, shape, 0) == lax.broadcasted_iota(jnp.int32, shape, 1)
    return lambda row: jnp.sum(jnp.where(unit, row, 0.0), axis=1, keepdims=True)


def ends(lane, first, last):
    return jnp.where(lane == 0, first, jnp.where(lane == lane.shape[1] - 1, last, 0.0))


def trial_kernel(
    group_count, rhs, trial, diag, inverse, coupling, prolong, aggregate, near, far,
    trial_twice, partial, own, wide, work,
):
    apply_blocks(inverse, wrong(rhs, trial, diag, coupling, work), trial, trial_twice)
    work[...] = wrong(rhs, trial_twice, diag, coupling, work)
    pieces = apply_transposed(prolong, work)
    picked = [chosen(aggregate, group_count, half) for half in (0, 1)]
    both = product(jnp.concatenate(picked, axis=0), pieces, ((1,), (1,)))
    rows_out = group_count // 2
    partial[...] = jnp.concatenate([both[:rows_out], both[rows_out:]], axis=1)

    size = rhs.shape[0]
    even = even_device()
    near, far = near[: TILES * size].astype(F32), far[: TILES * size].astype(F32)
    lasts, firsts = (
        [side[k * size : (k + 1) * size] for k in range(TILES)]
        for side in (jnp.where(even, near, far), jnp.where(even, far, near))
    )
    turned_last, turned_first = jnp.transpose(lasts[1]), jnp.transpose(firsts[1])
    turned_third = jnp.transpose(firsts[3])[size:]
    lasts = [(tile[:, :size], tile[:, size:]) for tile in lasts]
    firsts = [(tile[:, :size], tile[:, size:]) for tile in firsts]
    blocks = (
        lasts[0][0], firsts[0][0], lasts[4][1], lasts[0][1], firsts[0][1], firsts[4][1],
        lasts[1][0], firsts[1][0], turned_first[:size], turned_first[size:],
        lasts[4][0], firsts[4][0], lasts[1][1], firsts[1][1], turned_last[:size], turned_third,
        lasts[3][0], lasts[2][1], lasts[2][0], firsts[2][0], firsts[2][1], firsts[3][0],
    )
    for k, block in enumerate(blocks):
        own[k] = block
    for i in range(size):
        wide[i] = prolong[i].astype(F32)


def second_kernel(
    group_count, trial_partial, trial_twice, own, rows, far, near, twice, partial, ghosts,
):
    size, count = trial_twice.shape
    sides, (left, right) = beyond_ends(even_device(), near, far, size)
    (left_blocks, _), (right_blocks, right_pair) = sides
    column = columns_from(size)
    half = EDGE_ROWS
    left_diag, left_inverse = left_blocks[0]
    (right_diag, right_inverse), (right_coupling, _) = right_blocks[:2]
    right_turned = jnp.transpose(right_pair)[:size]
    last_diag, first_diag = own[0], own[1]
    before_inverse, last_inverse, first_inverse, second_inverse = (own[2 + k] for k in range(4))
    last_coupling, first_coupling, first_turned, second_turned = (own[6 + k] for k in range(4))
    first_start, first_trial, last_start, last_trial = (
        column(rows[k : k + 1]) for k in (0, 1, half, half + 1)
    )
    left_start, left_trial = (column(left[half + k : half + k + 1]) for k in (0, 1))
    right_start, right_trial = (column(right[k : k + 1]) for k in (0, 1))
    left_wrong, right_wrong = left[half + 2 : half + 3], right[2:3]

    first_change = -to_column(first_inverse, to_row(first_turned, left_start))
    last_change = -to_column(last_inverse, to_row(right_coupling, right_start))
    left_change = -to_column(left_inverse, to_row(first_coupling, first_start))
    right_change = -to_column(right_inverse, to_row(right_turned, last_start))
    left_once, right_once = left_trial + left_change, right_trial + right_change
    first_added = to_row(first_diag, first_change) + to_row(first_turned, left_once)
    last_added = to_row(last_diag, last_change) + to_row(right_coupling, right_once)
    left_added = to_row(left_diag, left_change)
    left_added = left_added + to_row(first_coupling, first_trial + first_change)
    right_added = to_row(right_diag, right_change)
    right_added = right_added + to_row(right_turned, last_trial + last_change)
    left_twice = left_once + to_column(left_inverse, left_wrong - left_added)
    right_twice = right_once + to_column(right_inverse, right_wrong - right_added)
    second_added = to_row(second_turned, first_change)
    before_added = to_row(last_coupling, last_change)
    lane = lax.broadcasted_iota(jnp.int32, (size, count), 1)
    first_new = first_change - to_column(first_inverse, first_added)
    second_new = -to_column(second_inverse, second_added)
    before_new = -to_column(before_inverse, before_added)
    last_new = last_change - to_column(last_inverse, last_added)
    change = ends(lane, first_new, last_new)
    change = jnp.where(lane == 1, second_new, change)
    change = jnp.where(lane == count - 2, before_new, change)
    twice[...] = trial_twice[...] + change
    tile = jnp.zeros((size, count), F32)
    for k, ghost in enumerate((left_twice, left_change, right_twice, right_change)):
        tile = jnp.where(lane == k, ghost, tile)
    ghosts[...] = tile
    before_diag, second_diag, before_coupling, second_coupling = (own[10 + k] for k in range(4))
    last_turned, third_turned = own[14], own[15]
    prolongs = [own[16 + k] for k in range(6)]
    added = (
        to_row(before_coupling, before_new),
        to_row(before_diag, before_new) + to_row(last_coupling, last_new),
        to_row(last_diag, last_new) + to_row(last_turned, before_new)
        + to_row(right_coupling, right_twice),
        to_row(first_diag, first_new) + to_row(second_coupling, second_new)
        + to_row(first_turned, left_twice),
        to_row(second_diag, second_new) + to_row(second_turned, first_new),
        to_row(third_turned, second_new),
    )
    pieces = [to_row(block, column(row)) for block, row in zip(prolongs, added)]
    order = (half + 9, half + 8, half + 7, 7, 8, 9)
    names = [rows[k : k + 1] for k in order]
    blank = jnp.zeros((ROWS - 6, size), F32)
    pieces = jnp.concatenate(pieces + [blank], axis=0)
    names = jnp.concatenate(names + [blank], axis=0)[:, 0:1]
    rows_out = group_count // 2
    start = (lax.axis_index("grp") * group_count).astype(F32)
    row = lax.broadcasted_iota(jnp.int32, (ROWS, 2 * rows_out), 1)
    half_row = lax.rem(row, rows_out)
    named = (half_row // ROWS) * (2 * ROWS) + lax.rem(row, ROWS) + (row // rows_out) * ROWS
    mine = jnp.where(names - start == named.astype(F32), 1.0, 0.0)
    both = product(mine, pieces, ((0,), (0,)))
    both = jnp.concatenate([both[:rows_out], both[rows_out:]], axis=1)
    partial[...] = trial_partial[...] - both


def chosen(aggregate, group_count, half):
    rows = group_count // 2
    local_index = jnp.broadcast_to(lax.rem(aggregate[...], group_count), (rows, aggregate.shape[1]))
    row = lax.broadcasted_iota(jnp.int32, local_index.shape, 0)
    named = (row // ROWS) * (2 * ROWS) + lax.rem(row, ROWS) + half * ROWS
    return jnp.where(local_index == named, 1.0, 0.0).astype(F32)


def coarse_kernel(shares, coarse_inverse, out):
    size = coarse_inverse.shape[0]
    rows = shares.shape[0] // ROWS
    share = shares[0:ROWS]
    for row in range(1, rows):
        share = share + shares[row * ROWS : (row + 1) * ROWS]
    share = jnp.concatenate([share[:, :size], share[:, size:]], axis=0)
    lane = lanes(share)
    value = jnp.zeros_like(share)
    for i in range(size):
        total = jnp.sum(coarse_inverse[i].astype(F32) * share, axis=1, keepdims=True)
        value = jnp.where(lane == i, total, value)
    value = jnp.concatenate([value[:ROWS], value[ROWS:]], axis=1)
    for row in range(out.shape[0] // ROWS):
        out[row * ROWS : (row + 1) * ROWS] = value


def third_kernel(
    group_count, rhs, twice, values, diag, inverse, coupling, own, near, far, ghosts,
    prolong, aggregate, solution_out, residual, start, once, work,
):
    size, count = rhs.shape
    every = values.shape[0]
    in_group = group_count // 2
    group = pl.ds(pl.multiple_of(lax.axis_index("grp") * in_group, ROWS), in_group)
    mine = three(values[group, :])
    picked = [chosen(aggregate, group_count, half) for half in (0, 1)]
    picked = jnp.concatenate(picked, axis=1).astype(BF16)
    spread = jnp.zeros((size, count), F32)
    for part in mine:
        both = lax.dot_general(part, picked, (((0,), (0,)), ((), ())), preferred_element_type=F32)
        spread = spread + (both[:size, :count] + both[size:, count:])
    apply_blocks(prolong, spread, twice, start)

    sides, (left, right) = beyond_ends(even_device(), near, far, size)
    (left_blocks, left_pair), (right_blocks, right_pair) = sides
    column = columns_from(size)
    lane = lax.broadcasted_iota(jnp.int32, (size, count), 1)
    half = EDGE_ROWS
    blank = jnp.zeros((2, size), F32)
    names = jnp.concatenate([left[half + 7 : half + 10], right[7:10], blank], axis=0)[:, 0:1]
    source = lax.broadcasted_iota(jnp.int32, (ROWS, every), 1)
    first_name = (source // ROWS) * (2 * ROWS) + lax.rem(source, ROWS)
    everything = three(values[...])
    named = [
        jnp.where(names == (first_name + k * ROWS).astype(F32), 1.0, 0.0) for k in (0, 1)
    ]
    named = jnp.concatenate(named, axis=0).astype(BF16)
    coarse = jnp.zeros((ROWS, size), F32)
    for part in everything:
        both = jnp.dot(named, part, preferred_element_type=F32)
        coarse = coarse + (both[:ROWS, :size] + both[ROWS:, size:])

    (left_diag, left_inverse), (left_coupling, _) = left_blocks[:2]
    left_next_diag, left_next_inverse = left_blocks[4]
    left_pair, right_pair = jnp.transpose(left_pair), jnp.transpose(right_pair)
    left_turned, left_next_turned = left_pair[:size], left_pair[size:]
    (right_diag, right_inverse), (right_coupling, right_next_coupling) = right_blocks[:2]
    right_next_diag, right_next_inverse = right_blocks[4]
    right_turned, right_next_turned = right_pair[:size], right_pair[size:]
    right_third_coupling = right_blocks[3][1]
    first_coupling, first_turned = own[7], own[8]
    left_x, left_change, right_x, right_change = (ghosts[:, k : k + 1] for k in range(4))
    left_y, left_z = (column(left[half + k : half + k + 1]) for k in (3, 4))
    right_y, right_z = (column(right[k : k + 1]) for k in (3, 4))
    left_y = left_y - to_column(left_next_inverse, to_row(left_coupling, left_change))
    right_y = right_y - to_column(right_next_inverse, to_row(right_next_turned, right_change))
    prolongs = (left_blocks[2][0], left_blocks[2][1], left_blocks[3][0])
    prolongs = prolongs + (right_blocks[2][0], right_blocks[2][1], right_blocks[3][0])
    known = (left_x, left_y, left_z, right_x, right_y, right_z)
    left_x, left_y, left_z, right_x, right_y, right_z = (
        value + to_column(block, coarse[k : k + 1])
        for k, (value, block) in enumerate(zip(known, prolongs))
    )
    left_rhs, left_next_rhs = left[half + 5 : half + 6], left[half + 6 : half + 7]
    right_rhs, right_next_rhs = right[5:6], right[6:7]

    def added(left_column, right_column):
        return ends(
            lane,
            column(to_row(first_turned, left_column)),
            column(to_row(right_coupling, right_column)),
        )

    def nearest(vector, left_x, left_y, right_x, right_y):
        left_sum = to_row(left_diag, left_x) + to_row(left_turned, left_y)
        left_sum = left_sum + to_row(first_coupling, vector[:, 0:1])
        right_sum = to_row(right_diag, right_x) + to_row(right_turned, vector[:, count - 1 : count])
        right_sum = right_sum + to_row(right_next_coupling, right_y)
        return (
            left_x + to_column(left_inverse, left_rhs - left_sum),
            right_x + to_column(right_inverse, right_rhs - right_sum),
        )

    defect = wrong(rhs, start, diag, coupling, work) - added(left_x, right_x)
    left_once, right_once = nearest(start, left_x, left_y, right_x, right_y)
    left_sum = to_row(left_next_diag, left_y) + to_row(left_next_turned, left_z)
    left_sum = left_sum + to_row(left_coupling, left_x)
    left_y = left_y + to_column(left_next_inverse, left_next_rhs - left_sum)
    right_sum = to_row(right_next_diag, right_y) + to_row(right_next_turned, right_x)
    right_sum = right_sum + to_row(right_third_coupling, right_z)
    right_y = right_y + to_column(right_next_inverse, right_next_rhs - right_sum)
    apply_blocks(inverse, defect, start, once)
    defect = wrong(rhs, once, diag, coupling, work) - added(left_once, right_once)
    left_twice, right_twice = nearest(once, left_once, left_y, right_once, right_y)
    apply_blocks(inverse, defect, once, solution_out)
    defect = wrong(rhs, solution_out, diag, coupling, work)
    residual[...] = defect - added(left_twice, right_twice)


def call(kernel, outs, scratch, *operands, space=pltpu.VMEM, cost=None):
    inside = pl.BlockSpec(memory_space=pltpu.VMEM)
    if space == pltpu.HBM:
        operands = [pltpu.with_memory_space_constraint(x, space) for x in operands]
    single = not isinstance(outs, tuple)
    return pl.pallas_call(
        kernel,
        out_shape=outs,
        in_specs=[pl.BlockSpec(memory_space=space)] * len(operands),
        out_specs=inside if single else (inside,) * len(outs),
        scratch_shapes=scratch,
        cost_estimate=cost,
        compiler_params=pltpu.CompilerParams(vmem_limit_bytes=24 << 20),
    )(*operands)


def local(rhs, guess, diag_blocks, diag_inverse, coupling, prolong, coarse_inverse, aggregate):
    size, count = rhs.shape
    members = lax.axis_size("row")
    group_count = count * members // AGG
    assert coarse_inverse.shape[2] == 2 * ROWS and 2 * size == count and members % 2 == 0
    aggregate = aggregate.reshape(1, count)
    coarse_inverse = jnp.transpose(coarse_inverse, (0, 2, 1))

    def shape(*sizes, kind=F32):
        return jax.ShapeDtypeStruct(sizes, kind)

    tile = shape(size, count)
    blocks = shape(size, size, count)
    packed = shape(group_count // 2, count)
    edge = shape(TILES * size + 2 * EDGES, count, kind=BF16)
    line = shape(EDGES, size)
    plain = pltpu.VMEM((size, count), F32)
    half = pltpu.VMEM((size, size, count), BF16)
    loads = 2 + 3 * (size // LOAD) + 3
    (
        rhs, diag, inverse, coupling, prolong, coarse_inverse, aggregate,
        trial, near, far, rows,
    ) = call(
        first_kernel,
        (
            tile, blocks, blocks, blocks,
            shape(size, size, count, kind=BF16),
            shape(*coarse_inverse.shape, kind=BF16),
            shape(1, count, kind=jnp.int32),
            tile, edge, edge, line,
        ),
        [
            plain, half, half, half, plain,
            pltpu.SemaphoreType.DMA((loads,)),
        ],
        rhs, guess, diag_blocks, diag_inverse, coupling, prolong, coarse_inverse, aggregate,
        space=pltpu.HBM,
    )
    trial_twice, trial_partial, own, wide = call(
        functools.partial(trial_kernel, group_count), (tile, packed, shape(22, size, size), blocks), [plain],
        rhs, trial, diag, inverse, coupling, prolong, aggregate, near, far,
        cost=pl.CostEstimate(flops=8 * size**2 * count, bytes_accessed=8 * size**2 * count, transcendentals=0),
    )
    far = swap(far, 1)
    near = swap(near, 0)
    twice, partial, ghosts = call(
        functools.partial(second_kernel, group_count), (tile, packed, tile), [],
        trial_partial, trial_twice, own, rows, far, near,
    )
    shares = lax.all_to_all(partial, "row", 0, 0, tiled=True)
    corrected = call(
        coarse_kernel, shape(lax.axis_size(BOTH) * ROWS, count), [], shares, coarse_inverse
    )
    values = lax.all_to_all(corrected, BOTH, 0, 0, tiled=True)
    return call(
        functools.partial(third_kernel, group_count), (tile, tile), [plain, plain, plain],
        rhs, twice, values, diag, inverse, coupling, own, near, far, ghosts, wide, aggregate,
    )


def solution(mesh):
    vector = P(None, BOTH)
    blocks = P(None, None, BOTH)
    return jax.shard_map(
        local,
        mesh=mesh,
        in_specs=(vector, vector, blocks, blocks, blocks, blocks, blocks, P(BOTH)),
        out_specs=(vector, vector),
        check_vma=False,
    )
```

```python
import functools

import jax
import jax.numpy as jnp
from jax import lax
from jax.experimental import pallas as pl
from jax.experimental.pallas import tpu as pltpu
from jax.sharding import PartitionSpec as P

AGG = 8
BOTH = ("grp", "row")
F32 = jnp.float32
BF16 = jnp.bfloat16
ROWS = 8
LOAD = 32
EDGES = 24
EDGE_ROWS = 10
TILES = 5


def swap(block, first):
    pairs = [(i, i + 1) for i in range(first, lax.axis_size(BOTH) - 1, 2)]
    return lax.ppermute(block, BOTH, pairs + [(j, i) for i, j in pairs])


def even_device():
    return lax.rem(lax.axis_index("row"), 2) == 0


def lanes(like):
    return lax.broadcasted_iota(jnp.int32, like.shape, 1)


def turn(tile, shift):
    return pltpu.roll(tile, shift % tile.shape[1], 1)


def three(tile):
    high = tile.astype(BF16)
    rest = tile - high.astype(F32)
    middle = rest.astype(BF16)
    return high, middle, (rest - middle.astype(F32)).astype(BF16)


def product(left, right, dims):
    left = left.astype(BF16)
    parts = [
        lax.dot_general(left, part, (dims, ((), ())), preferred_element_type=F32)
        for part in three(right)
    ]
    return parts[0] + (parts[1] + parts[2])


def stack(rows):
    return jnp.concatenate([part.astype(F32) for part in three(rows)], axis=0)


def to_column(block, row):
    return jnp.sum(block * row, axis=1, keepdims=True)


def to_row(block, column):
    return jnp.sum(block * column, axis=0, keepdims=True)


def operate(diag, coupling, vector_ref, out_ref, lower):
    vector = vector_ref[...]

    def step(chunk, upward):
        start = pl.multiple_of(chunk * ROWS, ROWS)
        own = vector_ref[pl.ds(start, ROWS), :]
        sums = []
        for s in range(ROWS):
            pair = coupling[start + s]
            terms = diag[start + s] * vector + pair * lower
            sums.append(jnp.sum(terms, axis=0, keepdims=True))
            upward = upward + pair * own[s : s + 1, :]
        out_ref[pl.ds(start, ROWS), :] = jnp.concatenate(sums, axis=0)
        return upward

    return loop(vector.shape[0] // ROWS, step, jnp.zeros_like(vector))


def apply_blocks(blocks, vector, base_ref, out_ref):
    def step(chunk, carry):
        start = pl.multiple_of(chunk * ROWS, ROWS)
        sums = [
            jnp.sum(blocks[start + s].astype(F32) * vector, axis=0, keepdims=True)
            for s in range(ROWS)
        ]
        base = base_ref[pl.ds(start, ROWS), :]
        out_ref[pl.ds(start, ROWS), :] = base + jnp.concatenate(sums, axis=0)
        return carry

    loop(vector.shape[0] // ROWS, step, 0)


def apply_transposed(blocks, vector_ref):
    def step(chunk, total):
        start = pl.multiple_of(chunk * ROWS, ROWS)
        own = vector_ref[pl.ds(start, ROWS), :]
        for s in range(ROWS):
            total = total + blocks[start + s].astype(F32) * own[s : s + 1, :]
        return total

    zero = jnp.zeros(vector_ref.shape, F32)
    return loop(vector_ref.shape[0] // ROWS, step, zero)


def loop(count, step, carry):
    return lax.fori_loop(0, count, step, carry, unroll=True)


def place(tile, block, row):
    shape = (tile.shape[0] // ROWS, ROWS, tile.shape[1])
    lane = lax.broadcasted_iota(jnp.int32, (1,) + shape[1:], 2)
    mine = lax.shift_right_logical(lane, 3) == row
    turned = pltpu.roll(block, 8 * row + 4, 1).reshape(shape)
    return jnp.where(mine, turned, tile.reshape(shape)).reshape(tile.shape)


def picker(size, width, ends):
    shape = (size * len(ends), width)
    row = lax.broadcasted_iota(jnp.int32, shape, 0)
    lane = lax.broadcasted_iota(jnp.int32, shape, 1)
    target = 8 * lax.rem(row, size) + row // size + ends[0]
    return jnp.where(lane == target, 1.0, 0.0).astype(BF16)


def end_blocks(tiles, ends):
    packed = jnp.concatenate(tiles, axis=1).astype(BF16)
    size = packed.shape[0]
    blocks = lax.dot_general(
        picker(size, packed.shape[1], ends), packed, (((1,), (1,)), ((), ())),
        preferred_element_type=F32,
    )
    return [blocks[k * size : (k + 1) * size] for k in range(len(ends))]


def end_blocks_turned(tiles, ends):
    packed = jnp.concatenate(tiles, axis=1).astype(BF16)
    return lax.dot_general(
        packed, picker(packed.shape[0], packed.shape[1], ends), (((1,), (1,)), ((), ())),
        preferred_element_type=F32,
    )


def edge_rows(firsts, lasts, count):
    lane = lanes(firsts[0][0])
    tile = jnp.zeros(lane.shape, F32)
    for k, (column, where) in enumerate(firsts + lasts):
        tile = jnp.where(lane == k, turn(column, k - where), tile)
    return jnp.transpose(tile)[:EDGES]


def wrong(rhs_ref, vector_ref, diag, coupling, work):
    vector = vector_ref[...]
    lane = lanes(vector)
    lower = jnp.where(lane == 0, 0.0, turn(vector, 1))
    upward = operate(diag, coupling, vector_ref, work, lower)
    upper = jnp.where(lane == vector.shape[1] - 1, 0.0, turn(upward, -1))
    return rhs_ref[...] - (work[...] + upper)


def first_kernel(
    rhs_in, guess_in, diag_in, inverse_in, coupling_in, prolong_in, coarse_in, aggregate_in,
    rhs, diag, inverse, coupling, prolong, coarse, aggregate,
    trial, near, far, rows_out,
    guess, diag_half, inverse_half, coupling_half, work, sems,
):
    size, count = guess.shape
    parts = diag_half.shape[0] // LOAD
    copies = [
        pltpu.make_async_copy(guess_in, guess, sems.at[0]),
        pltpu.make_async_copy(rhs_in, rhs, sems.at[1]),
    ]
    for p in range(parts):
        rows = pl.ds(p * LOAD, LOAD)
        for source, target in ((coupling_in, coupling_half), (diag_in, diag_half)):
            copies.append(
                pltpu.make_async_copy(source.at[rows], target.at[rows], sems.at[len(copies)])
            )
    for p in range(parts):
        rows = pl.ds(p * LOAD, LOAD)
        copies.append(
            pltpu.make_async_copy(inverse_in.at[rows], inverse_half.at[rows], sems.at[len(copies)])
        )
    for source, target in ((prolong_in, prolong), (coarse_in, coarse), (aggregate_in, aggregate)):
        copies.append(pltpu.make_async_copy(source, target, sems.at[len(copies)]))
    for copy in copies:
        copy.start()
    copies[0].wait()

    start = guess[...]
    lane = lanes(start)
    lower = jnp.where(lane == 0, 0.0, turn(start, 1))
    upward = jnp.zeros_like(start)
    diag_ends = [jnp.zeros_like(start) for _ in range(4)]
    inverse_ends, coupling_ends, prolong_ends = list(diag_ends), list(diag_ends), list(diag_ends)
    for chunk in range(size // ROWS):
        if chunk * ROWS % LOAD == 0:
            at = 2 + 2 * (chunk * ROWS // LOAD)
            copies[at].wait()
            copies[at + 1].wait()
        sums = []
        for i in range(chunk * ROWS, chunk * ROWS + ROWS):
            pair = coupling_half[i].astype(F32)
            block = diag_half[i].astype(F32)
            coupling[i] = pair
            diag[i] = block
            t, row = divmod(i, size // 4)
            diag_ends[t] = place(diag_ends[t], block, row)
            coupling_ends[t] = place(coupling_ends[t], pair, row)
            sums.append(jnp.sum(block * start + pair * lower, axis=0, keepdims=True))
            upward = upward + pair * guess[i : i + 1, :]
        work[pl.ds(chunk * ROWS, ROWS), :] = jnp.concatenate(sums, axis=0)
    upper = jnp.where(lane == count - 1, 0.0, turn(upward, -1))
    copies[1].wait()
    defect = rhs[...] - (work[...] + upper)

    for chunk in range(size // ROWS):
        if chunk * ROWS % LOAD == 0:
            copies[2 + 2 * parts + chunk * ROWS // LOAD].wait()
        rows = pl.ds(chunk * ROWS, ROWS)
        sums = []
        for i in range(chunk * ROWS, chunk * ROWS + ROWS):
            block = inverse_half[i].astype(F32)
            inverse[i] = block
            t, row = divmod(i, size // 4)
            inverse_ends[t] = place(inverse_ends[t], block, row)
            sums.append(jnp.sum(block * defect, axis=0, keepdims=True))
        trial[rows, :] = guess[rows, :] + jnp.concatenate(sums, axis=0)

    for copy in copies[-3:]:
        copy.wait()
    for i in range(size):
        t, row = divmod(i, size // 4)
        prolong_ends[t] = place(prolong_ends[t], prolong[i].astype(F32), row)
    diag_turned = end_blocks_turned(diag_ends, (1, 2, 3, 4, 5, 6))
    coupling_turned = end_blocks_turned(coupling_ends, (1, 2, 3, 4, 5, 6))
    inverses = end_blocks(inverse_ends, (1, 2, 3, 4, 5, 6))
    couplings = end_blocks(coupling_ends, (2, 3, 4, 5, 6, 7))
    prolongs = end_blocks(prolong_ends, (1, 2, 3, 4, 5, 6))
    turned_diag = [diag_turned[:, k * size : (k + 1) * size] for k in range(6)]
    turned = [coupling_turned[:, k * size : (k + 1) * size] for k in range(6)]

    second = trial[...]
    last = count - 1
    named = jnp.broadcast_to(aggregate[...].astype(F32), (size, count))
    both = [(start, 0)] + [(second, k) for k in range(3)] + [(rhs[...], k) for k in range(3)]
    both = both + [(named, k) for k in range(3)]
    known = edge_rows(both, [(column, last - k) for column, k in both], count)
    shape = (size, size)
    unit = lax.broadcasted_iota(jnp.int32, shape, 0) == lax.broadcasted_iota(jnp.int32, shape, 1)
    defects, after = [], []
    for k in range(6):
        own_row = (k - 3) if k > 2 else EDGE_ROWS + (2 - k)
        lane_of = (k - 3) if k > 2 else last - (2 - k)
        total = to_row(turned_diag[k], trial[:, lane_of : lane_of + 1])
        if k != 3:
            total = total + to_row(turned[k], trial[:, lane_of - 1 : lane_of])
        if k != 2:
            total = total + to_row(couplings[k], trial[:, lane_of + 1 : lane_of + 2])
        defect_row = known[own_row + 4 : own_row + 5] - total
        step = to_column(inverses[k], defect_row)
        step = jnp.sum(jnp.where(unit, step, 0.0), axis=0, keepdims=True)
        defects.append(defect_row)
        after.append(known[own_row + 1 : own_row + 2] + step)
    rows = []
    for base, nearest, next_one, third in ((0, 3, 4, 5), (EDGE_ROWS, 2, 1, 0)):
        rows = rows + [
            known[base : base + 2], defects[nearest], after[next_one], after[third],
            known[base + 4 : base + 6], known[base + 7 : base + 10],
        ]
    rows = rows + [jnp.zeros((EDGES - 2 * EDGE_ROWS, size), F32)]
    rows = jnp.concatenate(rows, axis=0)
    rows_out[...] = rows
    lasts = (
        (turned_diag[2], inverses[2]), (couplings[1], couplings[0]), (prolongs[2], prolongs[1]),
        (prolongs[0], couplings[4]), (turned_diag[1], inverses[1]),
    )
    firsts = (
        (turned_diag[3], inverses[3]), (couplings[2], couplings[3]), (prolongs[3], prolongs[4]),
        (prolongs[5], couplings[4]), (turned_diag[4], inverses[4]),
    )
    even = even_device()
    for k, (one, other) in enumerate(zip(lasts, firsts)):
        one, other = jnp.concatenate(one, axis=1), jnp.concatenate(other, axis=1)
        at = slice(k * size, (k + 1) * size)
        near[at] = jnp.where(even, one, other).astype(BF16)
        far[at] = jnp.where(even, other, one).astype(BF16)
    high, middle, low = (part.astype(F32) for part in three(rows))
    shares = jnp.concatenate(
        [jnp.concatenate([high, low], axis=1), jnp.concatenate([middle, low], axis=1)], axis=0
    ).astype(BF16)
    near[TILES * size :] = shares
    far[TILES * size :] = shares

def beyond_ends(even, near, far, size):
    near, far = near[...].astype(F32), far[...].astype(F32)
    sides, rows = [], []
    for side in (jnp.where(even, far, near), jnp.where(even, near, far)):
        pairs = [side[k * size : (k + 1) * size] for k in range(TILES)]
        sides.append(([(pair[:, :size], pair[:, size:]) for pair in pairs], pairs[1]))
        tail = side[TILES * size :]
        rows.append(tail[:EDGES, :size] + tail[EDGES:, :size] + tail[:EDGES, size:])
    return sides, rows


def columns_from(size):
    shape = (size, size)
    unit = lax.broadcasted_iota(jnp.int32, shape, 0) == lax.broadcasted_iota(jnp.int32, shape, 1)
    return lambda row: jnp.sum(jnp.where(unit, row, 0.0), axis=1, keepdims=True)


def ends(lane, first, last):
    return jnp.where(lane == 0, first, jnp.where(lane == lane.shape[1] - 1, last, 0.0))


def trial_kernel(
    group_count, rhs, trial, diag, inverse, coupling, prolong, aggregate, near, far,
    trial_twice, partial, own, work,
):
    apply_blocks(inverse, wrong(rhs, trial, diag, coupling, work), trial, trial_twice)
    work[...] = wrong(rhs, trial_twice, diag, coupling, work)
    pieces = apply_transposed(prolong, work)
    picked = [chosen(aggregate, group_count, half) for half in (0, 1)]
    both = product(jnp.concatenate(picked, axis=0), pieces, ((1,), (1,)))
    rows_out = group_count // 2
    partial[...] = jnp.concatenate([both[:rows_out], both[rows_out:]], axis=1)

    size = rhs.shape[0]
    even = even_device()
    near, far = near[: TILES * size].astype(F32), far[: TILES * size].astype(F32)
    lasts, firsts = (
        [side[k * size : (k + 1) * size] for k in range(TILES)]
        for side in (jnp.where(even, near, far), jnp.where(even, far, near))
    )
    turned_last, turned_first = jnp.transpose(lasts[1]), jnp.transpose(firsts[1])
    turned_third = jnp.transpose(firsts[3])[size:]
    lasts = [(tile[:, :size], tile[:, size:]) for tile in lasts]
    firsts = [(tile[:, :size], tile[:, size:]) for tile in firsts]
    blocks = (
        lasts[0][0], firsts[0][0], lasts[4][1], lasts[0][1], firsts[0][1], firsts[4][1],
        lasts[1][0], firsts[1][0], turned_first[:size], turned_first[size:],
        lasts[4][0], firsts[4][0], lasts[1][1], firsts[1][1], turned_last[:size], turned_third,
        lasts[3][0], lasts[2][1], lasts[2][0], firsts[2][0], firsts[2][1], firsts[3][0],
    )
    for k, block in enumerate(blocks):
        own[k] = block


def second_kernel(
    group_count, trial_partial, trial_twice, own, rows, far, near, twice, partial, ghosts,
):
    size, count = trial_twice.shape
    sides, (left, right) = beyond_ends(even_device(), near, far, size)
    (left_blocks, _), (right_blocks, right_pair) = sides
    column = columns_from(size)
    half = EDGE_ROWS
    left_diag, left_inverse = left_blocks[0]
    (right_diag, right_inverse), (right_coupling, _) = right_blocks[:2]
    right_turned = jnp.transpose(right_pair)[:size]
    last_diag, first_diag = own[0], own[1]
    before_inverse, last_inverse, first_inverse, second_inverse = (own[2 + k] for k in range(4))
    last_coupling, first_coupling, first_turned, second_turned = (own[6 + k] for k in range(4))
    first_start, first_trial, last_start, last_trial = (
        column(rows[k : k + 1]) for k in (0, 1, half, half + 1)
    )
    left_start, left_trial = (column(left[half + k : half + k + 1]) for k in (0, 1))
    right_start, right_trial = (column(right[k : k + 1]) for k in (0, 1))
    left_wrong, right_wrong = left[half + 2 : half + 3], right[2:3]

    first_change = -to_column(first_inverse, to_row(first_turned, left_start))
    last_change = -to_column(last_inverse, to_row(right_coupling, right_start))
    left_change = -to_column(left_inverse, to_row(first_coupling, first_start))
    right_change = -to_column(right_inverse, to_row(right_turned, last_start))
    left_once, right_once = left_trial + left_change, right_trial + right_change
    first_added = to_row(first_diag, first_change) + to_row(first_turned, left_once)
    last_added = to_row(last_diag, last_change) + to_row(right_coupling, right_once)
    left_added = to_row(left_diag, left_change)
    left_added = left_added + to_row(first_coupling, first_trial + first_change)
    right_added = to_row(right_diag, right_change)
    right_added = right_added + to_row(right_turned, last_trial + last_change)
    left_twice = left_once + to_column(left_inverse, left_wrong - left_added)
    right_twice = right_once + to_column(right_inverse, right_wrong - right_added)
    second_added = to_row(second_turned, first_change)
    before_added = to_row(last_coupling, last_change)
    lane = lax.broadcasted_iota(jnp.int32, (size, count), 1)
    first_new = first_change - to_column(first_inverse, first_added)
    second_new = -to_column(second_inverse, second_added)
    before_new = -to_column(before_inverse, before_added)
    last_new = last_change - to_column(last_inverse, last_added)
    change = ends(lane, first_new, last_new)
    change = jnp.where(lane == 1, second_new, change)
    change = jnp.where(lane == count - 2, before_new, change)
    twice[...] = trial_twice[...] + change
    tile = jnp.zeros((size, count), F32)
    for k, ghost in enumerate((left_twice, left_change, right_twice, right_change)):
        tile = jnp.where(lane == k, ghost, tile)
    ghosts[...] = tile
    before_diag, second_diag, before_coupling, second_coupling = (own[10 + k] for k in range(4))
    last_turned, third_turned = own[14], own[15]
    prolongs = [own[16 + k] for k in range(6)]
    added = (
        to_row(before_coupling, before_new),
        to_row(before_diag, before_new) + to_row(last_coupling, last_new),
        to_row(last_diag, last_new) + to_row(last_turned, before_new)
        + to_row(right_coupling, right_twice),
        to_row(first_diag, first_new) + to_row(second_coupling, second_new)
        + to_row(first_turned, left_twice),
        to_row(second_diag, second_new) + to_row(second_turned, first_new),
        to_row(third_turned, second_new),
    )
    pieces = [to_row(block, column(row)) for block, row in zip(prolongs, added)]
    order = (half + 9, half + 8, half + 7, 7, 8, 9)
    names = [rows[k : k + 1] for k in order]
    blank = jnp.zeros((ROWS - 6, size), F32)
    pieces = jnp.concatenate(pieces + [blank], axis=0)
    names = jnp.concatenate(names + [blank], axis=0)[:, 0:1]
    rows_out = group_count // 2
    start = (lax.axis_index("grp") * group_count).astype(F32)
    row = lax.broadcasted_iota(jnp.int32, (ROWS, 2 * rows_out), 1)
    half_row = lax.rem(row, rows_out)
    named = (half_row // ROWS) * (2 * ROWS) + lax.rem(row, ROWS) + (row // rows_out) * ROWS
    mine = jnp.where(names - start == named.astype(F32), 1.0, 0.0)
    both = product(mine, pieces, ((0,), (0,)))
    both = jnp.concatenate([both[:rows_out], both[rows_out:]], axis=1)
    partial[...] = trial_partial[...] - both


def chosen(aggregate, group_count, half):
    rows = group_count // 2
    local_index = jnp.broadcast_to(lax.rem(aggregate[...], group_count), (rows, aggregate.shape[1]))
    row = lax.broadcasted_iota(jnp.int32, local_index.shape, 0)
    named = (row // ROWS) * (2 * ROWS) + lax.rem(row, ROWS) + half * ROWS
    return jnp.where(local_index == named, 1.0, 0.0).astype(F32)


def coarse_kernel(shares, coarse_inverse, out):
    size = coarse_inverse.shape[0]
    rows = shares.shape[0] // ROWS
    share = shares[0:ROWS]
    for row in range(1, rows):
        share = share + shares[row * ROWS : (row + 1) * ROWS]
    share = jnp.concatenate([share[:, :size], share[:, size:]], axis=0)
    lane = lanes(share)
    value = jnp.zeros_like(share)
    for i in range(size):
        total = jnp.sum(coarse_inverse[i].astype(F32) * share, axis=1, keepdims=True)
        value = jnp.where(lane == i, total, value)
    value = jnp.concatenate([value[:ROWS], value[ROWS:]], axis=1)
    for row in range(out.shape[0] // ROWS):
        out[row * ROWS : (row + 1) * ROWS] = value


def third_kernel(
    group_count, rhs, twice, values, diag, inverse, coupling, own, near, far, ghosts,
    prolong, aggregate, solution_out, residual, start, once, work,
):
    size, count = rhs.shape
    every = values.shape[0]
    in_group = group_count // 2
    group = pl.ds(pl.multiple_of(lax.axis_index("grp") * in_group, ROWS), in_group)
    mine = three(values[group, :])
    picked = [chosen(aggregate, group_count, half) for half in (0, 1)]
    picked = jnp.concatenate(picked, axis=1).astype(BF16)
    spread = jnp.zeros((size, count), F32)
    for part in mine:
        both = lax.dot_general(part, picked, (((0,), (0,)), ((), ())), preferred_element_type=F32)
        spread = spread + (both[:size, :count] + both[size:, count:])
    apply_blocks(prolong, spread, twice, start)

    sides, (left, right) = beyond_ends(even_device(), near, far, size)
    (left_blocks, left_pair), (right_blocks, right_pair) = sides
    column = columns_from(size)
    lane = lax.broadcasted_iota(jnp.int32, (size, count), 1)
    half = EDGE_ROWS
    blank = jnp.zeros((2, size), F32)
    names = jnp.concatenate([left[half + 7 : half + 10], right[7:10], blank], axis=0)[:, 0:1]
    source = lax.broadcasted_iota(jnp.int32, (ROWS, every), 1)
    first_name = (source // ROWS) * (2 * ROWS) + lax.rem(source, ROWS)
    everything = three(values[...])
    named = [
        jnp.where(names == (first_name + k * ROWS).astype(F32), 1.0, 0.0) for k in (0, 1)
    ]
    named = jnp.concatenate(named, axis=0).astype(BF16)
    coarse = jnp.zeros((ROWS, size), F32)
    for part in everything:
        both = jnp.dot(named, part, preferred_element_type=F32)
        coarse = coarse + (both[:ROWS, :size] + both[ROWS:, size:])

    (left_diag, left_inverse), (left_coupling, _) = left_blocks[:2]
    left_next_diag, left_next_inverse = left_blocks[4]
    left_pair, right_pair = jnp.transpose(left_pair), jnp.transpose(right_pair)
    left_turned, left_next_turned = left_pair[:size], left_pair[size:]
    (right_diag, right_inverse), (right_coupling, right_next_coupling) = right_blocks[:2]
    right_next_diag, right_next_inverse = right_blocks[4]
    right_turned, right_next_turned = right_pair[:size], right_pair[size:]
    right_third_coupling = right_blocks[3][1]
    first_coupling, first_turned = own[7], own[8]
    left_x, left_change, right_x, right_change = (ghosts[:, k : k + 1] for k in range(4))
    left_y, left_z = (column(left[half + k : half + k + 1]) for k in (3, 4))
    right_y, right_z = (column(right[k : k + 1]) for k in (3, 4))
    left_y = left_y - to_column(left_next_inverse, to_row(left_coupling, left_change))
    right_y = right_y - to_column(right_next_inverse, to_row(right_next_turned, right_change))
    prolongs = (left_blocks[2][0], left_blocks[2][1], left_blocks[3][0])
    prolongs = prolongs + (right_blocks[2][0], right_blocks[2][1], right_blocks[3][0])
    known = (left_x, left_y, left_z, right_x, right_y, right_z)
    left_x, left_y, left_z, right_x, right_y, right_z = (
        value + to_column(block, coarse[k : k + 1])
        for k, (value, block) in enumerate(zip(known, prolongs))
    )
    left_rhs, left_next_rhs = left[half + 5 : half + 6], left[half + 6 : half + 7]
    right_rhs, right_next_rhs = right[5:6], right[6:7]

    def added(left_column, right_column):
        return ends(
            lane,
            column(to_row(first_turned, left_column)),
            column(to_row(right_coupling, right_column)),
        )

    def nearest(vector, left_x, left_y, right_x, right_y):
        left_sum = to_row(left_diag, left_x) + to_row(left_turned, left_y)
        left_sum = left_sum + to_row(first_coupling, vector[:, 0:1])
        right_sum = to_row(right_diag, right_x) + to_row(right_turned, vector[:, count - 1 : count])
        right_sum = right_sum + to_row(right_next_coupling, right_y)
        return (
            left_x + to_column(left_inverse, left_rhs - left_sum),
            right_x + to_column(right_inverse, right_rhs - right_sum),
        )

    defect = wrong(rhs, start, diag, coupling, work) - added(left_x, right_x)
    left_once, right_once = nearest(start, left_x, left_y, right_x, right_y)
    left_sum = to_row(left_next_diag, left_y) + to_row(left_next_turned, left_z)
    left_sum = left_sum + to_row(left_coupling, left_x)
    left_y = left_y + to_column(left_next_inverse, left_next_rhs - left_sum)
    right_sum = to_row(right_next_diag, right_y) + to_row(right_next_turned, right_x)
    right_sum = right_sum + to_row(right_third_coupling, right_z)
    right_y = right_y + to_column(right_next_inverse, right_next_rhs - right_sum)
    apply_blocks(inverse, defect, start, once)
    defect = wrong(rhs, once, diag, coupling, work) - added(left_once, right_once)
    left_twice, right_twice = nearest(once, left_once, left_y, right_once, right_y)
    apply_blocks(inverse, defect, once, solution_out)
    defect = wrong(rhs, solution_out, diag, coupling, work)
    residual[...] = defect - added(left_twice, right_twice)


def call(kernel, outs, scratch, *operands, space=pltpu.VMEM, cost=None):
    inside = pl.BlockSpec(memory_space=pltpu.VMEM)
    if space == pltpu.HBM:
        operands = [pltpu.with_memory_space_constraint(x, space) for x in operands]
    single = not isinstance(outs, tuple)
    return pl.pallas_call(
        kernel,
        out_shape=outs,
        in_specs=[pl.BlockSpec(memory_space=space)] * len(operands),
        out_specs=inside if single else (inside,) * len(outs),
        scratch_shapes=scratch,
        cost_estimate=cost,
        compiler_params=pltpu.CompilerParams(vmem_limit_bytes=24 << 20),
    )(*operands)


def local(rhs, guess, diag_blocks, diag_inverse, coupling, prolong, coarse_inverse, aggregate):
    size, count = rhs.shape
    members = lax.axis_size("row")
    group_count = count * members // AGG
    assert coarse_inverse.shape[2] == 2 * ROWS and 2 * size == count and members % 2 == 0
    aggregate = aggregate.reshape(1, count)
    coarse_inverse = jnp.transpose(coarse_inverse, (0, 2, 1))

    def shape(*sizes, kind=F32):
        return jax.ShapeDtypeStruct(sizes, kind)

    tile = shape(size, count)
    blocks = shape(size, size, count)
    packed = shape(group_count // 2, count)
    edge = shape(TILES * size + 2 * EDGES, count, kind=BF16)
    line = shape(EDGES, size)
    plain = pltpu.VMEM((size, count), F32)
    half = pltpu.VMEM((size, size, count), BF16)
    loads = 2 + 3 * (size // LOAD) + 3
    (
        rhs, diag, inverse, coupling, prolong, coarse_inverse, aggregate,
        trial, near, far, rows,
    ) = call(
        first_kernel,
        (
            tile, blocks, blocks, blocks,
            shape(size, size, count, kind=BF16),
            shape(*coarse_inverse.shape, kind=BF16),
            shape(1, count, kind=jnp.int32),
            tile, edge, edge, line,
        ),
        [
            plain, half, half, half, plain,
            pltpu.SemaphoreType.DMA((loads,)),
        ],
        rhs, guess, diag_blocks, diag_inverse, coupling, prolong, coarse_inverse, aggregate,
        space=pltpu.HBM,
    )
    trial_twice, trial_partial, own = call(
        functools.partial(trial_kernel, group_count), (tile, packed, shape(22, size, size)), [plain],
        rhs, trial, diag, inverse, coupling, prolong, aggregate, near, far,
        cost=pl.CostEstimate(flops=8 * size**2 * count, bytes_accessed=8 * size**2 * count, transcendentals=0),
    )
    far = swap(far, 1)
    near = swap(near, 0)
    twice, partial, ghosts = call(
        functools.partial(second_kernel, group_count), (tile, packed, tile), [],
        trial_partial, trial_twice, own, rows, far, near,
    )
    shares = lax.all_to_all(partial, "row", 0, 0, tiled=True)
    corrected = call(
        coarse_kernel, shape(lax.axis_size(BOTH) * ROWS, count), [], shares, coarse_inverse
    )
    values = lax.all_to_all(corrected, BOTH, 0, 0, tiled=True)
    return call(
        functools.partial(third_kernel, group_count), (tile, tile), [plain, plain, plain],
        rhs, twice, values, diag, inverse, coupling, own, near, far, ghosts, prolong, aggregate,
    )


def solution(mesh):
    vector = P(None, BOTH)
    blocks = P(None, None, BOTH)
    return jax.shard_map(
        local,
        mesh=mesh,
        in_specs=(vector, vector, blocks, blocks, blocks, blocks, blocks, P(BOTH)),
        out_specs=(vector, vector),
        check_vma=False,
    )
```
